32 devices in a mesh: grp: 4 (over y, x), dev: 8 (over z, core).
Axes of the slice: x: 2, y: 2, z: 4, core: 2. Of those that a mesh axis runs over, the one named last changes fastest.
Arguments:
- tokens: bfloat16 [8192, 1024], P(('grp', 'dev')), may hold values from -6 to 6
- cotangent: bfloat16 [8192, 1024], P(('grp', 'dev')), may hold values from -6 to 6
- lengths: int32 [8], replicated, may hold values from 256 to 1024, as said below
- offsets: int32 [8], replicated, may hold values from 0 to 768, as said below
- ln_gain: bfloat16 [1024], P(('grp', 'dev')), may hold values from 0.5 to 1.5
- ln_bias: bfloat16 [1024], P(('grp', 'dev')), may hold values from -2 to 2
- w_qkv: bfloat16 [1024, 3072], P(('grp', 'dev')), may hold values from -0.1875 to 0.1875
- w_out: bfloat16 [1024, 1024], P(('grp', 'dev')), may hold values from -3 to 3
- w_fc1: bfloat16 [1024, 4096], P(('grp', 'dev')), may hold values from -0.1875 to 0.1875
- b_fc1: bfloat16 [4096], P(('grp', 'dev')), may hold values from -2 to 2
- w_fc2: bfloat16 [4096, 1024], P(('grp', 'dev')), may hold values from -0.09375 to 0.09375
- b_fc2: bfloat16 [1024], P(('grp', 'dev')), may hold values from -2 to 2
Outputs:
- mixed: bfloat16 [8192, 1024], P(('grp', 'dev'))
- token_grad: bfloat16 [8192, 1024], P(('grp', 'dev'))
- g_ln_gain: float32 [1024], P('dev')
- g_ln_bias: float32 [1024], P('dev')
- g_w_qkv: float32 [1024, 3072], P('dev')
- g_w_out: float32 [1024, 1024], P('dev')
- g_w_fc1: float32 [1024, 4096], P('dev')
- g_b_fc1: float32 [4096], P('dev')
- g_w_fc2: float32 [4096, 1024], P('dev')
- g_b_fc2: float32 [1024], P('dev')
The draws below stay inside these ranges and needn't reach their ends.
Inputs may be any that keep to these rules, and one draw needn't show every extreme that they name: `lengths`: one slot in every draw has length 1024 and one has 256. offsets + lengths <= 1024; one slot of length 256 ends at place 1024 - 1.
All inputs are finite; a program needn't handle non-finite values.
Results may differ from the reference program's by a relative error of at most 0.015.
Values may be sent and summed in bfloat16 or wider, within the bound.
A program may use at most 192 MiB of HBM per device.

```python
import math
import jax
import jax.numpy as jnp
from jax import lax

D = 1024
HEADS = 16
HD = 64
ROT = 32
FF = 4096
TOK_DEV = 256
SLOT = 1024
LEAST = 256
SLOTS = 8
TOKENS = 8192


def slot_shapes(key):
    base_key = jax.random.fold_in(key, 11)
    key_len, key_pick, key_off = jax.random.split(base_key, 3)
    drawn_lengths = jax.random.randint(key_len, (SLOTS,), LEAST, SLOT + 1)
    chosen = jax.random.permutation(key_pick, SLOTS)
    drawn_lengths = drawn_lengths.at[chosen[0]].set(SLOT).at[chosen[1]].set(LEAST)
    drawn_offsets = jax.random.randint(key_off, (SLOTS,), 0, SLOT - drawn_lengths + 1)
    drawn_offsets = drawn_offsets.at[chosen[0]].set(0).at[chosen[1]].set(SLOT - LEAST)
    return (drawn_lengths.astype(jnp.int32), drawn_offsets.astype(jnp.int32))


def draw_lengths(key, part):
    return slot_shapes(key)[0]


def draw_offsets(key, part):
    return slot_shapes(key)[1]


def steps_of(key, dims, shards, low, largest):
    level, own = 1.0, jax.random.fold_in(key, 6)
    for position, shards_of in shards:
        steps = jnp.exp(jax.random.uniform(jax.random.fold_in(own, position), (shards_of,), jnp.float32, low / len(shards), largest / len(shards)))
        level = level * jnp.repeat(steps, dims[position] // shards_of).reshape([-1 if axis == position else 1 for axis in range(len(dims))])
    return level


def noise(key, dims, deviation, most, cuts=(), kind=jnp.bfloat16):
    values = jax.random.normal(key, dims, jnp.float32) * deviation
    if len(cuts) > 0:
        values = steps_of(key, dims, cuts, -0.22, 0.18) * values
    return jnp.clip(values, min=-most, max=most).astype(kind)


def setup_inputs(seed: int = 0) -> dict:
    seeds = jax.random.split(jax.random.key(seed), 13)
    return {
        "tokens": noise(seeds[0], (TOKENS, D), 1.0, 6.0, ((0, 32),)),
        "cotangent": noise(seeds[1], (TOKENS, D), 1.0, 6.0, ((0, 32),)),
        "lengths": draw_lengths(jax.random.fold_in(seeds[12], 71), 0),
        "offsets": draw_offsets(jax.random.fold_in(seeds[12], 71), 0),
        "ln_gain": jnp.clip(1.0 + 0.1 * jax.random.normal(seeds[4], (D,), jnp.float32), 0.5, 1.5).astype(jnp.bfloat16),
        "ln_bias": noise(seeds[5], (D,), 0.3, 2.0, ((0, 32),)),
        "w_qkv": noise(seeds[6], (D, 3 * D), D ** -0.5, 0.1875, ((0, 32),)),
        "w_out": noise(seeds[7], (D, D), (max(D // 256, 1)) ** -0.5, 3.0, ((0, 32),)),
        "w_fc1": noise(seeds[8], (D, FF), D ** -0.5, 0.1875, ((0, 32),)),
        "b_fc1": noise(seeds[9], (FF,), 0.3, 2.0, ((0, 32),)),
        "w_fc2": noise(seeds[10], (FF, D), FF ** -0.5, 0.09375, ((0, 32),)),
        "b_fc2": noise(seeds[11], (D,), 0.3, 2.0, ((0, 32),)),
    }


@jax.custom_vjp
def low(v):
    return lax.optimization_barrier(v.astype(jnp.bfloat16)).astype(jnp.float32)

@jax.custom_vjp
def low_back(v):
    return v

def low_keep(v):
    return (low(v), None)

def low_pass(kept, grad):
    return (grad,)

def back_keep(v):
    return (v, None)

def back_low(kept, grad):
    return (low(grad),)
low.defvjp(low_keep, low_pass)
low_back.defvjp(back_keep, back_low)

def product(left_side, right_side):
    return jnp.dot(left_side, right_side, precision=lax.Precision.HIGHEST, preferred_element_type=jnp.float32)

def gelu_tanh(values_in):
    return 0.5 * values_in * (1.0 + jnp.tanh(0.7978845608028654 * (values_in + 0.044715 * values_in * values_in * values_in)))

def turn_tables(places):
    half_rot = ROT // 2
    frequency = jnp.exp(jnp.arange(half_rot, dtype=jnp.float32) * (-2.0 * math.log(10000.0) / ROT))
    angles = places[:, None] * frequency[None, :]
    return (jnp.cos(angles)[:, None, :], jnp.sin(angles)[:, None, :])

def rotate(field_in, cosine, sine_table):
    half_rot = ROT // 2
    first_half = field_in[..., :half_rot]
    second = field_in[..., half_rot:ROT]
    return jnp.concatenate([first_half * cosine - second * sine_table, second * cosine + first_half * sine_table, field_in[..., ROT:]], axis=-1)

def slot_places():
    local = jnp.arange(SLOT, dtype=jnp.int32)
    piece = local // TOK_DEV
    inner = local % TOK_DEV
    half_rows = TOK_DEV // 2
    return jnp.where(inner < half_rows, piece * half_rows + inner, SLOT - (piece + 1) * half_rows + (inner - half_rows)).astype(jnp.int32)

def slot_layer(tokens_in, weights, places, turned, live_rows):
    norm_gain, norm_bias, w_qkv, w_out, w_fc1, b_fc1, w_fc2, b_fc2 = weights
    row_count = tokens_in.shape[0]
    centred = tokens_in - lax.optimization_barrier(jnp.mean(tokens_in, axis=-1, keepdims=True))
    inverse = lax.rsqrt(lax.optimization_barrier(jnp.mean(centred * centred, axis=-1, keepdims=True)) + 1e-05)
    hidden_in = low(centred * inverse * norm_gain + norm_bias)
    mixed_qkv = low_back(product(hidden_in, w_qkv))
    cosine, sine_table = turn_tables(turned)
    queries = low(rotate(mixed_qkv[:, :D].reshape(row_count, HEADS, HD), cosine, sine_table))
    key_rows = low(rotate(mixed_qkv[:, D:2 * D].reshape(row_count, HEADS, HD), cosine, sine_table))
    values = low(mixed_qkv[:, 2 * D:].reshape(row_count, HEADS, HD))
    key_places = places
    block_rows = min(512, row_count)
    score_scale = 1.0 / math.sqrt(HD)

    def attend(first_row):
        block_query = lax.dynamic_slice_in_dim(queries, first_row, block_rows, 0)
        query_places = lax.dynamic_slice_in_dim(places, first_row, block_rows, 0)
        scores = low_back(jnp.einsum('qhd,khd->hqk', block_query, key_rows, precision=lax.Precision.HIGHEST) * score_scale)
        allowed = (key_places[None, :] <= query_places[:, None]) & (live_rows[None, :] | (key_places[None, :] == query_places[:, None]))
        scores = jnp.where(allowed[None], scores, -1e+30)
        row_max = lax.optimization_barrier(jnp.max(scores, axis=-1, keepdims=True))
        expo = jnp.exp(scores - row_max)
        probs_low = low(expo / lax.optimization_barrier(jnp.sum(expo, axis=-1, keepdims=True)))
        return jnp.einsum('hqk,khd->qhd', probs_low, values, precision=lax.Precision.HIGHEST)
    starts = jnp.arange(row_count // block_rows, dtype=jnp.int32) * block_rows
    attended = lax.map(jax.checkpoint(attend), starts).reshape(row_count, D)
    attended = low(low_back(attended))
    act_low = low(gelu_tanh(low_back(product(hidden_in, w_fc1) + b_fc1)))
    branch_sum = tokens_in + product(attended, w_out) + product(act_low, w_fc2) + b_fc2
    return live_rows.astype(jnp.float32)[:, None] * branch_sum

def reference(tokens, cotangent, lengths, offsets, ln_gain, ln_bias, w_qkv, w_out, w_fc1, b_fc1, w_fc2, b_fc2):
    weights = tuple((weight.astype(jnp.float32) for weight in (ln_gain, ln_bias, w_qkv, w_out, w_fc1, b_fc1, w_fc2, b_fc2)))
    inputs = tokens.astype(jnp.float32).reshape(SLOTS, SLOT, D)
    grads_in = cotangent.astype(jnp.float32).reshape(SLOTS, SLOT, D)
    places = slot_places()

    def one_slot(running, slot_item):
        slot_tokens, slot_grad, length, offset = slot_item
        live_rows = (places >= offset) & (places < offset + length)
        turned = (places - offset).astype(jnp.float32)

        def layer_fn(tokens_in, params):
            return slot_layer(tokens_in, params, places, turned, live_rows)
        result, pullback = jax.vjp(layer_fn, slot_tokens, weights)
        grad_tokens, grad_weights = pullback(slot_grad)
        running = jax.tree.map(lambda left_sum, right_sum: left_sum + right_sum, running, grad_weights)
        return (running, (result.astype(jnp.bfloat16), grad_tokens.astype(jnp.bfloat16)))
    start_sums = jax.tree.map(jnp.zeros_like, weights)
    totals, outputs = lax.scan(one_slot, start_sums, (inputs, grads_in, lengths, offsets))
    return (outputs[0].reshape(TOKENS, D), outputs[1].reshape(TOKENS, D), totals[0], totals[1], totals[2], totals[3], totals[4], totals[5], totals[6], totals[7])
```

```python
import functools
import math

import jax
import jax.numpy as jnp
import numpy as np
from jax import lax
from jax.experimental import pallas as pl
from jax.experimental.pallas import tpu as pltpu
from jax.sharding import PartitionSpec as P

HEADS = 16
HD = 64
ROT = 32
MESH = pl.DeviceIdType.MESH
BF = jnp.bfloat16
F32 = jnp.float32


class Dims:
    def __init__(self, mesh, rows, width, ff):
        self.n_grp, self.n_dev = mesh.shape["grp"], mesh.shape["dev"]
        self.n_gy, self.n_zp = self.n_grp // 2, self.n_dev // 4
        assert self.n_gy == self.n_zp
        self.n_all = self.n_grp * self.n_dev
        self.rows, self.width, self.ff = rows, width, ff
        self.r1 = width // self.n_all
        self.r2 = ff // self.n_all
        self.ffs = ff // 8
        self.qs = 3 * width // 8
        self.ca = self.ffs + self.qs
        self.rd = width // self.n_dev
        self.rdg = self.rd // self.n_gy
        self.c2 = width // self.n_gy
        self.ng = self.n_gy * self.n_zp


class Me:
    def __init__(self, d):
        grp, dev = lax.axis_index("grp"), lax.axis_index("dev")
        self.grp, self.dev = grp, dev
        self.gy, self.gx = grp // 2, lax.rem(grp, 2)
        self.zp, self.q = dev // 4, lax.rem(dev, 4)
        self.zl, self.c = self.q // 2, lax.rem(self.q, 2)
        self.f = grp * d.n_dev + dev
        self.rank = self.gx * 4 + self.q


def place(gy, gx, zp, q):
    return {"grp": gy * 2 + gx, "dev": zp * 4 + q}


def remote(src, dst, send, recv, device):
    return pltpu.make_async_remote_copy(
        src_ref=src,
        dst_ref=dst,
        send_sem=send,
        recv_sem=recv,
        device_id=device,
        device_id_type=MESH,
    )


def gather_kernel(d, tok, cot, p1, wo, wf2, sm, TOK, COT, WA, WO, WF2, SM, loc, ts, tr, cs, cr,
                  w1s, w1r, m1s, m1r, zs, zr, ys, yr, os_, or_):
    me = Me(d)
    gy, gx, zp, q = me.gy, me.gx, me.zp, me.q
    half = d.rows // 2
    local = [
        pltpu.make_async_copy(tok, TOK.at[gx, q], loc.at[0]),
        pltpu.make_async_copy(cot, COT.at[gx, q], loc.at[1]),
        pltpu.make_async_copy(p1.at[me.rank], WA.at[gy, gx, zp, q], loc.at[2]),
        pltpu.make_async_copy(wf2, WF2.at[gy, zp], loc.at[3]),
        pltpu.make_async_copy(sm, SM.at[gy, gx, zp, q], loc.at[4]),
    ]

    def token_send(src, buf, send, recv, slot, bx, bq, h, device):
        return remote(
            src.at[pl.ds(h * half, half)],
            buf.at[bx, bq, pl.ds(h * half, half)],
            send.at[slot, h],
            recv.at[bx * 4 + bq, h],
            device,
        )

    x_dev, z_dev, c_dev = place(gy, 1 - gx, zp, q), place(gy, gx, zp, lax.rem(q + 2, 4)), place(
        gy, gx, zp, me.zl * 2 + 1 - me.c
    )
    qz = lax.rem(q + 2, 4)

    sends = []

    def go(copy):
        copy.start()
        sends.append(copy)

    def arrived(buf, send, recv, bx, bq, h):
        token_send(buf.at[bx, bq], buf, send, recv, 0, bx, bq, h, x_dev).wait_recv()

    for h in range(2):
        go(token_send(tok, TOK, ts, tr, 0, gx, q, h, x_dev))
        go(token_send(cot, COT, cs, cr, 0, gx, q, h, z_dev))
    for i in range(1, 8):
        other = lax.rem(me.rank + i, 8)
        dev = place(gy, other // 4, zp, lax.rem(other, 4))
        go(remote(p1.at[other], WA.at[gy, gx, zp, q], w1s.at[other], w1r.at[me.rank], dev))
        go(remote(sm, SM.at[gy, gx, zp, q], m1s.at[other], m1r.at[me.rank], dev))
    for copy in local:
        copy.start()
    for i in range(1, d.n_zp):
        oz = lax.rem(zp + i, d.n_zp)
        go(remote(wf2, WF2.at[gy, zp], zs.at[2, oz], zr.at[2, zp], place(gy, gx, oz, q)))
    per = 128 // d.r1
    owner = me.f // per
    part = lax.rem(me.f, per)
    ox, oq = owner // 4, lax.rem(owner, 4)
    for i in range(d.ng):
        group = lax.rem(gy * d.n_zp + zp + i, d.ng)
        oy, oz = group // d.n_zp, lax.rem(group, d.n_zp)
        copy = remote(wo, WO.at[part], os_.at[i], or_.at[part], place(oy, ox, oz, oq))
        if i == 0:
            mine = jnp.logical_and(ox == gx, oq == q)

            @pl.when(mine)
            def _():
                here = pltpu.make_async_copy(wo, WO.at[part], loc.at[5])
                here.start()
                here.wait()

            @pl.when(jnp.logical_not(mine))
            def _():
                copy.start()
                copy.wait_send()
        else:
            go(copy)
    for h in range(2):
        go(token_send(tok, TOK, ts, tr, 1, gx, q, h, z_dev))
        go(token_send(cot, COT, cs, cr, 1, gx, q, h, x_dev))
        go(token_send(tok, TOK, ts, tr, 3, gx, q, h, c_dev))
        go(token_send(cot, COT, cs, cr, 3, gx, q, h, c_dev))
    for h in range(2):
        arrived(TOK, ts, tr, 1 - gx, q, h)
        go(token_send(TOK.at[1 - gx, q], TOK, ts, tr, 2, 1 - gx, q, h, z_dev))
        go(token_send(TOK.at[1 - gx, q], TOK, ts, tr, 4, 1 - gx, q, h, c_dev))
        arrived(COT, cs, cr, gx, qz, h)
        go(token_send(COT.at[gx, qz], COT, cs, cr, 2, gx, qz, h, x_dev))
        go(token_send(COT.at[gx, qz], COT, cs, cr, 4, gx, qz, h, c_dev))
    for copy in local:
        copy.wait()
    for i in range(1, 8):
        other = lax.rem(me.rank + i, 8)
        ox_, oq_ = other // 4, lax.rem(other, 4)
        dev = place(gy, ox_, zp, oq_)
        remote(p1.at[0], WA.at[gy, ox_, zp, oq_], w1s.at[other], w1r.at[other], dev).wait_recv()
        remote(sm, SM.at[gy, ox_, zp, oq_], m1s.at[other], m1r.at[other], dev).wait_recv()
    for i in range(1, d.n_zp):
        oz = lax.rem(zp + i, d.n_zp)
        dev = place(gy, gx, oz, q)
        go(remote(WA.at[gy, :, zp], WA.at[gy, :, zp], zs.at[0, oz], zr.at[0, zp], dev))
        go(remote(SM.at[gy, :, zp], SM.at[gy, :, zp], zs.at[1, oz], zr.at[1, zp], dev))
    for i in range(1, d.n_zp):
        oz = lax.rem(zp + i, d.n_zp)
        remote(wf2, WF2.at[gy, oz], zs.at[2, oz], zr.at[2, oz], place(gy, gx, oz, q)).wait_recv()
    for i in range(1, d.n_gy):
        oy = lax.rem(gy + i, d.n_gy)
        go(remote(WF2.at[gy], WF2.at[gy], ys.at[2, oy], yr.at[2, gy], place(oy, gx, zp, q)))
    for h in range(2):
        arrived(TOK, ts, tr, gx, qz, h)
        go(token_send(TOK.at[gx, qz], TOK, ts, tr, 5, gx, qz, h, c_dev))
        arrived(COT, cs, cr, 1 - gx, q, h)
        go(token_send(COT.at[1 - gx, q], COT, cs, cr, 5, 1 - gx, q, h, c_dev))
    for h in range(2):
        arrived(TOK, ts, tr, 1 - gx, qz, h)
        go(token_send(TOK.at[1 - gx, qz], TOK, ts, tr, 6, 1 - gx, qz, h, c_dev))
        arrived(COT, cs, cr, 1 - gx, qz, h)
        go(token_send(COT.at[1 - gx, qz], COT, cs, cr, 6, 1 - gx, qz, h, c_dev))
    for i in range(1, d.n_zp):
        oz = lax.rem(zp + i, d.n_zp)
        dev = place(gy, gx, oz, q)
        remote(WA.at[gy, :, oz], WA.at[gy, :, oz], zs.at[0, oz], zr.at[0, oz], dev).wait_recv()
        remote(SM.at[gy, :, oz], SM.at[gy, :, oz], zs.at[1, oz], zr.at[1, oz], dev).wait_recv()
    for i in range(1, d.n_gy):
        oy = lax.rem(gy + i, d.n_gy)
        dev = place(oy, gx, zp, q)
        go(remote(WA.at[gy], WA.at[gy], ys.at[0, oy], yr.at[0, gy], dev))
        go(remote(SM.at[gy], SM.at[gy], ys.at[1, oy], yr.at[1, gy], dev))
    qc = me.zl * 2 + 1 - me.c
    qcz = lax.rem(qc + 2, 4)
    for bx in (gx, 1 - gx):
        for bq in (qc, qcz):
            for h in range(2):
                arrived(TOK, ts, tr, bx, bq, h)
                arrived(COT, cs, cr, bx, bq, h)
    for i in range(1, d.n_gy):
        oy = lax.rem(gy + i, d.n_gy)
        dev = place(oy, gx, zp, q)
        for k, buf in enumerate((WA, SM, WF2)):
            remote(buf.at[oy], buf.at[oy], ys.at[k, oy], yr.at[k, oy], dev).wait_recv()
    for i in range(per):
        source = me.rank * per + i

        @pl.when(source != me.f)
        def _():
            remote(wo, WO.at[i], os_.at[0], or_.at[i], x_dev).wait_recv()

    for copy in sends:
        copy.wait_send()


def gather(d, tok, cot, p1, wo, wf2, sm):
    any_spec = pl.BlockSpec(memory_space=pl.ANY)
    dma = pltpu.SemaphoreType.DMA
    shape = jax.ShapeDtypeStruct
    return pl.pallas_call(
        functools.partial(gather_kernel, d),
        out_shape=(
            shape((2, 4, d.rows, d.width), BF),
            shape((2, 4, d.rows, d.width), BF),
            shape((d.n_gy, 2, d.n_zp, 4, d.r1, d.ca), BF),
            shape((128 // d.r1, d.r1, d.width), BF),
            shape((d.n_gy, d.n_zp, d.r2, d.width), BF),
            shape((d.n_gy, 2, d.n_zp, 4, 16, 128), BF),
        ),
        in_specs=[any_spec] * 6,
        out_specs=(any_spec,) * 6,
        scratch_shapes=[
            dma((6,)), dma((7, 2)), dma((8, 2)), dma((7, 2)), dma((8, 2)),
            dma((8,)), dma((8,)), dma((8,)), dma((8,)),
            dma((3, d.n_zp)), dma((3, d.n_zp)), dma((3, d.n_gy)), dma((3, d.n_gy)),
            dma((d.ng,)), dma((128 // d.r1,)),
        ],
        compiler_params=pltpu.CompilerParams(has_side_effects=True),
        name="gather",
    )(tok, cot, p1, wo, wf2, sm)


def add_blocks(out, *terms):
    n = out.shape[0]

    @pl.loop(0, n)
    def _(i):
        total = terms[0][i].astype(F32)
        for term in terms[1:]:
            total = total + term[i].astype(F32)
        out[i] = total.astype(out.dtype)


def reduce_kernel(d, mix, gh, ga, gf2, gwo, smg, MIX, GH, FA, FF2, FWO, FSM,
                  mt, m2, m3, ht, h2, h3, ya, y2, yo, za, z2, zo, s1, s2,
                  tsem, asem, fsem, osem, ssem, dsem):
    me = Me(d)
    gy, gx, zp, q, zl, c = me.gy, me.gx, me.zp, me.q, me.zl, me.c
    x_dev, z_dev, c_dev = place(gy, 1 - gx, zp, q), place(gy, gx, zp, lax.rem(q + 2, 4)), place(
        gy, gx, zp, zl * 2 + 1 - c
    )
    sends = []

    def go(copy):
        copy.start()
        sends.append(copy)

    for i in range(1, d.n_gy):
        oy = lax.rem(gy + i, d.n_gy)
        dev = place(oy, gx, zp, q)
        go(remote(gf2.at[:, :, oy], y2.at[gy], fsem.at[0, 0, oy], fsem.at[0, 1, gy], dev))
        go(remote(gwo.at[oy], yo.at[gy], osem.at[0, 0, oy], osem.at[0, 1, gy], dev))
        go(remote(ga.at[:, :, oy], ya.at[gy], asem.at[0, 0, oy], asem.at[0, 1, gy], dev))
    row_sums = ((mix, mt, m2, m3, MIX, 0), (gh, ht, h2, h3, GH, 1))
    for src, t_buf, _, _, _, k in row_sums:
        go(remote(src.at[:, :, 1 - c], t_buf, tsem.at[k, 0, 0], tsem.at[k, 1, 0], c_dev))
    for i in range(1, 8):
        other = lax.rem(me.rank + i, 8)
        oq = lax.rem(other, 4)
        go(remote(smg.at[oq], s1.at[me.rank], ssem.at[0, 0, other], ssem.at[0, 1, me.rank],
                  place(gy, other // 4, zp, oq)))
    for src, t_buf, b2, b3, _, k in row_sums:
        remote(src.at[:, :, 1 - c], t_buf, tsem.at[k, 0, 0], tsem.at[k, 1, 0], c_dev).wait_recv()
        for bx in range(2):
            for bz in range(2):
                add_blocks(t_buf.at[bx, bz], t_buf.at[bx, bz], src.at[bx, bz, c])
        if k == 0:
            go(remote(t_buf.at[1 - gx], b2, tsem.at[k, 0, 1], tsem.at[k, 1, 1], x_dev))
        else:
            go(remote(t_buf.at[:, 1 - zl], b2, tsem.at[k, 0, 1], tsem.at[k, 1, 1], z_dev))
    for i in range(1, d.n_gy):
        oy = lax.rem(gy + i, d.n_gy)
        dev = place(oy, gx, zp, q)
        remote(gf2.at[:, :, oy], y2.at[oy], fsem.at[0, 0, oy], fsem.at[0, 1, oy], dev).wait_recv()
        remote(gwo.at[oy], yo.at[oy], osem.at[0, 0, oy], osem.at[0, 1, oy], dev).wait_recv()
    others = [lax.rem(gy + i, d.n_gy) for i in range(1, d.n_gy)]
    for a in range(d.n_gy):
        for b in range(d.n_zp):
            add_blocks(y2.at[gy, a, b], gf2.at[a, b, gy], *[y2.at[o, a, b] for o in others])
    add_blocks(yo.at[gy], gwo.at[gy], *[yo.at[o] for o in others])
    for i in range(1, d.n_zp):
        oz = lax.rem(zp + i, d.n_zp)
        dev = place(gy, gx, oz, q)
        go(remote(y2.at[gy, oz], z2.at[zp], fsem.at[1, 0, oz], fsem.at[1, 1, zp], dev))
        go(remote(yo.at[gy], zo.at[zp], osem.at[1, 0, oz], osem.at[1, 1, zp], dev))
    for i in range(1, d.n_gy):
        oy = lax.rem(gy + i, d.n_gy)
        dev = place(oy, gx, zp, q)
        remote(ga.at[:, :, oy], ya.at[oy], asem.at[0, 0, oy], asem.at[0, 1, oy], dev).wait_recv()
    for a in range(d.n_zp):
        for b in range(4):
            add_blocks(ya.at[gy, a, b], ga.at[a, b, gy], *[ya.at[o, a, b] for o in others])
    for i in range(1, d.n_zp):
        oz = lax.rem(zp + i, d.n_zp)
        go(remote(ya.at[gy, oz], za.at[zp], asem.at[1, 0, oz], asem.at[1, 1, zp],
                  place(gy, gx, oz, q)))
    for i in range(1, 8):
        other = lax.rem(me.rank + i, 8)
        remote(smg.at[0], s1.at[other], ssem.at[0, 0, other], ssem.at[0, 1, other],
               x_dev).wait_recv()
    s1[me.rank] = smg[q]
    total = s1[0]
    for i in range(1, 8):
        total = total + s1[i]
    s2[d.ng] = total
    own_group = gy * d.n_zp + zp
    for i in range(1, d.ng):
        group = lax.rem(own_group + i, d.ng)
        oy, oz = group // d.n_zp, lax.rem(group, d.n_zp)
        go(remote(s2.at[d.ng, oz], s2.at[own_group, 0], ssem.at[1, 0, group],
                  ssem.at[1, 1, own_group], place(oy, gx, oz, q)))
    for src, t_buf, b2, b3, _, k in row_sums:
        if k == 0:
            remote(t_buf.at[1 - gx], b2, tsem.at[k, 0, 1], tsem.at[k, 1, 1], x_dev).wait_recv()
            for b in range(2):
                add_blocks(b2.at[b], b2.at[b], t_buf.at[gx, b])
            go(remote(b2.at[1 - zl], b3, tsem.at[k, 0, 2], tsem.at[k, 1, 2], z_dev))
        else:
            remote(t_buf.at[:, 1 - zl], b2, tsem.at[k, 0, 1], tsem.at[k, 1, 1], z_dev).wait_recv()
            for b in range(2):
                add_blocks(b2.at[b], b2.at[b], t_buf.at[b, zl])
            go(remote(b2.at[1 - gx], b3, tsem.at[k, 0, 2], tsem.at[k, 1, 2], x_dev))
    zothers = [lax.rem(zp + i, d.n_zp) for i in range(1, d.n_zp)]
    for o in zothers:
        dev = place(gy, gx, o, q)
        remote(y2.at[gy, o], z2.at[o], fsem.at[1, 0, o], fsem.at[1, 1, o], dev).wait_recv()
        remote(yo.at[gy], zo.at[o], osem.at[1, 0, o], osem.at[1, 1, o], dev).wait_recv()
    hz = d.n_zp // 2
    for b in range(d.n_zp):
        add_blocks(z2.at[zp, b], y2.at[gy, zp, b], *[z2.at[o, b] for o in zothers])
    add_blocks(zo.at[zp], yo.at[gy], *[zo.at[o] for o in zothers])
    for j in range(2):
        dq = gx * 2 + j
        for ox in range(2):
            mine = jnp.logical_and(ox == gx, dq == q)
            src = z2.at[zp, pl.ds(j * hz, hz)]
            dst = FF2.at[gy, q]
            copy = remote(src, dst, dsem.at[0, 0, j * 2 + ox], dsem.at[0, 1, q],
                          place(gy, ox, zp, dq))

            @pl.when(mine)
            def _():
                here = pltpu.make_async_copy(src, dst, dsem.at[0, 2, 0])
                here.start()
                here.wait()

            @pl.when(jnp.logical_not(mine))
            def _():
                copy.start()
    nwo = 128 // d.rd
    wo_zp = me.rank * d.n_zp // 8
    for j in range(nwo):
        dq = lax.rem(me.rank * nwo + j, 4)
        for ox in range(2):
            here_too = jnp.logical_and(ox == gx, dq == q)
            src = zo.at[zp, pl.ds(j * (d.rd // 16), d.rd // 16)]
            dst = FWO.at[gy]
            copy = remote(src, dst, dsem.at[1, 0, j * 2 + ox], dsem.at[1, 1, 0],
                          place(gy, ox, zp, dq))

            @pl.when(jnp.logical_and(wo_zp == zp, here_too))
            def _():
                here = pltpu.make_async_copy(src, dst, dsem.at[1, 2, 0])
                here.start()
                here.wait()

            @pl.when(jnp.logical_and(wo_zp == zp, jnp.logical_not(here_too)))
            def _():
                copy.start()
    for o in zothers:
        dev = place(gy, gx, o, q)
        remote(ya.at[gy, o], za.at[o], asem.at[1, 0, o], asem.at[1, 1, o], dev).wait_recv()
    for b in range(4):
        add_blocks(za.at[zp, b], ya.at[gy, zp, b], *[za.at[o, b] for o in zothers])
    for i in range(1, 8):
        other = lax.rem(me.rank + i, 8)
        ox, oq = other // 4, lax.rem(other, 4)
        go(remote(za.at[zp, oq], FA.at[gy, gx, q], dsem.at[2, 0, other],
                  dsem.at[2, 1, me.rank], place(gy, ox, zp, oq)))
    here = pltpu.make_async_copy(za.at[zp, q], FA.at[gy, gx, q], dsem.at[2, 2, 0])
    here.start()
    here.wait()
    for src, t_buf, b2, b3, out, k in row_sums:
        if k == 0:
            remote(b2.at[1 - zl], b3, tsem.at[k, 0, 2], tsem.at[k, 1, 2], z_dev).wait_recv()
            mine = b2.at[zl]
        else:
            remote(b2.at[1 - gx], b3, tsem.at[k, 0, 2], tsem.at[k, 1, 2], x_dev).wait_recv()
            mine = b2.at[gx]
        n = out.shape[0]
        for i in range(n):
            out[i] = mine[i].astype(F32) + b3[i].astype(F32)
    for sq in range(4):
        away = jnp.logical_not(jnp.logical_and(gx == zl, sq == q))

        @pl.when(away)
        def _():
            remote(z2.at[0, pl.ds(0, hz)], FF2.at[gy, sq], dsem.at[0, 0, 0], dsem.at[0, 1, sq],
                   x_dev).wait_recv()
    source = (zp * 4 + q) // nwo
    sx, sq = source // 4, lax.rem(source, 4)

    @pl.when(jnp.logical_not(jnp.logical_and(sx == gx, sq == q)))
    def _():
        remote(zo.at[0, pl.ds(0, d.rd // 16)], FWO.at[gy], dsem.at[1, 0, 0], dsem.at[1, 1, 0],
               x_dev).wait_recv()
    for o in others:
        dev = place(o, gx, zp, q)
        go(remote(FF2.at[gy], FF2.at[gy], fsem.at[2, 0, o], fsem.at[2, 1, gy], dev))
        go(remote(FWO.at[gy], FWO.at[gy], osem.at[2, 0, o], osem.at[2, 1, gy], dev))
    for i in range(1, 8):
        other = lax.rem(me.rank + i, 8)
        ox, oq = other // 4, lax.rem(other, 4)
        remote(za.at[0, 0], FA.at[gy, ox, oq], dsem.at[2, 0, other], dsem.at[2, 1, other],
               x_dev).wait_recv()
    for o in others:
        dev = place(o, gx, zp, q)
        go(remote(FA.at[gy], FA.at[gy], asem.at[2, 0, o], asem.at[2, 1, gy], dev))
    for i in range(1, d.ng):
        group = lax.rem(own_group + i, d.ng)
        remote(s2.at[d.ng, 0], s2.at[group, 0], ssem.at[1, 0, group], ssem.at[1, 1, group],
               x_dev).wait_recv()
    total = s2[d.ng, zp]
    for i in range(1, d.ng):
        total = total + s2[lax.rem(own_group + i, d.ng), 0]
    FSM[...] = total
    for o in others:
        dev = place(o, gx, zp, q)
        for buf, sem in ((FF2, fsem), (FWO, osem), (FA, asem)):
            remote(buf.at[o], buf.at[o], sem.at[2, 0, o], sem.at[2, 1, o], dev).wait_recv()
    for copy in sends:
        copy.wait_send()
    for j in range(2):
        for ox in range(2):
            away = jnp.logical_not(jnp.logical_and(ox == gx, gx * 2 + j == q))

            @pl.when(away)
            def _():
                remote(z2.at[zp, pl.ds(j * hz, hz)], FF2.at[gy, q], dsem.at[0, 0, j * 2 + ox],
                       dsem.at[0, 1, q], x_dev).wait_send()
    for j in range(nwo):
        dq = lax.rem(me.rank * nwo + j, 4)
        for ox in range(2):
            away = jnp.logical_not(jnp.logical_and(ox == gx, dq == q))

            @pl.when(jnp.logical_and(wo_zp == zp, away))
            def _():
                remote(zo.at[zp, pl.ds(j * (d.rd // 16), d.rd // 16)], FWO.at[gy], dsem.at[1, 0, j * 2 + ox],
                       dsem.at[1, 1, 0], x_dev).wait_send()


def reduce_all(d, mix, gh, ga, gf2, gwo, smg):
    vm = pl.BlockSpec(memory_space=pltpu.VMEM)
    dma = pltpu.SemaphoreType.DMA
    shape = jax.ShapeDtypeStruct
    R = d.rows
    slabs = R // 16
    return pl.pallas_call(
        functools.partial(reduce_kernel, d),
        out_shape=(
            shape((slabs, 16, d.width), F32),
            shape((slabs, 16, d.width), F32),
            shape((d.n_gy, 2, 4, d.rdg // 16, 16, d.ca), BF),
            shape((d.n_gy, 4, d.n_zp // 2, d.r2 // 16, 16, d.c2), BF),
            shape((d.n_gy, d.rd // 16, 16, d.c2), BF),
            shape((8, 128), F32),
        ),
        in_specs=[vm] * 6,
        out_specs=(vm,) * 6,
        scratch_shapes=[
            pltpu.VMEM((2, 2, slabs, 16, d.width), BF),
            pltpu.VMEM((2, slabs, 16, d.width), BF),
            pltpu.VMEM((slabs, 16, d.width), BF),
            pltpu.VMEM((2, 2, slabs, 16, d.width), BF),
            pltpu.VMEM((2, slabs, 16, d.width), BF),
            pltpu.VMEM((slabs, 16, d.width), BF),
            pltpu.VMEM((d.n_gy, d.n_zp, 4, d.rdg // 16, 16, d.ca), BF),
            pltpu.VMEM((d.n_gy, d.n_gy, d.n_zp, d.r2 // 16, 16, d.c2), BF),
            pltpu.VMEM((d.n_gy, 8, 16, d.c2), BF),
            pltpu.VMEM((d.n_zp, 4, d.rdg // 16, 16, d.ca), BF),
            pltpu.VMEM((d.n_zp, d.n_zp, d.r2 // 16, 16, d.c2), BF),
            pltpu.VMEM((d.n_zp, 8, 16, d.c2), BF),
            pltpu.VMEM((8, d.n_zp, 8, 128), F32),
            pltpu.VMEM((d.ng + 1, d.n_zp, 8, 128), F32),
            dma((2, 2, 3)),
            dma((3, 2, max(d.n_gy, d.n_zp))),
            dma((3, 2, max(d.n_gy, d.n_zp))),
            dma((3, 2, max(d.n_gy, d.n_zp))),
            dma((2, 2, max(8, d.ng))),
            dma((3, 3, 8)),
        ],
        compiler_params=pltpu.CompilerParams(
            has_side_effects=True, vmem_limit_bytes=62 * 1024 * 1024
        ),
        name="reduce",
    )(mix, gh, ga, gf2, gwo, smg)


def gelu_parts(v):
    tangent = jnp.tanh(0.7978845608028654 * (v + 0.044715 * v * v * v))
    inner = 0.7978845608028654 * (1.0 + 0.134145 * v * v)
    act = 0.5 * v * (1.0 + tangent)
    slope = 0.5 * (1.0 + tangent) + 0.5 * v * (1.0 - tangent * tangent) * inner
    return act, slope


def places_of_slot(rows):
    slot = 4 * rows
    row = jnp.arange(slot, dtype=jnp.int32)
    piece, inner, half = row // rows, row % rows, rows // 2
    return jnp.where(inner < half, piece * half + inner, slot - (piece + 1) * half + inner - half)


def spread(vec, lane):
    n = vec.shape[0]
    if n == 128:
        return vec
    tiled = jnp.tile(vec, 128 // n)
    at = jnp.arange(128, dtype=jnp.int32) // n
    return jnp.where(at == lane, tiled, jnp.zeros_like(tiled))


def dot(a, b, dims):
    return lax.dot_general(a, b, (dims, ((), ())), preferred_element_type=F32)


def local(d, tokens, cotangent, lengths, offsets, ln_gain, ln_bias, w_qkv, w_out, w_fc1, b_fc1,
          w_fc2, b_fc2):
    me = Me(d)
    R, W = d.rows, d.width
    fc1 = w_fc1.reshape(d.r1, d.n_gy, 2, d.n_zp, 4, d.r2).transpose(2, 4, 0, 1, 3, 5)
    fc1 = fc1.reshape(8, d.r1, d.ffs)
    qkv = w_qkv.reshape(d.r1, 3, 8, 128).transpose(2, 0, 1, 3).reshape(8, d.r1, d.qs)
    p1 = jnp.concatenate([fc1, qkv], axis=2)
    lane = lax.rem(me.f, 128 // d.r1)
    pad = jnp.zeros((128 - d.r2,), BF)
    sm = jnp.stack([spread(ln_gain, lane), spread(ln_bias, lane), spread(b_fc2, lane),
                    jnp.concatenate([b_fc1, pad]) if d.r2 < 128 else b_fc1])
    sm = jnp.concatenate([sm, jnp.zeros((12, 128), BF)])
    TOK, COT, WA, WO, WF2, SM = gather(d, tokens, cotangent, p1, w_out, w_fc2, sm)
    sums = SM.reshape(8, d.n_all // 8, 16, 128).astype(F32).sum(axis=1)
    gain, bias, bfc2 = sums[:, 0].reshape(W), sums[:, 1].reshape(W), sums[:, 2].reshape(W)
    mine = lax.dynamic_index_in_dim(
        lax.dynamic_index_in_dim(SM, me.gx, 1, False), me.q, 2, False
    )
    bfc1 = mine[:, :, 3, : d.r2].reshape(d.ffs).astype(F32)
    WA = WA.reshape(W, d.ca)
    wfc1, wqkv = WA[:, : d.ffs], WA[:, d.ffs :]
    wout = WO.reshape(128, W)
    wfc2 = WF2.reshape(d.ffs, W)
    slot0 = (me.gy * 2) * d.n_zp + me.zp
    lens = jnp.stack([lengths[slot0], lengths[slot0 + d.n_zp]])
    offs = jnp.stack([offsets[slot0], offsets[slot0 + d.n_zp]])
    places = places_of_slot(R)
    live = (places[None] >= offs[:, None]) & (places[None] < (offs + lens)[:, None])
    live_f = live.reshape(8 * R, 1).astype(F32)
    tok = TOK.reshape(8 * R, W).astype(F32)
    centred = tok - jnp.mean(tok, axis=-1, keepdims=True)
    inverse = lax.rsqrt(jnp.mean(centred * centred, axis=-1, keepdims=True) + 1e-5)
    normed = centred * inverse
    h = (normed * gain + bias).astype(BF)
    grad_y = (COT.reshape(8 * R, W).astype(F32) * live_f).astype(BF)
    qkv = dot(h, wqkv, ((1,), (0,)))
    freq = jnp.exp(jnp.arange(ROT // 2, dtype=F32) * (-2.0 * math.log(10000.0) / ROT))
    angles = (places[None] - offs[:, None]).astype(F32).reshape(8 * R)[:, None] * freq[None]
    cos, sin = jnp.cos(angles)[:, None], jnp.sin(angles)[:, None]

    def turn(x, sign):
        a, b = x[..., : ROT // 2], x[..., ROT // 2 : ROT]
        return jnp.concatenate(
            [a * cos - sign * b * sin, b * cos + sign * a * sin, x[..., ROT:]], axis=-1
        )

    queries = turn(qkv[:, :128].reshape(8 * R, 2, HD), 1.0).astype(BF).reshape(2, 4 * R, 2, HD)
    keys = turn(qkv[:, 128:256].reshape(8 * R, 2, HD), 1.0).astype(BF).reshape(2, 4 * R, 2, HD)
    values = qkv[:, 256:].astype(BF).reshape(2, 4 * R, 2, HD)
    scores = jnp.einsum("sqhd,skhd->shqk", queries, keys, preferred_element_type=F32) * 0.125
    allowed = (places[None, None, :] <= places[None, :, None]) & (
        live[:, None, :] | (places[None, None, :] == places[None, :, None])
    )
    scores = jnp.where(allowed[:, None], scores, -1e30)
    expo = jnp.exp(scores - jnp.max(scores, axis=-1, keepdims=True))
    prob = expo / jnp.sum(expo, axis=-1, keepdims=True)
    low = prob.astype(BF)
    att = jnp.einsum("shqk,skhd->sqhd", low, values, preferred_element_type=F32)
    att = att.astype(BF).reshape(8 * R, 128)
    pre = dot(h, wfc1, ((1,), (0,))) + bfc1
    act, slope = gelu_parts(pre)
    act = act.astype(BF)
    mix = dot(att, wout, ((1,), (0,))) + dot(act, wfc2, ((1,), (0,)))
    g_wo = dot(att, grad_y, ((0,), (0,)))
    g_f2 = dot(act, grad_y, ((0,), (0,)))
    grad_pre = (dot(grad_y, wfc2, ((1,), (1,))) * slope).astype(BF)
    g_f1 = dot(h, grad_pre, ((0,), (0,)))
    g_bf1 = grad_pre.astype(F32).sum(axis=0)
    grad_att = dot(grad_y, wout, ((1,), (1,))).astype(BF).reshape(2, 4 * R, 2, HD)
    g_prob = jnp.einsum("sqhd,skhd->shqk", grad_att, values, preferred_element_type=F32)
    row_dot = jnp.sum(prob * g_prob, axis=-1, keepdims=True)
    g_score = (prob * (g_prob - row_dot)).astype(BF)
    g_v = jnp.einsum("shqk,sqhd->skhd", low, grad_att, preferred_element_type=F32)
    g_q = jnp.einsum("shqk,skhd->sqhd", g_score, keys, preferred_element_type=F32) * 0.125
    g_k = jnp.einsum("shqk,sqhd->skhd", g_score, queries, preferred_element_type=F32) * 0.125
    g_q = turn(g_q.reshape(8 * R, 2, HD), -1.0).reshape(8 * R, 128)
    g_k = turn(g_k.reshape(8 * R, 2, HD), -1.0).reshape(8 * R, 128)
    g_qkv = jnp.concatenate([g_q, g_k, g_v.reshape(8 * R, 128)], axis=1).astype(BF)
    g_wqkv = dot(h, g_qkv, ((0,), (0,)))
    gh = dot(grad_pre, wfc1, ((1,), (1,))) + dot(g_qkv, wqkv, ((1,), (1,)))
    g_gain, g_bias = (gh * normed).sum(axis=0), gh.sum(axis=0)
    g_bf2 = jnp.where(me.rank == 0, grad_y.astype(F32).sum(axis=0), 0.0)
    nd, per = d.n_dev, W // d.n_dev

    def wide(x):
        x = x.reshape(nd, -1)
        n = x.shape[1]
        if n < 128:
            x = jnp.concatenate([x, jnp.zeros((nd, 128 - n), F32)], axis=1)
        return x.reshape(nd, -1, 128)

    bf1_rows = max(d.ff // nd // 128, 1)
    full = jnp.zeros((d.n_gy, 2, d.n_zp, 4, d.r2), F32)
    full = lax.dynamic_update_slice(
        full, g_bf1.reshape(d.n_gy, 1, d.n_zp, 1, d.r2), (0, me.gx, 0, me.q, 0)
    )
    smg = jnp.concatenate(
        [wide(g_gain), wide(g_bias), wide(g_bf2), wide(full.reshape(d.ff)),
         jnp.zeros((nd, 5 - bf1_rows, 128), F32)], axis=1,
    )
    smg = smg.reshape(d.n_zp, 4, 8, 128).transpose(1, 0, 2, 3)
    slabs = R // 16
    mix_p = mix.astype(BF).reshape(2, 2, 2, slabs, 16, W)
    gh_p = gh.astype(BF).reshape(2, 2, 2, slabs, 16, W)
    ga = jnp.concatenate([g_f1, g_wqkv], axis=1).astype(BF)
    ga = ga.reshape(d.n_zp, 4, d.n_gy, d.rdg // 16, 16, d.ca)
    gf2 = g_f2.astype(BF).reshape(d.n_gy, d.n_zp, d.r2 // 16, 16, d.n_gy, d.c2)
    gf2 = gf2.transpose(0, 1, 4, 2, 3, 5)
    gwo = g_wo.astype(BF).reshape(8, 16, d.n_gy, d.c2).transpose(2, 0, 1, 3)
    MIX, GH, FA, FF2, FWO, FSM = reduce_all(d, mix_p, gh_p, ga, gf2, gwo, smg)
    own = me.gx * 4 + me.q

    def own_rows(x):
        return lax.dynamic_index_in_dim(x.reshape(8, R, x.shape[-1]), own, 0, False)

    my_live, my_normed, my_inv = own_rows(live_f), own_rows(normed), own_rows(inverse)
    mixed = (my_live * (tokens.astype(F32) + MIX.reshape(R, W) + bfc2)).astype(BF)
    scaled = GH.reshape(R, W) * gain
    grad_norm = my_inv * (
        scaled - jnp.mean(scaled, axis=-1, keepdims=True)
        - my_normed * jnp.mean(scaled * my_normed, axis=-1, keepdims=True)
    )
    token_grad = (cotangent.astype(F32) * my_live + grad_norm).astype(BF)
    FA = FA.reshape(d.n_gy, 2, 4, d.rdg, d.ca)
    o_f1 = FA[..., : d.ffs].reshape(d.n_gy, 2, 4, d.rdg, d.n_gy, d.n_zp, d.r2)
    o_f1 = o_f1.transpose(0, 3, 4, 1, 5, 2, 6).reshape(d.rd, d.ff).astype(F32)
    o_qkv = FA[..., d.ffs :].reshape(d.n_gy, 8, d.rdg, 3, 128)
    o_qkv = o_qkv.transpose(0, 2, 3, 1, 4).reshape(d.rd, 3 * W).astype(F32)
    o_f2 = FF2.reshape(d.n_gy, 4, d.n_zp // 2, d.r2, d.c2).transpose(2, 1, 3, 0, 4)
    o_f2 = o_f2.reshape(d.ff // nd, W).astype(F32)
    o_wo = FWO.reshape(d.n_gy, d.rd, d.c2).transpose(1, 0, 2).reshape(d.rd, W).astype(F32)
    o_gain, o_bias, o_bf2 = FSM[0, :per], FSM[1, :per], FSM[2, :per]
    o_bf1 = FSM[3 : 3 + bf1_rows].reshape(-1)[: d.ff // nd]
    return mixed, token_grad, o_gain, o_bias, o_qkv, o_wo, o_f1, o_bf1, o_f2, o_bf2


def cdot(a, b, ca, cb):
    return lax.dot_general(a, b, (((ca,), (cb,)), ((), ())), preferred_element_type=F32)


def rows_at(start, n):
    return pl.ds(pl.multiple_of(start, n), n)


def layer_kernel(d, lens, offs, tok, cot, wqkv, wo, wfc1, wf2, sm, c0, s0,
                 MIXED, TGRAD, F1, FQ, F2, FWO, FSM,
                 TOK, COT, H, HT, Q, K, V, KT, VT, P0, P1, P2, P3, ACT, AT, SG, ATT, GATT, GQKV,
                 DK, DV, MIXP, WF1, WQ, WF2, WO, SM, VEC, BF1, SMG, SUMS, OWN,
                 mt, m2, m3, ht, h2, h3, GB, GA, GQ, yb, ya, yq, zb, za, zq, s1, s2,
                 loc, ts, tr, cs, cr, w1s, w1r, zs, zr, ys, yr, os_, or_,
                 tsem, bsem, asem, qsem, ssem, dsem):
    me = Me(d)
    gy, gx, zp, q, zl, c = me.gy, me.gx, me.zp, me.q, me.zl, me.c
    half, R, W = d.rows // 2, d.rows, d.width
    S = 4 * R
    PT = (P0, P1, P2, P3)
    qz, qc = lax.rem(q + 2, 4), zl * 2 + 1 - c
    qcz = lax.rem(qc + 2, 4)
    x_dev, z_dev, c_dev = place(gy, 1 - gx, zp, q), place(gy, gx, zp, qz), place(gy, gx, zp, qc)
    oz, oy = 1 - zp, 1 - gy
    zz_dev, yy_dev = place(gy, gx, oz, q), place(oy, gx, zp, q)
    sends, cot_sends = [], []

    def go(copy, kept=sends):
        copy.start()
        kept.append(copy)

    def block(bx, bq, h):
        pb = bq if h == 0 else 7 - bq
        return rows_at(bx * S + pb * half, half)

    def tsend(src, buf, send, recv, slot, bx, bq, h, device):
        return remote(src, buf.at[block(bx, bq, h)], send.at[slot, h], recv.at[bx * 4 + bq, h], device)

    TOKS, COTS = (tok, TOK, ts, tr, sends), (cot, COT, cs, cr, cot_sends)

    def x_first(arr, h):
        return arr is TOKS and h == 0

    def own_half(src, h):
        return src.at[pl.ds(h * half, half)]

    def first(arr, h):
        src, buf, send, recv, kept = arr
        go(tsend(own_half(src, h), buf, send, recv, 0, gx, q, h, x_dev if x_first(arr, h) else z_dev), kept)

    def second(arr, h):
        src, buf, send, recv, kept = arr
        go(tsend(own_half(src, h), buf, send, recv, 1, gx, q, h, z_dev if x_first(arr, h) else x_dev), kept)
        go(tsend(own_half(src, h), buf, send, recv, 3, gx, q, h, c_dev), kept)

    def wait_block(arr, bx, bq, h):
        _, buf, send, recv, kept = arr
        tsend(buf.at[block(bx, bq, h)], buf, send, recv, 0, bx, bq, h, x_dev).wait_recv()

    def pass_on(arr, slot, bx, bq, h, device):
        _, buf, send, recv, kept = arr
        go(tsend(buf.at[block(bx, bq, h)], buf, send, recv, slot, bx, bq, h, device), kept)

    def relay_first(arr, h):
        bx, bq = (1 - gx, q) if x_first(arr, h) else (gx, qz)
        wait_block(arr, bx, bq, h)
        pass_on(arr, 2, bx, bq, h, z_dev if x_first(arr, h) else x_dev)
        pass_on(arr, 4, bx, bq, h, c_dev)

    def relay_second(arr, h):
        bx, bq = (gx, qz) if x_first(arr, h) else (1 - gx, q)
        wait_block(arr, bx, bq, h)
        pass_on(arr, 5, bx, bq, h, c_dev)
        wait_block(arr, 1 - gx, qz, h)
        pass_on(arr, 6, 1 - gx, qz, h, c_dev)

    def wait_twin(arr):
        for bx in (gx, 1 - gx):
            for bq in (qc, qcz):
                for h in range(2):
                    wait_block(arr, bx, bq, h)

    own_rows = rows_at(q * d.r1, d.r1)
    local = [
        pltpu.make_async_copy(sm, SM.at[gy, gx, zp, q], loc.at[0]),
        pltpu.make_async_copy(wf2, WF2.at[gy, zp], loc.at[1]),
    ]
    for h in range(2):
        local.append(pltpu.make_async_copy(own_half(tok, h), TOK.at[block(gx, q, h)], loc.at[2 + h]))
        local.append(pltpu.make_async_copy(own_half(cot, h), COT.at[block(gx, q, h)], loc.at[4 + h]))
    local.append(pltpu.make_async_copy(cot, OWN, loc.at[7]))

    def fc1_pieces(ox, oq):
        for b in range(d.ng):
            f = ((b // d.n_zp * 2 + ox) * d.n_zp + b % d.n_zp) * 4 + oq
            yield (wfc1.at[:, rows_at(f * d.r2, d.r2)],
                   WF1.at[gy, gx, zp, own_rows, pl.ds(b * d.r2, d.r2)])

    def qkv_pieces(rank):
        for k in range(3):
            yield (wqkv.at[:, rows_at(k * W + rank * 128, 128)],
                   WQ.at[gy, gx, zp, own_rows, pl.ds(k * 128, 128)])

    for i in range(1, 8):
        other = lax.rem(me.rank + i, 8)
        ox, oq = other // 4, lax.rem(other, 4)
        dev = place(gy, ox, zp, oq)
        for src, dst in qkv_pieces(other):
            remote(src, dst, w1s.at[0, other], w1r.at[0, me.rank], dev).start()
        go(remote(sm, SM.at[gy, gx, zp, q], w1s.at[2, other], w1r.at[2, me.rank], dev))
    for src, dst in qkv_pieces(me.rank):
        pltpu.make_async_copy(src, dst, w1r.at[0, me.rank]).start()
    for h in range(2):
        first(TOKS, h)
    for copy in local:
        copy.start()
    for i in range(1, 8):
        other = lax.rem(me.rank + i, 8)
        ox, oq = other // 4, lax.rem(other, 4)
        for src, dst in fc1_pieces(ox, oq):
            remote(src, dst, w1s.at[1, other], w1r.at[1, me.rank], place(gy, ox, zp, oq)).start()
    for src, dst in fc1_pieces(gx, q):
        pltpu.make_async_copy(src, dst, w1r.at[1, me.rank]).start()
    def w1_region(buf, ox, oq):
        return buf.at[gy, ox, zp, rows_at(oq * d.r1, d.r1)]

    def wait_w1(k, buf):
        for i in range(1, 8):
            other = lax.rem(me.rank + i, 8)
            dst = w1_region(buf, other // 4, lax.rem(other, 4))
            remote(dst, dst, w1s.at[k, other], w1r.at[k, other], x_dev).wait_recv()
        dst = w1_region(buf, gx, q)
        pltpu.make_async_copy(dst, dst, w1r.at[k, me.rank]).wait()

    for copy in local:
        copy.wait()
    wait_w1(0, WQ)
    for i in range(1, 8):
        other = lax.rem(me.rank + i, 8)
        dst = SM.at[gy, other // 4, zp, lax.rem(other, 4)]
        remote(sm, dst, w1s.at[2, other], w1r.at[2, other], x_dev).wait_recv()
    go(remote(SM.at[gy, :, zp], SM.at[gy, :, zp], zs.at[2], zr.at[2], zz_dev))
    go(remote(WQ.at[gy, :, zp], WQ.at[gy, :, zp], zs.at[0], zr.at[0], zz_dev))
    for h in range(2):
        second(TOKS, h)
    wait_w1(1, WF1)
    go(remote(WF1.at[gy, :, zp], WF1.at[gy, :, zp], zs.at[1], zr.at[1], zz_dev))
    for h in range(2):
        relay_first(TOKS, h)
    go(remote(wf2, WF2.at[gy, zp], zs.at[3], zr.at[3], zz_dev))
    for h in range(2):
        first(COTS, h)
    for h in range(2):
        second(COTS, h)
    per = 128 // d.r1
    owner = me.f // per
    part = lax.rem(me.f, per)
    wx, wq = owner // 4, lax.rem(owner, 4)
    wo_mine = jnp.logical_and(wx == gx, wq == q)
    wo_dst = WO.at[rows_at(part * d.r1, d.r1)]
    wo_own = remote(wo, wo_dst, os_.at[0], or_.at[part], place(gy, wx, zp, wq))
    wo_here = pltpu.make_async_copy(wo, wo_dst, loc.at[6])
    for i in range(1, d.ng):
        group = lax.rem(gy * d.n_zp + zp + i, d.ng)
        go(remote(wo, wo_dst, os_.at[i], or_.at[part],
                  place(group // d.n_zp, wx, lax.rem(group, d.n_zp), wq)))

    @pl.when(wo_mine)
    def _():
        wo_here.start()

    @pl.when(jnp.logical_not(wo_mine))
    def _():
        wo_own.start()

    remote(SM.at[gy, :, oz], SM.at[gy, :, oz], zs.at[2], zr.at[2], zz_dev).wait_recv()
    go(remote(SM.at[gy], SM.at[gy], ys.at[2], yr.at[2], yy_dev))
    remote(WQ.at[gy, :, oz], WQ.at[gy, :, oz], zs.at[0], zr.at[0], zz_dev).wait_recv()
    go(remote(WQ.at[gy], WQ.at[gy], ys.at[0], yr.at[0], yy_dev))
    for h in range(2):
        relay_second(TOKS, h)
    wait_twin(TOKS)
    remote(SM.at[oy], SM.at[oy], ys.at[2], yr.at[2], yy_dev).wait_recv()
    in_lane = lax.broadcasted_iota(jnp.int32, (8, 128), 1) // d.r1
    parts = 128 // d.r1
    for j in range(8):
        rows3 = [jnp.zeros((8, 128), F32)] * 3
        for k in range(parts):
            g_, dv = divmod(j * parts + k, d.n_dev)
            packed = SM[g_ // 2, g_ % 2, dv // 4, dv % 4].astype(F32)[0:8]
            for v in range(3):
                turn = (k - v) % parts * d.r1
                moved = pltpu.roll(packed, turn, 1) if turn else packed
                rows3[v] = jnp.where(in_lane == k, moved, rows3[v])
        for v in range(3):
            VEC[v : v + 1, j * 128 : (j + 1) * 128] = rows3[v][0:1]
    for b in range(d.ng):
        BF1[:, b * 128 : (b + 1) * 128] = SM[b // d.n_zp, gx, b % d.n_zp, q].astype(F32)
    SUMS[...] = jnp.zeros_like(SUMS)

    def slot_of(s):
        index = (gy * 2 + s) * d.n_zp + zp
        return lens[index], offs[index]

    def normalise(rows):
        x = rows.astype(F32)
        centred = x - jnp.mean(x, axis=-1, keepdims=True)
        inverse = lax.rsqrt(jnp.mean(centred * centred, axis=-1, keepdims=True) + 1e-5)
        return centred * inverse, inverse

    def live_column(s, first_place, n):
        length, offset = slot_of(s)
        at = lax.broadcasted_iota(jnp.int32, (n, 1), 0) + first_place
        return jnp.logical_and(at >= offset, at < offset + length)

    def live_row(s, first_place, n):
        length, offset = slot_of(s)
        at = lax.broadcasted_iota(jnp.int32, (1, n), 1) + first_place
        return jnp.logical_and(at >= offset, at < offset + length)

    @pl.loop(0, 8)
    def _(i):
        normed, _ = normalise(TOK[rows_at(i * R, R), :])
        h = (normed * VEC[0:1, :] + VEC[1:2, :]).astype(BF)
        H[rows_at(i * R, R), :] = h
        HT[:, rows_at(i * R, R)] = h.T

    relay_first(COTS, 0)
    remote(WF1.at[gy, :, oz], WF1.at[gy, :, oz], zs.at[1], zr.at[1], zz_dev).wait_recv()
    go(remote(WF1.at[gy], WF1.at[gy], ys.at[1], yr.at[1], yy_dev))
    remote(WQ.at[oy], WQ.at[oy], ys.at[0], yr.at[0], yy_dev).wait_recv()

    lane = lax.rem(lax.broadcasted_iota(jnp.int32, (1, 128), 1), 64)

    def turn_tables_of(s, t):
        _, offset = slot_of(s)
        co, so = c0[pl.ds(offset, 1), :], s0[pl.ds(offset, 1), :]
        cc, ss = c0[rows_at(t * R, R), :], s0[rows_at(t * R, R), :]
        cos = cc * co + ss * so
        sin = ss * co - cc * so
        cos = jnp.where(lane < ROT, cos, 1.0)
        sin = jnp.where(lane < ROT // 2, -sin, jnp.where(lane < ROT, sin, 0.0))
        return cos, sin

    def turned(x, cos, sin):
        other = jnp.where(lane < ROT // 2, pltpu.roll(x, 128 - ROT // 2, 1), pltpu.roll(x, ROT // 2, 1))
        return x * cos + other * sin

    wq_all = (W, d.qs)

    @pl.loop(0, 8)
    def _(i):
        s, t = i // 4, lax.rem(i, 4)
        rows = rows_at(i * R, R)
        qkv = cdot(H[rows, :], WQ[...].reshape(wq_all), 1, 0)
        cos, sin = turn_tables_of(s, t)
        query = turned(qkv[:, :128], cos, sin).astype(BF)
        Q[rows, :] = (query.astype(F32) * 0.125).astype(BF)
        key = turned(qkv[:, 128:256], cos, sin).astype(BF)
        K[rows, :] = key
        KT[:, rows] = key.T
        value = qkv[:, 256:].astype(BF)
        V[rows, :] = value
        VT[:, rows] = value.T

    relay_first(COTS, 1)
    remote(WF2.at[gy, oz], WF2.at[gy, oz], zs.at[3], zr.at[3], zz_dev).wait_recv()
    go(remote(WF2.at[gy], WF2.at[gy], ys.at[3], yr.at[3], yy_dev))
    lane128 = lax.broadcasted_iota(jnp.int32, (1, 128), 1)

    def of_head(x, j):
        keep = (lane128 < 64) if j == 0 else (lane128 >= 64)
        return jnp.where(keep, x, jnp.zeros_like(x))

    def attend(s, t):
        n = (t + 1) * R
        base = pl.multiple_of(s * S, S)
        rows = rows_at(s * S + t * R, R)
        query = Q[rows, :]
        bias = jnp.where(live_column(s, 0, n), 0.0, -1e30)
        key_at = lax.broadcasted_iota(jnp.int32, (R, R), 0)
        query_at = lax.broadcasted_iota(jnp.int32, (R, R), 1)
        for j in range(2):
            scores = cdot(K[pl.ds(base, n), :], of_head(query, j), 1, 1)
            diag = scores[t * R :] + jnp.where(key_at == query_at, 0.0, bias[t * R :])
            diag = jnp.where(key_at <= query_at, diag, -1e30)
            top = jnp.max(diag, axis=0, keepdims=True)
            if t > 0:
                left = scores[: t * R] + bias[: t * R]
                top = jnp.maximum(top, jnp.max(left, axis=0, keepdims=True))
                left = jnp.exp(left - top)
            diag = jnp.exp(diag - top)
            total = jnp.sum(diag, axis=0, keepdims=True)
            if t > 0:
                total = total + jnp.sum(left, axis=0, keepdims=True)
            scale = 1.0 / total
            prob = PT[t].at[s * 2 + j]
            prob[pl.ds(t * R, R), :] = (diag * scale).astype(BF)
            if t > 0:
                prob[pl.ds(0, t * R), :] = (left * scale).astype(BF)
            out = cdot(VT[pl.ds(j * 64, 64), pl.ds(base, n)], prob[...], 1, 0)
            ATT[rows, pl.ds(j * 64, 64)] = out.T.astype(BF)
            keep = live_row(s, t * R, R)
            AT[pl.ds(d.ffs + j * 64, 64), rows] = jnp.where(keep, out, 0.0).astype(BF)

    @pl.loop(0, 2)
    def _(s):
        for t in range(4):
            attend(s, t)

    relay_second(COTS, 0)
    remote(WF1.at[oy], WF1.at[oy], ys.at[1], yr.at[1], yy_dev).wait_recv()

    @pl.loop(0, 8)
    def _(i):
        rows = rows_at(i * R, R)
        pre = cdot(H[rows, :], WF1[...].reshape((W, d.ffs)), 1, 0) + BF1[3:4, :]
        act, slope = gelu_parts(pre)
        act = act.astype(BF)
        ACT[rows, :] = act
        SG[rows, :] = slope.astype(BF)
        keep = live_column(i // 4, lax.rem(i, 4) * R, R)
        AT[pl.ds(0, d.ffs), rows] = jnp.where(keep, act, jnp.zeros_like(act)).T

    relay_second(COTS, 1)
    wait_twin(COTS)

    def over_gy(part, buf, sem):
        return remote(part.at[oy], buf, sem.at[0, 0], sem.at[1, 0], yy_dev)

    for side in (oy, gy):
        for m in range(d.c2 // 256):
            cols = pl.ds(m * 256, 256)
            out = cdot(AT[...], COT[:, rows_at(side * d.c2 + m * 256, 256)], 1, 0).astype(BF)
            GB[side, :, cols] = out
            if side is oy:
                remote(GB.at[oy, :, cols], yb.at[:, cols], bsem.at[0, 0], bsem.at[1, 0], yy_dev).start()
    sends.append(over_gy(GB, yb, bsem))
    remote(WF2.at[oy], WF2.at[oy], ys.at[3], yr.at[3], yy_dev).wait_recv()
    for i in range(per):
        source = me.rank * per + i
        dst = WO.at[pl.ds(i * d.r1, d.r1)]

        @pl.when(source != me.f)
        def _():
            remote(wo, dst, os_.at[0], or_.at[i], x_dev).wait_recv()

    @pl.when(wo_mine)
    def _():
        wo_here.wait()

    def to_twin(src, t_buf, k, s, t):
        h = t // 2
        bz = jnp.where(t < 2, t, 3 - t)
        pb = 2 * t + jnp.where(t < 2, 1 - c, c)
        n = (s * 2 + bz) * 2 + h
        remote(src.at[rows_at(s * S + pb * half, half)], t_buf.at[s, bz, h], tsem.at[k, 0, n],
               tsem.at[k, 1, n], c_dev).start()

    def twin_blocks(src, t_buf, k):
        for bx in range(2):
            for bz in range(2):
                for h in range(2):
                    n = (bx * 2 + bz) * 2 + h
                    own = src.at[block(bx, bz * 2 + c, h)]
                    copy = remote(own, t_buf.at[bx, bz, h], tsem.at[k, 0, n], tsem.at[k, 1, n], c_dev)
                    yield bx, bz, h, own, copy

    def add_twin(src, t_buf, k):
        for bx, bz, h, own, copy in twin_blocks(src, t_buf, k):
            copy.wait_recv()
            t_buf[bx, bz, h] = (t_buf[bx, bz, h].astype(F32) + own[...].astype(F32)).astype(BF)

    def twin_sent(src, t_buf, k):
        for _, _, _, _, copy in twin_blocks(src, t_buf, k):
            copy.wait_send()

    def block_of(h, part):
        mine = zl if h == 0 else gx
        return 1 - mine if part == 0 else mine

    def hop_one(t_buf, b2, k, h, part):
        b, n = block_of(h, part), 8 + h * 2 + part
        src, dev = (t_buf.at[1 - gx, b, 0], x_dev) if h == 0 else (t_buf.at[b, 1 - zl, 1], z_dev)
        return remote(src, b2.at[h, b], tsem.at[k, 0, n], tsem.at[k, 1, n], dev)

    def add_one(t_buf, b2, k, h, part):
        hop_one(t_buf, b2, k, h, part).wait_recv()
        b = block_of(h, part)
        own = t_buf[gx, b, 0] if h == 0 else t_buf[b, zl, 1]
        b2[h, b] = (b2[h, b].astype(F32) + own.astype(F32)).astype(BF)

    def hop_two(b2, b3, k, h):
        src, dev = (b2.at[0, 1 - zl], z_dev) if h == 0 else (b2.at[1, 1 - gx], x_dev)
        return remote(src, b3.at[h], tsem.at[k, 0, 12 + h], tsem.at[k, 1, 12 + h], dev)

    def rows_of(b2, b3, h):
        return b2[h, zl if h == 0 else gx].astype(F32) + b3[h].astype(F32)


    wf2_all = (d.ffs, W)

    @pl.loop(0, 8)
    def _(i):
        rows = rows_at(i * R, R)
        mix = cdot(ATT[rows, :], WO[...], 1, 0) + cdot(ACT[rows, :], WF2[...].reshape(wf2_all), 1, 0)
        MIXP[rows, :] = mix.astype(BF)
        to_twin(MIXP, mt, 0, i // 4, lax.rem(i, 4))

    @pl.loop(0, 8)
    def _(i):
        rows = rows_at(i * R, R)
        keep = live_column(i // 4, lax.rem(i, 4) * R, R)
        grad = COT[rows, :]
        grad = jnp.where(keep, grad, jnp.zeros_like(grad))
        grad_act = cdot(grad, WF2[...].reshape(wf2_all), 1, 1)
        grad_pre = (grad_act * SG[rows, :].astype(F32)).astype(BF)
        SG[rows, :] = grad_pre
        GATT[rows, :] = cdot(grad, WO[...], 1, 1).astype(BF)
        SUMS[2:3, :] += jnp.sum(grad.astype(F32), axis=0, keepdims=True)
        SUMS[3:4, : d.ffs] += jnp.sum(grad_pre.astype(F32), axis=0, keepdims=True)

    add_twin(MIXP, mt, 0)
    for part in range(2):
        for h in range(2):
            go(hop_one(mt, m2, 0, h, part))

    @pl.loop(0, d.ffs // 256)
    def _(n):
        cols = rows_at(n * 256, 256)
        out = cdot(HT[...], SG[:, cols], 1, 0).astype(BF).reshape(8, 2, d.rdg, 256)
        GA[0, :, :, cols] = out[:, 0]
        GA[1, :, :, cols] = out[:, 1]
        remote(GA.at[oy, :, :, cols], ya.at[:, :, cols], asem.at[0, 0], asem.at[1, 0], yy_dev).start()

    sends.append(over_gy(GA, ya, asem))
    def y_sum(part, buf, sem, count):
        over_gy(part, buf, sem).wait_recv()
        for b in range(count):
            buf[b] = (buf[b].astype(F32) + part[gy, b].astype(F32)).astype(BF)

    over_gy(GB, yb, bsem).wait_recv()
    for b in range(5):
        rr = pl.ds(b * 128, 128)
        yb[rr, :] = (yb[rr, :].astype(F32) + GB[gy, rr, :].astype(F32)).astype(BF)
    b_rows = d.n_zp * d.r2
    f2_over_zp = remote(yb.at[rows_at(oz * b_rows, b_rows)], zb.at[pl.ds(0, b_rows)],
                        bsem.at[0, 1], bsem.at[1, 1], zz_dev)
    go(f2_over_zp)
    wo_zp = me.rank * d.n_zp // 8
    wo_over_zp = remote(yb.at[pl.ds(d.ffs, 128)], zb.at[pl.ds(b_rows, 128)],
                        bsem.at[0, 2], bsem.at[1, 2], zz_dev)

    @pl.when(wo_zp != zp)
    def _():
        wo_over_zp.start()

    def attend_back(s, t):
        n = (t + 1) * R
        base = pl.multiple_of(s * S, S)
        rows = rows_at(s * S + t * R, R)
        query, grad = Q[rows, :], GATT[rows, :]
        cos, sin = turn_tables_of(s, t)
        halves = []
        for j in range(2):
            grad_j = of_head(grad, j)
            prob_low = PT[t][s * 2 + j]
            grad_prob = cdot(V[pl.ds(base, n), :], grad_j, 1, 1)
            prob = prob_low.astype(F32)
            both = prob * grad_prob
            inner = jnp.sum(both, axis=0, keepdims=True)
            score = (both - prob * inner).astype(BF)
            DV[pl.ds(0, n), :] += cdot(prob_low, grad_j, 1, 0)
            DK[pl.ds(0, n), :] += cdot(score, of_head(query, j), 1, 0)
            halves.append(cdot(KT[pl.ds(j * 64, 64), pl.ds(base, n)], score, 1, 0))
        grad_q = jnp.concatenate(halves, axis=0).T * 0.125
        GQKV[rows, 0:128] = turned(grad_q, cos, -sin).astype(BF)

    @pl.loop(0, 2)
    def _(s):
        DK[...] = jnp.zeros_like(DK)
        DV[...] = jnp.zeros_like(DV)
        for t in range(4):
            attend_back(s, t)
        for t in range(4):
            rows = rows_at(s * S + t * R, R)
            cos, sin = turn_tables_of(s, t)
            GQKV[rows, 128:256] = turned(DK[pl.ds(t * R, R), :], cos, -sin).astype(BF)
            GQKV[rows, 256:384] = DV[pl.ds(t * R, R), :].astype(BF)

    out = cdot(HT[...], GQKV[...], 1, 0).astype(BF).reshape(8, 2, d.rdg, d.qs)
    GQ[0] = out[:, 0]
    GQ[1] = out[:, 1]
    go(over_gy(GQ, yq, qsem))
    for h in range(2):
        add_one(mt, m2, 0, h, 0)
        go(hop_two(m2, m3, 0, h))
    for h in range(2):
        add_one(mt, m2, 0, h, 1)
    y_sum(GA, ya, asem, 8)
    f1_over_zp = remote(ya.at[pl.ds(oz * 4, 4)], za, asem.at[0, 1], asem.at[1, 1], zz_dev)
    go(f1_over_zp)


    f2_over_zp.wait_recv()
    for b in range(d.n_zp):
        rr = pl.ds(b * 128, 128)
        own = yb[rows_at(zp * b_rows + b * 128, 128), :]
        zb[rr, :] = (zb[rr, :].astype(F32) + own.astype(F32)).astype(BF)
    f2_cols = rows_at(gy * d.c2, d.c2)
    f2_mine = F2.at[rows_at(q * 128, 128), f2_cols]

    def f2_copies():
        for j in range(2):
            for ox in range(2):
                away = jnp.logical_not(jnp.logical_and(ox == gx, gx * 2 + j == q))
                src = zb.at[pl.ds(j * 128, 128)]
                yield away, src, remote(src, f2_mine, dsem.at[0, 0, j * 2 + ox], dsem.at[0, 1, q],
                                        place(gy, ox, zp, gx * 2 + j))

    for away, src, copy in f2_copies():
        here = pltpu.make_async_copy(src, f2_mine, dsem.at[0, 2, 0])

        @pl.when(away)
        def _():
            copy.start()

        @pl.when(jnp.logical_not(away))
        def _():
            here.start()
            here.wait()

    wo_src = zb.at[pl.ds(b_rows, 128)]
    wo_final = remote(wo_src, FWO.at[:, f2_cols], dsem.at[1, 0, 0], dsem.at[1, 1, 0], x_dev)
    wo_stay = pltpu.make_async_copy(wo_src, FWO.at[:, f2_cols], dsem.at[1, 2, 0])

    @pl.when(wo_zp == zp)
    def _():
        wo_over_zp.wait_recv()
        rr = pl.ds(b_rows, 128)
        zb[rr, :] = (zb[rr, :].astype(F32) + yb[pl.ds(d.ffs, 128), :].astype(F32)).astype(BF)
        wo_final.start()
        wo_stay.start()
        wo_stay.wait()

    for copy in cot_sends:
        copy.wait_send()

    @pl.loop(0, 8)
    def _(i):
        rows = rows_at(i * R, R)
        grad = cdot(SG[rows, :], WF1[...].reshape((W, d.ffs)), 1, 1)
        grad = grad + cdot(GQKV[rows, :], WQ[...].reshape(wq_all), 1, 1)
        normed, _ = normalise(TOK[rows, :])
        SUMS[0:1, :] += jnp.sum(grad * normed, axis=0, keepdims=True)
        SUMS[1:2, :] += jnp.sum(grad, axis=0, keepdims=True)
        COT[rows, :] = grad.astype(BF)
        to_twin(COT, ht, 1, i // 4, lax.rem(i, 4))

    for sq in range(4):
        away = jnp.logical_not(jnp.logical_and(gx == zl, sq == q))

        @pl.when(away)
        def _():
            remote(zb.at[pl.ds(0, 128)], F2.at[rows_at(sq * 128, 128), f2_cols], dsem.at[0, 0, 0],
                   dsem.at[0, 1, sq], x_dev).wait_recv()

    @pl.when(wo_zp != zp)
    def _():
        wo_final.wait_recv()

    go(remote(F2.at[:, f2_cols], F2.at[:, f2_cols], bsem.at[0, 3], bsem.at[1, 3], yy_dev))
    go(remote(FWO.at[:, f2_cols], FWO.at[:, f2_cols], bsem.at[0, 4], bsem.at[1, 4], yy_dev))
    add_twin(COT, ht, 1)
    for h in range(2):
        go(hop_one(ht, h2, 1, h, 0))
    SMG[...] = jnp.zeros_like(SMG)
    first_rank = jnp.where(me.rank == 0, 1.0, 0.0)
    for dd in range(d.n_dev):
        for k in range(3):
            piece = SUMS[k : k + 1, dd * 128 : (dd + 1) * 128]
            SMG[dd % 4, dd // 4, k : k + 1, :] = piece * first_rank if k == 2 else piece
    for b in range(d.ng):
        dq = gx * 2 + b % d.n_zp
        SMG[dq, b // d.n_zp, pl.ds(3 + q, 1), :] = SUMS[3:4, b * 128 : (b + 1) * 128]
    for i in range(1, 8):
        other = lax.rem(me.rank + i, 8)
        go(remote(SMG.at[lax.rem(other, 4)], s1.at[me.rank], ssem.at[0, 0, other],
                  ssem.at[0, 1, me.rank], place(gy, other // 4, zp, lax.rem(other, 4))))
    f_rows = rows_at(gy * d.rdg, d.rdg)

    def f1_pieces():
        for b in range(d.ng):
            f = ((b // d.n_zp * 2 + gx) * d.n_zp + b % d.n_zp) * 4 + q
            yield b, F1.at[f_rows, rows_at(f * 128, 128)]

    def fq_pieces():
        for k in range(3):
            yield k, FQ.at[f_rows, rows_at(k * W + me.rank * 128, 128)]

    def finish(done, mine, pieces, k):
        for b in range(4):
            done[b] = (done[b].astype(F32) + mine[zp * 4 + b].astype(F32)).astype(BF)
        for i in range(1, 8):
            other = lax.rem(me.rank + i, 8)
            ox, oq = other // 4, lax.rem(other, 4)
            for n, dst in pieces():
                remote(done.at[oq, :, pl.ds(n * 128, 128)], dst, dsem.at[k, 0, other],
                       dsem.at[k, 1, me.rank], place(gy, ox, zp, oq)).start()
        for n, dst in pieces():
            pltpu.make_async_copy(done.at[q, :, pl.ds(n * 128, 128)], dst, dsem.at[k, 2, 0]).start()
        pltpu.make_async_copy(done.at[0], done.at[0], dsem.at[k, 2, 0]).wait()

    def finished(done, k):
        for i in range(1, 8):
            other = lax.rem(me.rank + i, 8)
            remote(done.at[0], done.at[0], dsem.at[k, 0, other], dsem.at[k, 1, other],
                   x_dev).wait_recv()

    def finish_sent(done, k):
        for i in range(1, 8):
            other = lax.rem(me.rank + i, 8)
            remote(done.at[0], done.at[0], dsem.at[k, 0, other], dsem.at[k, 1, other],
                   x_dev).wait_send()

    y_sum(GQ, yq, qsem, 8)
    fq_over_zp = remote(yq.at[pl.ds(oz * 4, 4)], zq, qsem.at[0, 1], qsem.at[1, 1], zz_dev)
    go(fq_over_zp)
    f1_over_zp.wait_recv()
    finish(za, ya, f1_pieces, 2)
    for h in range(2):
        go(hop_one(ht, h2, 1, h, 1))
    for h in range(2):
        hop_two(m2, m3, 0, h).wait_recv()
        first_place = (q if h == 0 else 7 - q) * half
        rr = pl.ds(h * half, half)
        total = rows_of(m2, m3, h) + VEC[2:3, :]
        total = total + TOK[block(gx, q, h), :].astype(F32)
        MIXED[rr, :] = jnp.where(live_column(gx, first_place, half), total, 0.0).astype(BF)
    for h in range(2):
        add_one(ht, h2, 1, h, 0)
        go(hop_two(h2, h3, 1, h))
    fq_over_zp.wait_recv()
    finish(zq, yq, fq_pieces, 3)
    finished(za, 2)
    go(remote(F1.at[f_rows], F1.at[f_rows], asem.at[0, 2], asem.at[1, 2], yy_dev))
    for h in range(2):
        add_one(ht, h2, 1, h, 1)
    for i in range(1, 8):
        other = lax.rem(me.rank + i, 8)
        remote(SMG.at[0], s1.at[other], ssem.at[0, 0, other], ssem.at[0, 1, other],
               x_dev).wait_recv()
    s1[me.rank] = SMG[q]
    total = s1[0]
    for i in range(1, 8):
        total = total + s1[i]
    s2[d.ng] = total
    own_group = gy * d.n_zp + zp
    for i in range(1, d.ng):
        group = lax.rem(own_group + i, d.ng)
        to_z = lax.rem(group, d.n_zp)
        go(remote(s2.at[d.ng, to_z], s2.at[own_group, 0], ssem.at[1, 0, group],
                  ssem.at[1, 1, own_group], place(group // d.n_zp, gx, to_z, q)))
    finished(zq, 3)
    go(remote(FQ.at[f_rows], FQ.at[f_rows], qsem.at[0, 2], qsem.at[1, 2], yy_dev))
    for h in range(2):
        hop_two(h2, h3, 1, h).wait_recv()
        first_place = (q if h == 0 else 7 - q) * half
        rr = pl.ds(h * half, half)
        normed, inverse = normalise(TOK[block(gx, q, h), :])
        scaled = rows_of(h2, h3, h) * VEC[0:1, :]
        grad = inverse * (
            scaled
            - jnp.mean(scaled, axis=-1, keepdims=True)
            - normed * jnp.mean(scaled * normed, axis=-1, keepdims=True)
        )
        own = jnp.where(live_column(gx, first_place, half), OWN[rr, :].astype(F32), 0.0)
        TGRAD[rr, :] = (own + grad).astype(BF)
    for i in range(1, d.ng):
        group = lax.rem(own_group + i, d.ng)
        remote(s2.at[d.ng, 0], s2.at[group, 0], ssem.at[1, 0, group], ssem.at[1, 1, group],
               x_dev).wait_recv()
    total = s2[d.ng, zp]
    for i in range(1, d.ng):
        total = total + s2[lax.rem(own_group + i, d.ng), 0]
    FSM[...] = total
    o_rows, o_cols = rows_at(oy * d.rdg, d.rdg), rows_at(oy * d.c2, d.c2)
    remote(F2.at[:, o_cols], F2.at[:, o_cols], bsem.at[0, 3], bsem.at[1, 3], yy_dev).wait_recv()
    remote(FWO.at[:, o_cols], FWO.at[:, o_cols], bsem.at[0, 4], bsem.at[1, 4], yy_dev).wait_recv()
    remote(F1.at[o_rows], F1.at[o_rows], asem.at[0, 2], asem.at[1, 2], yy_dev).wait_recv()
    remote(FQ.at[o_rows], FQ.at[o_rows], qsem.at[0, 2], qsem.at[1, 2], yy_dev).wait_recv()
    twin_sent(MIXP, mt, 0)
    twin_sent(COT, ht, 1)
    for copy in sends:
        copy.wait_send()
    for k, buf in enumerate((WQ, WF1)):
        for i in range(1, 8):
            other = lax.rem(me.rank + i, 8)
            dst = w1_region(buf, gx, q)
            remote(dst, dst, w1s.at[k, other], w1r.at[k, other], x_dev).wait_send()

    @pl.when(jnp.logical_not(wo_mine))
    def _():
        wo_own.wait_send()

    @pl.when(wo_zp != zp)
    def _():
        wo_over_zp.wait_send()

    @pl.when(wo_zp == zp)
    def _():
        wo_final.wait_send()

    for away, src, copy in f2_copies():

        @pl.when(away)
        def _():
            copy.wait_send()

    finish_sent(za, 2)
    finish_sent(zq, 3)


def layer(d, lens, offs, tok, cot, wqkv, wo, wfc1, wf2, sm, c0, s0):
    smem = pl.BlockSpec(memory_space=pltpu.SMEM)
    vm = pl.BlockSpec(memory_space=pltpu.VMEM)
    hbm = pl.BlockSpec(memory_space=pl.ANY)
    dma = pltpu.SemaphoreType.DMA
    shape = jax.ShapeDtypeStruct
    R, W, half = d.rows, d.width, d.rows // 2
    N = 8 * R

    def bf(*dims):
        return pltpu.VMEM(dims, BF)

    def f32(*dims):
        return pltpu.VMEM(dims, F32)

    return pl.pallas_call(
        functools.partial(layer_kernel, d),
        out_shape=(
            shape((R, W), BF),
            shape((R, W), BF),
            shape((d.rd, d.ff), BF),
            shape((d.rd, 3 * W), BF),
            shape((d.ff // d.n_dev, W), BF),
            shape((d.rd, W), BF),
            shape((8, 128), F32),
        ),
        in_specs=[smem, smem] + [hbm] * 7 + [vm] * 2,
        out_specs=(vm,) * 7,
        scratch_shapes=[
            bf(N, W), bf(N, W), bf(N, W), bf(W, N),
            bf(N, 128), bf(N, 128), bf(N, 128), bf(128, N), bf(128, N),
            bf(4, R, R), bf(4, 2 * R, R), bf(4, 3 * R, R), bf(4, 4 * R, R),
            bf(N, d.ffs), bf(d.ffs + 128, N), bf(N, d.ffs), bf(N, 128), bf(N, 128), bf(N, d.qs),
            f32(4 * R, 128), f32(4 * R, 128), bf(N, W),
            bf(d.n_gy, 2, d.n_zp, 4 * d.r1, d.ffs), bf(d.n_gy, 2, d.n_zp, 4 * d.r1, d.qs),
            bf(d.n_gy, d.n_zp, d.r2, W), bf(128, W), bf(d.n_gy, 2, d.n_zp, 4, 16, 128),
            f32(16, W), f32(16, d.ffs), f32(4, d.n_zp, 8, 128), f32(8, W), bf(R, W),
            bf(2, 2, 2, half, W), bf(2, 2, half, W), bf(2, half, W),
            bf(2, 2, 2, half, W), bf(2, 2, half, W), bf(2, half, W),
            bf(d.n_gy, d.ffs + 128, d.c2), bf(d.n_gy, 8, d.rdg, d.ffs), bf(d.n_gy, 8, d.rdg, d.qs),
            bf(d.ffs + 128, d.c2), bf(8, d.rdg, d.ffs), bf(8, d.rdg, d.qs),
            bf(d.ffs // d.n_zp + 128, d.c2), bf(4, d.rdg, d.ffs), bf(4, d.rdg, d.qs),
            f32(8, d.n_zp, 8, 128), f32(d.ng + 1, d.n_zp, 8, 128),
            dma((8,)), dma((7, 2)), dma((8, 2)), dma((7, 2)), dma((8, 2)),
            dma((3, 8)), dma((3, 8)), dma((4,)), dma((4,)), dma((4,)), dma((4,)),
            dma((d.ng,)), dma((128 // d.r1,)),
            dma((2, 2, 14)), dma((2, 5)), dma((2, 3)), dma((2, 3)), dma((2, 2, 8)), dma((4, 3, 8)),
        ],
        compiler_params=pltpu.CompilerParams(
            has_side_effects=True, vmem_limit_bytes=67043328
        ),
        name="layer",
    )(lens, offs, tok, cot, wqkv, wo, wfc1, wf2, sm, c0, s0)


def place_tables(slot):
    freq = np.exp(np.arange(ROT // 2) * (-2.0 * math.log(10000.0) / ROT))
    angle = np.arange(slot)[:, None] * freq[np.arange(128) % (ROT // 2)][None]
    return np.cos(angle).astype(np.float32), np.sin(angle).astype(np.float32)


def small_pack(d, ln_gain, ln_bias, b_fc1, b_fc2):
    gap = jnp.zeros((3 * 128 - 3 * d.r1,), BF)
    rest = jnp.zeros((12 * 128,), BF)
    return jnp.concatenate([ln_gain, ln_bias, b_fc2, gap, b_fc1, rest]).reshape(16, 128)


def local_one(d, tokens, cotangent, lengths, offsets, ln_gain, ln_bias, w_qkv, w_out, w_fc1, b_fc1,
              w_fc2, b_fc2):
    sm = small_pack(d, ln_gain, ln_bias, b_fc1, b_fc2)
    c0, s0 = place_tables(4 * d.rows)
    mixed, token_grad, f1, fq, f2, fwo, small = layer(
        d, lengths, offsets, tokens, cotangent, w_qkv, w_out, w_fc1, w_fc2, sm,
        jnp.asarray(c0), jnp.asarray(s0),
    )
    per = d.rd
    return (mixed, token_grad, small[0, :per], small[1, :per], fq.astype(F32), fwo.astype(F32),
            f1.astype(F32), small[3:7].reshape(-1), f2.astype(F32), small[2, :per])


def solution(mesh):
    rows = ("grp", "dev")

    def program(*args):
        tokens, w_fc1 = args[0], args[8]
        n = mesh.shape["grp"] * mesh.shape["dev"]
        d = Dims(mesh, tokens.shape[0] // n, tokens.shape[1], w_fc1.shape[1])
        whole_tiles = d.n_gy == 2 and d.r2 == 128 and d.r1 % 16 == 0 and d.rd == 128
        return jax.shard_map(
            functools.partial(local_one if whole_tiles else local, d),
            mesh=mesh,
            in_specs=(
                P(rows, None), P(rows, None), P(), P(), P(rows), P(rows), P(rows, None),
                P(rows, None), P(rows, None), P(rows), P(rows, None), P(rows),
            ),
            out_specs=(
                P(rows, None), P(rows, None), P("dev"), P("dev"), P("dev", None), P("dev", None),
                P("dev", None), P("dev"), P("dev", None), P("dev"),
            ),
            check_vma=False,
        )(*args)

    return program
```

```python
import functools
import math

import jax
import jax.numpy as jnp
import numpy as np
from jax import lax
from jax.experimental import pallas as pl
from jax.experimental.pallas import tpu as pltpu
from jax.sharding import PartitionSpec as P

HEADS = 16
HD = 64
ROT = 32
MESH = pl.DeviceIdType.MESH
BF = jnp.bfloat16
F32 = jnp.float32


class Dims:
    def __init__(self, mesh, rows, width, ff):
        self.n_grp, self.n_dev = mesh.shape["grp"], mesh.shape["dev"]
        self.n_gy, self.n_zp = self.n_grp // 2, self.n_dev // 4
        assert self.n_gy == self.n_zp
        self.n_all = self.n_grp * self.n_dev
        self.rows, self.width, self.ff = rows, width, ff
        self.r1 = width // self.n_all
        self.r2 = ff // self.n_all
        self.ffs = ff // 8
        self.qs = 3 * width // 8
        self.ca = self.ffs + self.qs
        self.rd = width // self.n_dev
        self.rdg = self.rd // self.n_gy
        self.c2 = width // self.n_gy
        self.ng = self.n_gy * self.n_zp


class Me:
    def __init__(self, d):
        grp, dev = lax.axis_index("grp"), lax.axis_index("dev")
        self.grp, self.dev = grp, dev
        self.gy, self.gx = grp // 2, lax.rem(grp, 2)
        self.zp, self.q = dev // 4, lax.rem(dev, 4)
        self.zl, self.c = self.q // 2, lax.rem(self.q, 2)
        self.f = grp * d.n_dev + dev
        self.rank = self.gx * 4 + self.q


def place(gy, gx, zp, q):
    return {"grp": gy * 2 + gx, "dev": zp * 4 + q}


def remote(src, dst, send, recv, device):
    return pltpu.make_async_remote_copy(
        src_ref=src,
        dst_ref=dst,
        send_sem=send,
        recv_sem=recv,
        device_id=device,
        device_id_type=MESH,
    )


def gather_kernel(d, tok, cot, p1, wo, wf2, sm, TOK, COT, WA, WO, WF2, SM, loc, ts, tr, cs, cr,
                  w1s, w1r, m1s, m1r, zs, zr, ys, yr, os_, or_):
    me = Me(d)
    gy, gx, zp, q = me.gy, me.gx, me.zp, me.q
    half = d.rows // 2
    local = [
        pltpu.make_async_copy(tok, TOK.at[gx, q], loc.at[0]),
        pltpu.make_async_copy(cot, COT.at[gx, q], loc.at[1]),
        pltpu.make_async_copy(p1.at[me.rank], WA.at[gy, gx, zp, q], loc.at[2]),
        pltpu.make_async_copy(wf2, WF2.at[gy, zp], loc.at[3]),
        pltpu.make_async_copy(sm, SM.at[gy, gx, zp, q], loc.at[4]),
    ]

    def token_send(src, buf, send, recv, slot, bx, bq, h, device):
        return remote(
            src.at[pl.ds(h * half, half)],
            buf.at[bx, bq, pl.ds(h * half, half)],
            send.at[slot, h],
            recv.at[bx * 4 + bq, h],
            device,
        )

    x_dev, z_dev, c_dev = place(gy, 1 - gx, zp, q), place(gy, gx, zp, lax.rem(q + 2, 4)), place(
        gy, gx, zp, me.zl * 2 + 1 - me.c
    )
    qz = lax.rem(q + 2, 4)

    sends = []

    def go(copy):
        copy.start()
        sends.append(copy)

    def arrived(buf, send, recv, bx, bq, h):
        token_send(buf.at[bx, bq], buf, send, recv, 0, bx, bq, h, x_dev).wait_recv()

    for h in range(2):
        go(token_send(tok, TOK, ts, tr, 0, gx, q, h, x_dev))
        go(token_send(cot, COT, cs, cr, 0, gx, q, h, z_dev))
    for i in range(1, 8):
        other = lax.rem(me.rank + i, 8)
        dev = place(gy, other // 4, zp, lax.rem(other, 4))
        go(remote(p1.at[other], WA.at[gy, gx, zp, q], w1s.at[other], w1r.at[me.rank], dev))
        go(remote(sm, SM.at[gy, gx, zp, q], m1s.at[other], m1r.at[me.rank], dev))
    for copy in local:
        copy.start()
    for i in range(1, d.n_zp):
        oz = lax.rem(zp + i, d.n_zp)
        go(remote(wf2, WF2.at[gy, zp], zs.at[2, oz], zr.at[2, zp], place(gy, gx, oz, q)))
    per = 128 // d.r1
    owner = me.f // per
    part = lax.rem(me.f, per)
    ox, oq = owner // 4, lax.rem(owner, 4)
    for i in range(d.ng):
        group = lax.rem(gy * d.n_zp + zp + i, d.ng)
        oy, oz = group // d.n_zp, lax.rem(group, d.n_zp)
        copy = remote(wo, WO.at[part], os_.at[i], or_.at[part], place(oy, ox, oz, oq))
        if i == 0:
            mine = jnp.logical_and(ox == gx, oq == q)

            @pl.when(mine)
            def _():
                here = pltpu.make_async_copy(wo, WO.at[part], loc.at[5])
                here.start()
                here.wait()

            @pl.when(jnp.logical_not(mine))
            def _():
                copy.start()
                copy.wait_send()
        else:
            go(copy)
    for h in range(2):
        go(token_send(tok, TOK, ts, tr, 1, gx, q, h, z_dev))
        go(token_send(cot, COT, cs, cr, 1, gx, q, h, x_dev))
        go(token_send(tok, TOK, ts, tr, 3, gx, q, h, c_dev))
        go(token_send(cot, COT, cs, cr, 3, gx, q, h, c_dev))
    for h in range(2):
        arrived(TOK, ts, tr, 1 - gx, q, h)
        go(token_send(TOK.at[1 - gx, q], TOK, ts, tr, 2, 1 - gx, q, h, z_dev))
        go(token_send(TOK.at[1 - gx, q], TOK, ts, tr, 4, 1 - gx, q, h, c_dev))
        arrived(COT, cs, cr, gx, qz, h)
        go(token_send(COT.at[gx, qz], COT, cs, cr, 2, gx, qz, h, x_dev))
        go(token_send(COT.at[gx, qz], COT, cs, cr, 4, gx, qz, h, c_dev))
    for copy in local:
        copy.wait()
    for i in range(1, 8):
        other = lax.rem(me.rank + i, 8)
        ox_, oq_ = other // 4, lax.rem(other, 4)
        dev = place(gy, ox_, zp, oq_)
        remote(p1.at[0], WA.at[gy, ox_, zp, oq_], w1s.at[other], w1r.at[other], dev).wait_recv()
        remote(sm, SM.at[gy, ox_, zp, oq_], m1s.at[other], m1r.at[other], dev).wait_recv()
    for i in range(1, d.n_zp):
        oz = lax.rem(zp + i, d.n_zp)
        dev = place(gy, gx, oz, q)
        go(remote(WA.at[gy, :, zp], WA.at[gy, :, zp], zs.at[0, oz], zr.at[0, zp], dev))
        go(remote(SM.at[gy, :, zp], SM.at[gy, :, zp], zs.at[1, oz], zr.at[1, zp], dev))
    for i in range(1, d.n_zp):
        oz = lax.rem(zp + i, d.n_zp)
        remote(wf2, WF2.at[gy, oz], zs.at[2, oz], zr.at[2, oz], place(gy, gx, oz, q)).wait_recv()
    for i in range(1, d.n_gy):
        oy = lax.rem(gy + i, d.n_gy)
        go(remote(WF2.at[gy], WF2.at[gy], ys.at[2, oy], yr.at[2, gy], place(oy, gx, zp, q)))
    for h in range(2):
        arrived(TOK, ts, tr, gx, qz, h)
        go(token_send(TOK.at[gx, qz], TOK, ts, tr, 5, gx, qz, h, c_dev))
        arrived(COT, cs, cr, 1 - gx, q, h)
        go(token_send(COT.at[1 - gx, q], COT, cs, cr, 5, 1 - gx, q, h, c_dev))
    for h in range(2):
        arrived(TOK, ts, tr, 1 - gx, qz, h)
        go(token_send(TOK.at[1 - gx, qz], TOK, ts, tr, 6, 1 - gx, qz, h, c_dev))
        arrived(COT, cs, cr, 1 - gx, qz, h)
        go(token_send(COT.at[1 - gx, qz], COT, cs, cr, 6, 1 - gx, qz, h, c_dev))
    for i in range(1, d.n_zp):
        oz = lax.rem(zp + i, d.n_zp)
        dev = place(gy, gx, oz, q)
        remote(WA.at[gy, :, oz], WA.at[gy, :, oz], zs.at[0, oz], zr.at[0, oz], dev).wait_recv()
        remote(SM.at[gy, :, oz], SM.at[gy, :, oz], zs.at[1, oz], zr.at[1, oz], dev).wait_recv()
    for i in range(1, d.n_gy):
        oy = lax.rem(gy + i, d.n_gy)
        dev = place(oy, gx, zp, q)
        go(remote(WA.at[gy], WA.at[gy], ys.at[0, oy], yr.at[0, gy], dev))
        go(remote(SM.at[gy], SM.at[gy], ys.at[1, oy], yr.at[1, gy], dev))
    qc = me.zl * 2 + 1 - me.c
    qcz = lax.rem(qc + 2, 4)
    for bx in (gx, 1 - gx):
        for bq in (qc, qcz):
            for h in range(2):
                arrived(TOK, ts, tr, bx, bq, h)
                arrived(COT, cs, cr, bx, bq, h)
    for i in range(1, d.n_gy):
        oy = lax.rem(gy + i, d.n_gy)
        dev = place(oy, gx, zp, q)
        for k, buf in enumerate((WA, SM, WF2)):
            remote(buf.at[oy], buf.at[oy], ys.at[k, oy], yr.at[k, oy], dev).wait_recv()
    for i in range(per):
        source = me.rank * per + i

        @pl.when(source != me.f)
        def _():
            remote(wo, WO.at[i], os_.at[0], or_.at[i], x_dev).wait_recv()

    for copy in sends:
        copy.wait_send()


def gather(d, tok, cot, p1, wo, wf2, sm):
    any_spec = pl.BlockSpec(memory_space=pl.ANY)
    dma = pltpu.SemaphoreType.DMA
    shape = jax.ShapeDtypeStruct
    return pl.pallas_call(
        functools.partial(gather_kernel, d),
        out_shape=(
            shape((2, 4, d.rows, d.width), BF),
            shape((2, 4, d.rows, d.width), BF),
            shape((d.n_gy, 2, d.n_zp, 4, d.r1, d.ca), BF),
            shape((128 // d.r1, d.r1, d.width), BF),
            shape((d.n_gy, d.n_zp, d.r2, d.width), BF),
            shape((d.n_gy, 2, d.n_zp, 4, 16, 128), BF),
        ),
        in_specs=[any_spec] * 6,
        out_specs=(any_spec,) * 6,
        scratch_shapes=[
            dma((6,)), dma((7, 2)), dma((8, 2)), dma((7, 2)), dma((8, 2)),
            dma((8,)), dma((8,)), dma((8,)), dma((8,)),
            dma((3, d.n_zp)), dma((3, d.n_zp)), dma((3, d.n_gy)), dma((3, d.n_gy)),
            dma((d.ng,)), dma((128 // d.r1,)),
        ],
        compiler_params=pltpu.CompilerParams(has_side_effects=True),
        name="gather",
    )(tok, cot, p1, wo, wf2, sm)


def add_blocks(out, *terms):
    n = out.shape[0]

    @pl.loop(0, n)
    def _(i):
        total = terms[0][i].astype(F32)
        for term in terms[1:]:
            total = total + term[i].astype(F32)
        out[i] = total.astype(out.dtype)


def reduce_kernel(d, mix, gh, ga, gf2, gwo, smg, MIX, GH, FA, FF2, FWO, FSM,
                  mt, m2, m3, ht, h2, h3, ya, y2, yo, za, z2, zo, s1, s2,
                  tsem, asem, fsem, osem, ssem, dsem):
    me = Me(d)
    gy, gx, zp, q, zl, c = me.gy, me.gx, me.zp, me.q, me.zl, me.c
    x_dev, z_dev, c_dev = place(gy, 1 - gx, zp, q), place(gy, gx, zp, lax.rem(q + 2, 4)), place(
        gy, gx, zp, zl * 2 + 1 - c
    )
    sends = []

    def go(copy):
        copy.start()
        sends.append(copy)

    for i in range(1, d.n_gy):
        oy = lax.rem(gy + i, d.n_gy)
        dev = place(oy, gx, zp, q)
        go(remote(gf2.at[:, :, oy], y2.at[gy], fsem.at[0, 0, oy], fsem.at[0, 1, gy], dev))
        go(remote(gwo.at[oy], yo.at[gy], osem.at[0, 0, oy], osem.at[0, 1, gy], dev))
        go(remote(ga.at[:, :, oy], ya.at[gy], asem.at[0, 0, oy], asem.at[0, 1, gy], dev))
    row_sums = ((mix, mt, m2, m3, MIX, 0), (gh, ht, h2, h3, GH, 1))
    for src, t_buf, _, _, _, k in row_sums:
        go(remote(src.at[:, :, 1 - c], t_buf, tsem.at[k, 0, 0], tsem.at[k, 1, 0], c_dev))
    for i in range(1, 8):
        other = lax.rem(me.rank + i, 8)
        oq = lax.rem(other, 4)
        go(remote(smg.at[oq], s1.at[me.rank], ssem.at[0, 0, other], ssem.at[0, 1, me.rank],
                  place(gy, other // 4, zp, oq)))
    for src, t_buf, b2, b3, _, k in row_sums:
        remote(src.at[:, :, 1 - c], t_buf, tsem.at[k, 0, 0], tsem.at[k, 1, 0], c_dev).wait_recv()
        for bx in range(2):
            for bz in range(2):
                add_blocks(t_buf.at[bx, bz], t_buf.at[bx, bz], src.at[bx, bz, c])
        if k == 0:
            go(remote(t_buf.at[1 - gx], b2, tsem.at[k, 0, 1], tsem.at[k, 1, 1], x_dev))
        else:
            go(remote(t_buf.at[:, 1 - zl], b2, tsem.at[k, 0, 1], tsem.at[k, 1, 1], z_dev))
    for i in range(1, d.n_gy):
        oy = lax.rem(gy + i, d.n_gy)
        dev = place(oy, gx, zp, q)
        remote(gf2.at[:, :, oy], y2.at[oy], fsem.at[0, 0, oy], fsem.at[0, 1, oy], dev).wait_recv()
        remote(gwo.at[oy], yo.at[oy], osem.at[0, 0, oy], osem.at[0, 1, oy], dev).wait_recv()
    others = [lax.rem(gy + i, d.n_gy) for i in range(1, d.n_gy)]
    for a in range(d.n_gy):
        for b in range(d.n_zp):
            add_blocks(y2.at[gy, a, b], gf2.at[a, b, gy], *[y2.at[o, a, b] for o in others])
    add_blocks(yo.at[gy], gwo.at[gy], *[yo.at[o] for o in others])
    for i in range(1, d.n_zp):
        oz = lax.rem(zp + i, d.n_zp)
        dev = place(gy, gx, oz, q)
        go(remote(y2.at[gy, oz], z2.at[zp], fsem.at[1, 0, oz], fsem.at[1, 1, zp], dev))
        go(remote(yo.at[gy], zo.at[zp], osem.at[1, 0, oz], osem.at[1, 1, zp], dev))
    for i in range(1, d.n_gy):
        oy = lax.rem(gy + i, d.n_gy)
        dev = place(oy, gx, zp, q)
        remote(ga.at[:, :, oy], ya.at[oy], asem.at[0, 0, oy], asem.at[0, 1, oy], dev).wait_recv()
    for a in range(d.n_zp):
        for b in range(4):
            add_blocks(ya.at[gy, a, b], ga.at[a, b, gy], *[ya.at[o, a, b] for o in others])
    for i in range(1, d.n_zp):
        oz = lax.rem(zp + i, d.n_zp)
        go(remote(ya.at[gy, oz], za.at[zp], asem.at[1, 0, oz], asem.at[1, 1, zp],
                  place(gy, gx, oz, q)))
    for i in range(1, 8):
        other = lax.rem(me.rank + i, 8)
        remote(smg.at[0], s1.at[other], ssem.at[0, 0, other], ssem.at[0, 1, other],
               x_dev).wait_recv()
    s1[me.rank] = smg[q]
    total = s1[0]
    for i in range(1, 8):
        total = total + s1[i]
    s2[d.ng] = total
    own_group = gy * d.n_zp + zp
    for i in range(1, d.ng):
        group = lax.rem(own_group + i, d.ng)
        oy, oz = group // d.n_zp, lax.rem(group, d.n_zp)
        go(remote(s2.at[d.ng, oz], s2.at[own_group, 0], ssem.at[1, 0, group],
                  ssem.at[1, 1, own_group], place(oy, gx, oz, q)))
    for src, t_buf, b2, b3, _, k in row_sums:
        if k == 0:
            remote(t_buf.at[1 - gx], b2, tsem.at[k, 0, 1], tsem.at[k, 1, 1], x_dev).wait_recv()
            for b in range(2):
                add_blocks(b2.at[b], b2.at[b], t_buf.at[gx, b])
            go(remote(b2.at[1 - zl], b3, tsem.at[k, 0, 2], tsem.at[k, 1, 2], z_dev))
        else:
            remote(t_buf.at[:, 1 - zl], b2, tsem.at[k, 0, 1], tsem.at[k, 1, 1], z_dev).wait_recv()
            for b in range(2):
                add_blocks(b2.at[b], b2.at[b], t_buf.at[b, zl])
            go(remote(b2.at[1 - gx], b3, tsem.at[k, 0, 2], tsem.at[k, 1, 2], x_dev))
    zothers = [lax.rem(zp + i, d.n_zp) for i in range(1, d.n_zp)]
    for o in zothers:
        dev = place(gy, gx, o, q)
        remote(y2.at[gy, o], z2.at[o], fsem.at[1, 0, o], fsem.at[1, 1, o], dev).wait_recv()
        remote(yo.at[gy], zo.at[o], osem.at[1, 0, o], osem.at[1, 1, o], dev).wait_recv()
    hz = d.n_zp // 2
    for b in range(d.n_zp):
        add_blocks(z2.at[zp, b], y2.at[gy, zp, b], *[z2.at[o, b] for o in zothers])
    add_blocks(zo.at[zp], yo.at[gy], *[zo.at[o] for o in zothers])
    for j in range(2):
        dq = gx * 2 + j
        for ox in range(2):
            mine = jnp.logical_and(ox == gx, dq == q)
            src = z2.at[zp, pl.ds(j * hz, hz)]
            dst = FF2.at[gy, q]
            copy = remote(src, dst, dsem.at[0, 0, j * 2 + ox], dsem.at[0, 1, q],
                          place(gy, ox, zp, dq))

            @pl.when(mine)
            def _():
                here = pltpu.make_async_copy(src, dst, dsem.at[0, 2, 0])
                here.start()
                here.wait()

            @pl.when(jnp.logical_not(mine))
            def _():
                copy.start()
    nwo = 128 // d.rd
    wo_zp = me.rank * d.n_zp // 8
    for j in range(nwo):
        dq = lax.rem(me.rank * nwo + j, 4)
        for ox in range(2):
            here_too = jnp.logical_and(ox == gx, dq == q)
            src = zo.at[zp, pl.ds(j * (d.rd // 16), d.rd // 16)]
            dst = FWO.at[gy]
            copy = remote(src, dst, dsem.at[1, 0, j * 2 + ox], dsem.at[1, 1, 0],
                          place(gy, ox, zp, dq))

            @pl.when(jnp.logical_and(wo_zp == zp, here_too))
            def _():
                here = pltpu.make_async_copy(src, dst, dsem.at[1, 2, 0])
                here.start()
                here.wait()

            @pl.when(jnp.logical_and(wo_zp == zp, jnp.logical_not(here_too)))
            def _():
                copy.start()
    for o in zothers:
        dev = place(gy, gx, o, q)
        remote(ya.at[gy, o], za.at[o], asem.at[1, 0, o], asem.at[1, 1, o], dev).wait_recv()
    for b in range(4):
        add_blocks(za.at[zp, b], ya.at[gy, zp, b], *[za.at[o, b] for o in zothers])
    for i in range(1, 8):
        other = lax.rem(me.rank + i, 8)
        ox, oq = other // 4, lax.rem(other, 4)
        go(remote(za.at[zp, oq], FA.at[gy, gx, q], dsem.at[2, 0, other],
                  dsem.at[2, 1, me.rank], place(gy, ox, zp, oq)))
    here = pltpu.make_async_copy(za.at[zp, q], FA.at[gy, gx, q], dsem.at[2, 2, 0])
    here.start()
    here.wait()
    for src, t_buf, b2, b3, out, k in row_sums:
        if k == 0:
            remote(b2.at[1 - zl], b3, tsem.at[k, 0, 2], tsem.at[k, 1, 2], z_dev).wait_recv()
            mine = b2.at[zl]
        else:
            remote(b2.at[1 - gx], b3, tsem.at[k, 0, 2], tsem.at[k, 1, 2], x_dev).wait_recv()
            mine = b2.at[gx]
        n = out.shape[0]
        for i in range(n):
            out[i] = mine[i].astype(F32) + b3[i].astype(F32)
    for sq in range(4):
        away = jnp.logical_not(jnp.logical_and(gx == zl, sq == q))

        @pl.when(away)
        def _():
            remote(z2.at[0, pl.ds(0, hz)], FF2.at[gy, sq], dsem.at[0, 0, 0], dsem.at[0, 1, sq],
                   x_dev).wait_recv()
    source = (zp * 4 + q) // nwo
    sx, sq = source // 4, lax.rem(source, 4)

    @pl.when(jnp.logical_not(jnp.logical_and(sx == gx, sq == q)))
    def _():
        remote(zo.at[0, pl.ds(0, d.rd // 16)], FWO.at[gy], dsem.at[1, 0, 0], dsem.at[1, 1, 0],
               x_dev).wait_recv()
    for o in others:
        dev = place(o, gx, zp, q)
        go(remote(FF2.at[gy], FF2.at[gy], fsem.at[2, 0, o], fsem.at[2, 1, gy], dev))
        go(remote(FWO.at[gy], FWO.at[gy], osem.at[2, 0, o], osem.at[2, 1, gy], dev))
    for i in range(1, 8):
        other = lax.rem(me.rank + i, 8)
        ox, oq = other // 4, lax.rem(other, 4)
        remote(za.at[0, 0], FA.at[gy, ox, oq], dsem.at[2, 0, other], dsem.at[2, 1, other],
               x_dev).wait_recv()
    for o in others:
        dev = place(o, gx, zp, q)
        go(remote(FA.at[gy], FA.at[gy], asem.at[2, 0, o], asem.at[2, 1, gy], dev))
    for i in range(1, d.ng):
        group = lax.rem(own_group + i, d.ng)
        remote(s2.at[d.ng, 0], s2.at[group, 0], ssem.at[1, 0, group], ssem.at[1, 1, group],
               x_dev).wait_recv()
    total = s2[d.ng, zp]
    for i in range(1, d.ng):
        total = total + s2[lax.rem(own_group + i, d.ng), 0]
    FSM[...] = total
    for o in others:
        dev = place(o, gx, zp, q)
        for buf, sem in ((FF2, fsem), (FWO, osem), (FA, asem)):
            remote(buf.at[o], buf.at[o], sem.at[2, 0, o], sem.at[2, 1, o], dev).wait_recv()
    for copy in sends:
        copy.wait_send()
    for j in range(2):
        for ox in range(2):
            away = jnp.logical_not(jnp.logical_and(ox == gx, gx * 2 + j == q))

            @pl.when(away)
            def _():
                remote(z2.at[zp, pl.ds(j * hz, hz)], FF2.at[gy, q], dsem.at[0, 0, j * 2 + ox],
                       dsem.at[0, 1, q], x_dev).wait_send()
    for j in range(nwo):
        dq = lax.rem(me.rank * nwo + j, 4)
        for ox in range(2):
            away = jnp.logical_not(jnp.logical_and(ox == gx, dq == q))

            @pl.when(jnp.logical_and(wo_zp == zp, away))
            def _():
                remote(zo.at[zp, pl.ds(j * (d.rd // 16), d.rd // 16)], FWO.at[gy], dsem.at[1, 0, j * 2 + ox],
                       dsem.at[1, 1, 0], x_dev).wait_send()


def reduce_all(d, mix, gh, ga, gf2, gwo, smg):
    vm = pl.BlockSpec(memory_space=pltpu.VMEM)
    dma = pltpu.SemaphoreType.DMA
    shape = jax.ShapeDtypeStruct
    R = d.rows
    slabs = R // 16
    return pl.pallas_call(
        functools.partial(reduce_kernel, d),
        out_shape=(
            shape((slabs, 16, d.width), F32),
            shape((slabs, 16, d.width), F32),
            shape((d.n_gy, 2, 4, d.rdg // 16, 16, d.ca), BF),
            shape((d.n_gy, 4, d.n_zp // 2, d.r2 // 16, 16, d.c2), BF),
            shape((d.n_gy, d.rd // 16, 16, d.c2), BF),
            shape((8, 128), F32),
        ),
        in_specs=[vm] * 6,
        out_specs=(vm,) * 6,
        scratch_shapes=[
            pltpu.VMEM((2, 2, slabs, 16, d.width), BF),
            pltpu.VMEM((2, slabs, 16, d.width), BF),
            pltpu.VMEM((slabs, 16, d.width), BF),
            pltpu.VMEM((2, 2, slabs, 16, d.width), BF),
            pltpu.VMEM((2, slabs, 16, d.width), BF),
            pltpu.VMEM((slabs, 16, d.width), BF),
            pltpu.VMEM((d.n_gy, d.n_zp, 4, d.rdg // 16, 16, d.ca), BF),
            pltpu.VMEM((d.n_gy, d.n_gy, d.n_zp, d.r2 // 16, 16, d.c2), BF),
            pltpu.VMEM((d.n_gy, 8, 16, d.c2), BF),
            pltpu.VMEM((d.n_zp, 4, d.rdg // 16, 16, d.ca), BF),
            pltpu.VMEM((d.n_zp, d.n_zp, d.r2 // 16, 16, d.c2), BF),
            pltpu.VMEM((d.n_zp, 8, 16, d.c2), BF),
            pltpu.VMEM((8, d.n_zp, 8, 128), F32),
            pltpu.VMEM((d.ng + 1, d.n_zp, 8, 128), F32),
            dma((2, 2, 3)),
            dma((3, 2, max(d.n_gy, d.n_zp))),
            dma((3, 2, max(d.n_gy, d.n_zp))),
            dma((3, 2, max(d.n_gy, d.n_zp))),
            dma((2, 2, max(8, d.ng))),
            dma((3, 3, 8)),
        ],
        compiler_params=pltpu.CompilerParams(
            has_side_effects=True, vmem_limit_bytes=62 * 1024 * 1024
        ),
        name="reduce",
    )(mix, gh, ga, gf2, gwo, smg)


def gelu_parts(v):
    tangent = jnp.tanh(0.7978845608028654 * (v + 0.044715 * v * v * v))
    inner = 0.7978845608028654 * (1.0 + 0.134145 * v * v)
    act = 0.5 * v * (1.0 + tangent)
    slope = 0.5 * (1.0 + tangent) + 0.5 * v * (1.0 - tangent * tangent) * inner
    return act, slope


def places_of_slot(rows):
    slot = 4 * rows
    row = jnp.arange(slot, dtype=jnp.int32)
    piece, inner, half = row // rows, row % rows, rows // 2
    return jnp.where(inner < half, piece * half + inner, slot - (piece + 1) * half + inner - half)


def spread(vec, lane):
    n = vec.shape[0]
    if n == 128:
        return vec
    tiled = jnp.tile(vec, 128 // n)
    at = jnp.arange(128, dtype=jnp.int32) // n
    return jnp.where(at == lane, tiled, jnp.zeros_like(tiled))


def dot(a, b, dims):
    return lax.dot_general(a, b, (dims, ((), ())), preferred_element_type=F32)


def local(d, tokens, cotangent, lengths, offsets, ln_gain, ln_bias, w_qkv, w_out, w_fc1, b_fc1,
          w_fc2, b_fc2):
    me = Me(d)
    R, W = d.rows, d.width
    fc1 = w_fc1.reshape(d.r1, d.n_gy, 2, d.n_zp, 4, d.r2).transpose(2, 4, 0, 1, 3, 5)
    fc1 = fc1.reshape(8, d.r1, d.ffs)
    qkv = w_qkv.reshape(d.r1, 3, 8, 128).transpose(2, 0, 1, 3).reshape(8, d.r1, d.qs)
    p1 = jnp.concatenate([fc1, qkv], axis=2)
    lane = lax.rem(me.f, 128 // d.r1)
    pad = jnp.zeros((128 - d.r2,), BF)
    sm = jnp.stack([spread(ln_gain, lane), spread(ln_bias, lane), spread(b_fc2, lane),
                    jnp.concatenate([b_fc1, pad]) if d.r2 < 128 else b_fc1])
    sm = jnp.concatenate([sm, jnp.zeros((12, 128), BF)])
    TOK, COT, WA, WO, WF2, SM = gather(d, tokens, cotangent, p1, w_out, w_fc2, sm)
    sums = SM.reshape(8, d.n_all // 8, 16, 128).astype(F32).sum(axis=1)
    gain, bias, bfc2 = sums[:, 0].reshape(W), sums[:, 1].reshape(W), sums[:, 2].reshape(W)
    mine = lax.dynamic_index_in_dim(
        lax.dynamic_index_in_dim(SM, me.gx, 1, False), me.q, 2, False
    )
    bfc1 = mine[:, :, 3, : d.r2].reshape(d.ffs).astype(F32)
    WA = WA.reshape(W, d.ca)
    wfc1, wqkv = WA[:, : d.ffs], WA[:, d.ffs :]
    wout = WO.reshape(128, W)
    wfc2 = WF2.reshape(d.ffs, W)
    slot0 = (me.gy * 2) * d.n_zp + me.zp
    lens = jnp.stack([lengths[slot0], lengths[slot0 + d.n_zp]])
    offs = jnp.stack([offsets[slot0], offsets[slot0 + d.n_zp]])
    places = places_of_slot(R)
    live = (places[None] >= offs[:, None]) & (places[None] < (offs + lens)[:, None])
    live_f = live.reshape(8 * R, 1).astype(F32)
    tok = TOK.reshape(8 * R, W).astype(F32)
    centred = tok - jnp.mean(tok, axis=-1, keepdims=True)
    inverse = lax.rsqrt(jnp.mean(centred * centred, axis=-1, keepdims=True) + 1e-5)
    normed = centred * inverse
    h = (normed * gain + bias).astype(BF)
    grad_y = (COT.reshape(8 * R, W).astype(F32) * live_f).astype(BF)
    qkv = dot(h, wqkv, ((1,), (0,)))
    freq = jnp.exp(jnp.arange(ROT // 2, dtype=F32) * (-2.0 * math.log(10000.0) / ROT))
    angles = (places[None] - offs[:, None]).astype(F32).reshape(8 * R)[:, None] * freq[None]
    cos, sin = jnp.cos(angles)[:, None], jnp.sin(angles)[:, None]

    def turn(x, sign):
        a, b = x[..., : ROT // 2], x[..., ROT // 2 : ROT]
        return jnp.concatenate(
            [a * cos - sign * b * sin, b * cos + sign * a * sin, x[..., ROT:]], axis=-1
        )

    queries = turn(qkv[:, :128].reshape(8 * R, 2, HD), 1.0).astype(BF).reshape(2, 4 * R, 2, HD)
    keys = turn(qkv[:, 128:256].reshape(8 * R, 2, HD), 1.0).astype(BF).reshape(2, 4 * R, 2, HD)
    values = qkv[:, 256:].astype(BF).reshape(2, 4 * R, 2, HD)
    scores = jnp.einsum("sqhd,skhd->shqk", queries, keys, preferred_element_type=F32) * 0.125
    allowed = (places[None, None, :] <= places[None, :, None]) & (
        live[:, None, :] | (places[None, None, :] == places[None, :, None])
    )
    scores = jnp.where(allowed[:, None], scores, -1e30)
    expo = jnp.exp(scores - jnp.max(scores, axis=-1, keepdims=True))
    prob = expo / jnp.sum(expo, axis=-1, keepdims=True)
    low = prob.astype(BF)
    att = jnp.einsum("shqk,skhd->sqhd", low, values, preferred_element_type=F32)
    att = att.astype(BF).reshape(8 * R, 128)
    pre = dot(h, wfc1, ((1,), (0,))) + bfc1
    act, slope = gelu_parts(pre)
    act = act.astype(BF)
    mix = dot(att, wout, ((1,), (0,))) + dot(act, wfc2, ((1,), (0,)))
    g_wo = dot(att, grad_y, ((0,), (0,)))
    g_f2 = dot(act, grad_y, ((0,), (0,)))
    grad_pre = (dot(grad_y, wfc2, ((1,), (1,))) * slope).astype(BF)
    g_f1 = dot(h, grad_pre, ((0,), (0,)))
    g_bf1 = grad_pre.astype(F32).sum(axis=0)
    grad_att = dot(grad_y, wout, ((1,), (1,))).astype(BF).reshape(2, 4 * R, 2, HD)
    g_prob = jnp.einsum("sqhd,skhd->shqk", grad_att, values, preferred_element_type=F32)
    row_dot = jnp.sum(prob * g_prob, axis=-1, keepdims=True)
    g_score = (prob * (g_prob - row_dot)).astype(BF)
    g_v = jnp.einsum("shqk,sqhd->skhd", low, grad_att, preferred_element_type=F32)
    g_q = jnp.einsum("shqk,skhd->sqhd", g_score, keys, preferred_element_type=F32) * 0.125
    g_k = jnp.einsum("shqk,sqhd->skhd", g_score, queries, preferred_element_type=F32) * 0.125
    g_q = turn(g_q.reshape(8 * R, 2, HD), -1.0).reshape(8 * R, 128)
    g_k = turn(g_k.reshape(8 * R, 2, HD), -1.0).reshape(8 * R, 128)
    g_qkv = jnp.concatenate([g_q, g_k, g_v.reshape(8 * R, 128)], axis=1).astype(BF)
    g_wqkv = dot(h, g_qkv, ((0,), (0,)))
    gh = dot(grad_pre, wfc1, ((1,), (1,))) + dot(g_qkv, wqkv, ((1,), (1,)))
    g_gain, g_bias = (gh * normed).sum(axis=0), gh.sum(axis=0)
    g_bf2 = jnp.where(me.rank == 0, grad_y.astype(F32).sum(axis=0), 0.0)
    nd, per = d.n_dev, W // d.n_dev

    def wide(x):
        x = x.reshape(nd, -1)
        n = x.shape[1]
        if n < 128:
            x = jnp.concatenate([x, jnp.zeros((nd, 128 - n), F32)], axis=1)
        return x.reshape(nd, -1, 128)

    bf1_rows = max(d.ff // nd // 128, 1)
    full = jnp.zeros((d.n_gy, 2, d.n_zp, 4, d.r2), F32)
    full = lax.dynamic_update_slice(
        full, g_bf1.reshape(d.n_gy, 1, d.n_zp, 1, d.r2), (0, me.gx, 0, me.q, 0)
    )
    smg = jnp.concatenate(
        [wide(g_gain), wide(g_bias), wide(g_bf2), wide(full.reshape(d.ff)),
         jnp.zeros((nd, 5 - bf1_rows, 128), F32)], axis=1,
    )
    smg = smg.reshape(d.n_zp, 4, 8, 128).transpose(1, 0, 2, 3)
    slabs = R // 16
    mix_p = mix.astype(BF).reshape(2, 2, 2, slabs, 16, W)
    gh_p = gh.astype(BF).reshape(2, 2, 2, slabs, 16, W)
    ga = jnp.concatenate([g_f1, g_wqkv], axis=1).astype(BF)
    ga = ga.reshape(d.n_zp, 4, d.n_gy, d.rdg // 16, 16, d.ca)
    gf2 = g_f2.astype(BF).reshape(d.n_gy, d.n_zp, d.r2 // 16, 16, d.n_gy, d.c2)
    gf2 = gf2.transpose(0, 1, 4, 2, 3, 5)
    gwo = g_wo.astype(BF).reshape(8, 16, d.n_gy, d.c2).transpose(2, 0, 1, 3)
    MIX, GH, FA, FF2, FWO, FSM = reduce_all(d, mix_p, gh_p, ga, gf2, gwo, smg)
    own = me.gx * 4 + me.q

    def own_rows(x):
        return lax.dynamic_index_in_dim(x.reshape(8, R, x.shape[-1]), own, 0, False)

    my_live, my_normed, my_inv = own_rows(live_f), own_rows(normed), own_rows(inverse)
    mixed = (my_live * (tokens.astype(F32) + MIX.reshape(R, W) + bfc2)).astype(BF)
    scaled = GH.reshape(R, W) * gain
    grad_norm = my_inv * (
        scaled - jnp.mean(scaled, axis=-1, keepdims=True)
        - my_normed * jnp.mean(scaled * my_normed, axis=-1, keepdims=True)
    )
    token_grad = (cotangent.astype(F32) * my_live + grad_norm).astype(BF)
    FA = FA.reshape(d.n_gy, 2, 4, d.rdg, d.ca)
    o_f1 = FA[..., : d.ffs].reshape(d.n_gy, 2, 4, d.rdg, d.n_gy, d.n_zp, d.r2)
    o_f1 = o_f1.transpose(0, 3, 4, 1, 5, 2, 6).reshape(d.rd, d.ff).astype(F32)
    o_qkv = FA[..., d.ffs :].reshape(d.n_gy, 8, d.rdg, 3, 128)
    o_qkv = o_qkv.transpose(0, 2, 3, 1, 4).reshape(d.rd, 3 * W).astype(F32)
    o_f2 = FF2.reshape(d.n_gy, 4, d.n_zp // 2, d.r2, d.c2).transpose(2, 1, 3, 0, 4)
    o_f2 = o_f2.reshape(d.ff // nd, W).astype(F32)
    o_wo = FWO.reshape(d.n_gy, d.rd, d.c2).transpose(1, 0, 2).reshape(d.rd, W).astype(F32)
    o_gain, o_bias, o_bf2 = FSM[0, :per], FSM[1, :per], FSM[2, :per]
    o_bf1 = FSM[3 : 3 + bf1_rows].reshape(-1)[: d.ff // nd]
    return mixed, token_grad, o_gain, o_bias, o_qkv, o_wo, o_f1, o_bf1, o_f2, o_bf2


def cdot(a, b, ca, cb):
    return lax.dot_general(a, b, (((ca,), (cb,)), ((), ())), preferred_element_type=F32)


def rows_at(start, n):
    return pl.ds(pl.multiple_of(start, n), n)


def layer_kernel(d, lens, offs, tok, cot, wqkv, wo, wfc1, wf2, sm, c0, s0,
                 MIXED, TGRAD, F1, FQ, F2, FWO, FSM,
                 TOK, COT, H, HT, Q, K, V, KT, VT, P0, P1, P2, P3, ACT, AT, SG, ATT, GATT, GQKV,
                 DK, DV, MIXP, WF1, WQ, WF2, WO, SM, VEC, BF1, SMG, SUMS, OWN,
                 mt, m2, m3, ht, h2, h3, GB, GA, GQ, yb, ya, yq, zb, za, zq, s1, s2,
                 loc, ts, tr, cs, cr, w1s, w1r, zs, zr, ys, yr, os_, or_,
                 tsem, bsem, asem, qsem, ssem, dsem):
    me = Me(d)
    gy, gx, zp, q, zl, c = me.gy, me.gx, me.zp, me.q, me.zl, me.c
    half, R, W = d.rows // 2, d.rows, d.width
    S = 4 * R
    PT = (P0, P1, P2, P3)
    qz, qc = lax.rem(q + 2, 4), zl * 2 + 1 - c
    qcz = lax.rem(qc + 2, 4)
    x_dev, z_dev, c_dev = place(gy, 1 - gx, zp, q), place(gy, gx, zp, qz), place(gy, gx, zp, qc)
    oz, oy = 1 - zp, 1 - gy
    zz_dev, yy_dev = place(gy, gx, oz, q), place(oy, gx, zp, q)
    sends, cot_sends = [], []

    def go(copy, kept=sends):
        copy.start()
        kept.append(copy)

    def block(bx, bq, h):
        pb = bq if h == 0 else 7 - bq
        return rows_at(bx * S + pb * half, half)

    def tsend(src, buf, send, recv, slot, bx, bq, h, device):
        return remote(src, buf.at[block(bx, bq, h)], send.at[slot, h], recv.at[bx * 4 + bq, h], device)

    TOKS, COTS = (tok, TOK, ts, tr, sends), (cot, COT, cs, cr, cot_sends)

    def x_first(arr, h):
        return h == 0

    def own_half(src, h):
        return src.at[pl.ds(h * half, half)]

    def first(arr, h):
        src, buf, send, recv, kept = arr
        go(tsend(own_half(src, h), buf, send, recv, 0, gx, q, h, x_dev if x_first(arr, h) else z_dev), kept)

    def second(arr, h):
        src, buf, send, recv, kept = arr
        go(tsend(own_half(src, h), buf, send, recv, 1, gx, q, h, z_dev if x_first(arr, h) else x_dev), kept)
        go(tsend(own_half(src, h), buf, send, recv, 3, gx, q, h, c_dev), kept)

    def wait_block(arr, bx, bq, h):
        _, buf, send, recv, kept = arr
        tsend(buf.at[block(bx, bq, h)], buf, send, recv, 0, bx, bq, h, x_dev).wait_recv()

    def pass_on(arr, slot, bx, bq, h, device):
        _, buf, send, recv, kept = arr
        go(tsend(buf.at[block(bx, bq, h)], buf, send, recv, slot, bx, bq, h, device), kept)

    def relay_first(arr, h):
        bx, bq = (1 - gx, q) if x_first(arr, h) else (gx, qz)
        wait_block(arr, bx, bq, h)
        pass_on(arr, 2, bx, bq, h, z_dev if x_first(arr, h) else x_dev)
        pass_on(arr, 4, bx, bq, h, c_dev)

    def relay_second(arr, h):
        bx, bq = (gx, qz) if x_first(arr, h) else (1 - gx, q)
        wait_block(arr, bx, bq, h)
        pass_on(arr, 5, bx, bq, h, c_dev)
        wait_block(arr, 1 - gx, qz, h)
        pass_on(arr, 6, 1 - gx, qz, h, c_dev)

    def wait_twin(arr):
        for bx in (gx, 1 - gx):
            for bq in (qc, qcz):
                for h in range(2):
                    wait_block(arr, bx, bq, h)

    own_rows = rows_at(q * d.r1, d.r1)
    local = [
        pltpu.make_async_copy(sm, SM.at[gy, gx, zp, q], loc.at[0]),
        pltpu.make_async_copy(wf2, WF2.at[gy, zp], loc.at[1]),
    ]
    for h in range(2):
        local.append(pltpu.make_async_copy(own_half(tok, h), TOK.at[block(gx, q, h)], loc.at[2 + h]))
        local.append(pltpu.make_async_copy(own_half(cot, h), COT.at[block(gx, q, h)], loc.at[4 + h]))
    local.append(pltpu.make_async_copy(cot, OWN, loc.at[7]))

    def fc1_pieces(ox, oq):
        for b in range(d.ng):
            f = ((b // d.n_zp * 2 + ox) * d.n_zp + b % d.n_zp) * 4 + oq
            yield (wfc1.at[:, rows_at(f * d.r2, d.r2)],
                   WF1.at[gy, gx, zp, own_rows, pl.ds(b * d.r2, d.r2)])

    def qkv_pieces(rank):
        for k in range(3):
            yield (wqkv.at[:, rows_at(k * W + rank * 128, 128)],
                   WQ.at[gy, gx, zp, own_rows, pl.ds(k * 128, 128)])

    for i in range(1, 8):
        other = lax.rem(me.rank + i, 8)
        ox, oq = other // 4, lax.rem(other, 4)
        dev = place(gy, ox, zp, oq)
        for src, dst in qkv_pieces(other):
            remote(src, dst, w1s.at[0, other], w1r.at[0, me.rank], dev).start()
        go(remote(sm, SM.at[gy, gx, zp, q], w1s.at[2, other], w1r.at[2, me.rank], dev))
    for src, dst in qkv_pieces(me.rank):
        pltpu.make_async_copy(src, dst, w1r.at[0, me.rank]).start()
    for h in range(2):
        first(TOKS, h)
    for copy in local:
        copy.start()
    for i in range(1, 8):
        other = lax.rem(me.rank + i, 8)
        ox, oq = other // 4, lax.rem(other, 4)
        for src, dst in fc1_pieces(ox, oq):
            remote(src, dst, w1s.at[1, other], w1r.at[1, me.rank], place(gy, ox, zp, oq)).start()
    for src, dst in fc1_pieces(gx, q):
        pltpu.make_async_copy(src, dst, w1r.at[1, me.rank]).start()
    def w1_region(buf, ox, oq):
        return buf.at[gy, ox, zp, rows_at(oq * d.r1, d.r1)]

    def wait_w1(k, buf):
        for i in range(1, 8):
            other = lax.rem(me.rank + i, 8)
            dst = w1_region(buf, other // 4, lax.rem(other, 4))
            remote(dst, dst, w1s.at[k, other], w1r.at[k, other], x_dev).wait_recv()
        dst = w1_region(buf, gx, q)
        pltpu.make_async_copy(dst, dst, w1r.at[k, me.rank]).wait()

    for copy in local:
        copy.wait()
    wait_w1(0, WQ)
    for i in range(1, 8):
        other = lax.rem(me.rank + i, 8)
        dst = SM.at[gy, other // 4, zp, lax.rem(other, 4)]
        remote(sm, dst, w1s.at[2, other], w1r.at[2, other], x_dev).wait_recv()
    def own_part(k, buf):
        part = buf.at[gy, :, zp]
        go(remote(part, part, zs.at[k], zr.at[k], zz_dev))
        go(remote(part, part, ys.at[k], yr.at[k], yy_dev))

    def far_part(k, buf):
        part = buf.at[gy, :, oz]
        remote(part, part, zs.at[k], zr.at[k], zz_dev).wait_recv()
        go(remote(part, part, ys.at[4 + k], yr.at[4 + k], yy_dev))

    def complete(k, buf):
        for part, n in ((zp, k), (oz, 4 + k)):
            dst = buf.at[oy, :, part]
            remote(dst, dst, ys.at[n], yr.at[n], yy_dev).wait_recv()

    own_part(2, SM)
    own_part(0, WQ)
    for h in range(2):
        second(TOKS, h)
    wait_w1(1, WF1)
    own_part(1, WF1)
    for h in range(2):
        relay_first(TOKS, h)
    go(remote(wf2, WF2.at[gy, zp], zs.at[3], zr.at[3], zz_dev))
    go(remote(wf2, WF2.at[gy, zp], ys.at[3], yr.at[3], yy_dev))
    for h in range(2):
        first(COTS, h)
    for h in range(2):
        second(COTS, h)
    per = 128 // d.r1
    owner = me.f // per
    part = lax.rem(me.f, per)
    wx, wq = owner // 4, lax.rem(owner, 4)
    wo_mine = jnp.logical_and(wx == gx, wq == q)
    wo_dst = WO.at[rows_at(part * d.r1, d.r1)]
    wo_own = remote(wo, wo_dst, os_.at[0], or_.at[part], place(gy, wx, zp, wq))
    wo_here = pltpu.make_async_copy(wo, wo_dst, loc.at[6])
    far_part(2, SM)
    far_part(0, WQ)
    for h in range(2):
        relay_second(TOKS, h)
    wait_twin(TOKS)
    complete(2, SM)
    in_lane = lax.broadcasted_iota(jnp.int32, (8, 128), 1) // d.r1
    parts = 128 // d.r1
    for j in range(8):
        rows3 = [jnp.zeros((8, 128), F32)] * 3
        for k in range(parts):
            g_, dv = divmod(j * parts + k, d.n_dev)
            packed = SM[g_ // 2, g_ % 2, dv // 4, dv % 4].astype(F32)[0:8]
            for v in range(3):
                turn = (k - v) % parts * d.r1
                moved = pltpu.roll(packed, turn, 1) if turn else packed
                rows3[v] = jnp.where(in_lane == k, moved, rows3[v])
        for v in range(3):
            VEC[v : v + 1, j * 128 : (j + 1) * 128] = rows3[v][0:1]
    for b in range(d.ng):
        BF1[:, b * 128 : (b + 1) * 128] = SM[b // d.n_zp, gx, b % d.n_zp, q].astype(F32)
    SUMS[...] = jnp.zeros_like(SUMS)

    def slot_of(s):
        index = (gy * 2 + s) * d.n_zp + zp
        return lens[index], offs[index]

    def normalise(rows):
        x = rows.astype(F32)
        centred = x - jnp.mean(x, axis=-1, keepdims=True)
        inverse = lax.rsqrt(jnp.mean(centred * centred, axis=-1, keepdims=True) + 1e-5)
        return centred * inverse, inverse

    def live_column(s, first_place, n):
        length, offset = slot_of(s)
        at = lax.broadcasted_iota(jnp.int32, (n, 1), 0) + first_place
        return jnp.logical_and(at >= offset, at < offset + length)

    def live_row(s, first_place, n):
        length, offset = slot_of(s)
        at = lax.broadcasted_iota(jnp.int32, (1, n), 1) + first_place
        return jnp.logical_and(at >= offset, at < offset + length)

    @pl.loop(0, 8)
    def _(i):
        normed, _ = normalise(TOK[rows_at(i * R, R), :])
        h = (normed * VEC[0:1, :] + VEC[1:2, :]).astype(BF)
        H[rows_at(i * R, R), :] = h
        HT[:, rows_at(i * R, R)] = h.T

    relay_first(COTS, 0)
    far_part(1, WF1)
    for i in range(1, d.ng):
        group = lax.rem(gy * d.n_zp + zp + i, d.ng)
        go(remote(wo, wo_dst, os_.at[i], or_.at[part],
                  place(group // d.n_zp, wx, lax.rem(group, d.n_zp), wq)))

    @pl.when(wo_mine)
    def _():
        wo_here.start()

    @pl.when(jnp.logical_not(wo_mine))
    def _():
        wo_own.start()

    complete(0, WQ)

    lane = lax.rem(lax.broadcasted_iota(jnp.int32, (1, 128), 1), 64)

    def turn_tables_of(s, t):
        _, offset = slot_of(s)
        co, so = c0[pl.ds(offset, 1), :], s0[pl.ds(offset, 1), :]
        cc, ss = c0[rows_at(t * R, R), :], s0[rows_at(t * R, R), :]
        cos = cc * co + ss * so
        sin = ss * co - cc * so
        cos = jnp.where(lane < ROT, cos, 1.0)
        sin = jnp.where(lane < ROT // 2, -sin, jnp.where(lane < ROT, sin, 0.0))
        return cos, sin

    def turned(x, cos, sin):
        other = jnp.where(lane < ROT // 2, pltpu.roll(x, 128 - ROT // 2, 1), pltpu.roll(x, ROT // 2, 1))
        return x * cos + other * sin

    wq_all = (W, d.qs)

    @pl.loop(0, 8)
    def _(i):
        s, t = i // 4, lax.rem(i, 4)
        rows = rows_at(i * R, R)
        qkv = cdot(H[rows, :], WQ[...].reshape(wq_all), 1, 0)
        cos, sin = turn_tables_of(s, t)
        query = turned(qkv[:, :128], cos, sin).astype(BF)
        Q[rows, :] = (query.astype(F32) * 0.125).astype(BF)
        key = turned(qkv[:, 128:256], cos, sin).astype(BF)
        K[rows, :] = key
        KT[:, rows] = key.T
        value = qkv[:, 256:].astype(BF)
        V[rows, :] = value
        VT[:, rows] = value.T

    relay_first(COTS, 1)
    remote(WF2.at[gy, oz], WF2.at[gy, oz], zs.at[3], zr.at[3], zz_dev).wait_recv()
    go(remote(WF2.at[gy, oz], WF2.at[gy, oz], ys.at[7], yr.at[7], yy_dev))
    lane128 = lax.broadcasted_iota(jnp.int32, (1, 128), 1)

    def of_head(x, j):
        keep = (lane128 < 64) if j == 0 else (lane128 >= 64)
        return jnp.where(keep, x, jnp.zeros_like(x))

    def attend(s, t):
        n = (t + 1) * R
        base = pl.multiple_of(s * S, S)
        rows = rows_at(s * S + t * R, R)
        query = Q[rows, :]
        bias = jnp.where(live_column(s, 0, n), 0.0, -1e30)
        key_at = lax.broadcasted_iota(jnp.int32, (R, R), 0)
        query_at = lax.broadcasted_iota(jnp.int32, (R, R), 1)
        for j in range(2):
            scores = cdot(K[pl.ds(base, n), :], of_head(query, j), 1, 1)
            diag = scores[t * R :] + jnp.where(key_at == query_at, 0.0, bias[t * R :])
            diag = jnp.where(key_at <= query_at, diag, -1e30)
            top = jnp.max(diag, axis=0, keepdims=True)
            if t > 0:
                left = scores[: t * R] + bias[: t * R]
                top = jnp.maximum(top, jnp.max(left, axis=0, keepdims=True))
                left = jnp.exp(left - top)
            diag = jnp.exp(diag - top)
            total = jnp.sum(diag, axis=0, keepdims=True)
            if t > 0:
                total = total + jnp.sum(left, axis=0, keepdims=True)
            scale = 1.0 / total
            prob = PT[t].at[s * 2 + j]
            prob[pl.ds(t * R, R), :] = (diag * scale).astype(BF)
            if t > 0:
                prob[pl.ds(0, t * R), :] = (left * scale).astype(BF)
            out = cdot(VT[pl.ds(j * 64, 64), pl.ds(base, n)], prob[...], 1, 0)
            ATT[rows, pl.ds(j * 64, 64)] = out.T.astype(BF)
            keep = live_row(s, t * R, R)
            AT[pl.ds(d.ffs + j * 64, 64), rows] = jnp.where(keep, out, 0.0).astype(BF)

    @pl.loop(0, 2)
    def _(s):
        for t in range(4):
            attend(s, t)

    relay_second(COTS, 0)
    complete(1, WF1)

    @pl.loop(0, 8)
    def _(i):
        rows = rows_at(i * R, R)
        pre = cdot(H[rows, :], WF1[...].reshape((W, d.ffs)), 1, 0) + BF1[3:4, :]
        act, slope = gelu_parts(pre)
        act = act.astype(BF)
        ACT[rows, :] = act
        SG[rows, :] = slope.astype(BF)
        keep = live_column(i // 4, lax.rem(i, 4) * R, R)
        AT[pl.ds(0, d.ffs), rows] = jnp.where(keep, act, jnp.zeros_like(act)).T

    relay_second(COTS, 1)
    wait_twin(COTS)

    def over_gy(part, buf, sem):
        return remote(part.at[oy], buf, sem.at[0, 0], sem.at[1, 0], yy_dev)

    for side in (oy, gy):
        for m in range(d.c2 // 256):
            cols = pl.ds(m * 256, 256)
            out = cdot(AT[...], COT[:, rows_at(side * d.c2 + m * 256, 256)], 1, 0).astype(BF)
            GB[side, :, cols] = out
            if side is oy:
                remote(GB.at[oy, :, cols], yb.at[:, cols], bsem.at[0, 0], bsem.at[1, 0], yy_dev).start()
    sends.append(over_gy(GB, yb, bsem))
    for part, n in ((zp, 3), (oz, 7)):
        dst = WF2.at[oy, part]
        remote(dst, dst, ys.at[n], yr.at[n], yy_dev).wait_recv()
    for i in range(per):
        source = me.rank * per + i
        dst = WO.at[pl.ds(i * d.r1, d.r1)]

        @pl.when(source != me.f)
        def _():
            remote(wo, dst, os_.at[0], or_.at[i], x_dev).wait_recv()

    @pl.when(wo_mine)
    def _():
        wo_here.wait()

    def to_twin(src, t_buf, k, s, t):
        h = t // 2
        bz = jnp.where(t < 2, t, 3 - t)
        pb = 2 * t + jnp.where(t < 2, 1 - c, c)
        n = (s * 2 + bz) * 2 + h
        remote(src.at[rows_at(s * S + pb * half, half)], t_buf.at[s, bz, h], tsem.at[k, 0, n],
               tsem.at[k, 1, n], c_dev).start()

    def twin_blocks(src, t_buf, k):
        for bx in range(2):
            for bz in range(2):
                for h in range(2):
                    n = (bx * 2 + bz) * 2 + h
                    own = src.at[block(bx, bz * 2 + c, h)]
                    copy = remote(own, t_buf.at[bx, bz, h], tsem.at[k, 0, n], tsem.at[k, 1, n], c_dev)
                    yield bx, bz, h, own, copy

    def add_twin(src, t_buf, k):
        for bx, bz, h, own, copy in twin_blocks(src, t_buf, k):
            copy.wait_recv()
            t_buf[bx, bz, h] = (t_buf[bx, bz, h].astype(F32) + own[...].astype(F32)).astype(BF)

    def twin_sent(src, t_buf, k):
        for _, _, _, _, copy in twin_blocks(src, t_buf, k):
            copy.wait_send()

    def block_of(h, part):
        mine = zl if h == 0 else gx
        return 1 - mine if part == 0 else mine

    def hop_one(t_buf, b2, k, h, part):
        b, n = block_of(h, part), 8 + h * 2 + part
        src, dev = (t_buf.at[1 - gx, b, 0], x_dev) if h == 0 else (t_buf.at[b, 1 - zl, 1], z_dev)
        return remote(src, b2.at[h, b], tsem.at[k, 0, n], tsem.at[k, 1, n], dev)

    def add_one(t_buf, b2, k, h, part):
        hop_one(t_buf, b2, k, h, part).wait_recv()
        b = block_of(h, part)
        own = t_buf[gx, b, 0] if h == 0 else t_buf[b, zl, 1]
        b2[h, b] = (b2[h, b].astype(F32) + own.astype(F32)).astype(BF)

    def hop_two(b2, b3, k, h):
        src, dev = (b2.at[0, 1 - zl], z_dev) if h == 0 else (b2.at[1, 1 - gx], x_dev)
        return remote(src, b3.at[h], tsem.at[k, 0, 12 + h], tsem.at[k, 1, 12 + h], dev)

    def rows_of(b2, b3, h):
        return b2[h, zl if h == 0 else gx].astype(F32) + b3[h].astype(F32)


    wf2_all = (d.ffs, W)

    @pl.loop(0, 8)
    def _(i):
        rows = rows_at(i * R, R)
        mix = cdot(ATT[rows, :], WO[...], 1, 0) + cdot(ACT[rows, :], WF2[...].reshape(wf2_all), 1, 0)
        MIXP[rows, :] = mix.astype(BF)
        to_twin(MIXP, mt, 0, i // 4, lax.rem(i, 4))

    @pl.loop(0, 8)
    def _(i):
        rows = rows_at(i * R, R)
        keep = live_column(i // 4, lax.rem(i, 4) * R, R)
        grad = COT[rows, :]
        grad = jnp.where(keep, grad, jnp.zeros_like(grad))
        grad_act = cdot(grad, WF2[...].reshape(wf2_all), 1, 1)
        grad_pre = (grad_act * SG[rows, :].astype(F32)).astype(BF)
        SG[rows, :] = grad_pre
        GATT[rows, :] = cdot(grad, WO[...], 1, 1).astype(BF)
        SUMS[2:3, :] += jnp.sum(grad.astype(F32), axis=0, keepdims=True)
        SUMS[3:4, : d.ffs] += jnp.sum(grad_pre.astype(F32), axis=0, keepdims=True)

    add_twin(MIXP, mt, 0)
    for part in range(2):
        for h in range(2):
            go(hop_one(mt, m2, 0, h, part))

    @pl.loop(0, d.ffs // 256)
    def _(n):
        cols = rows_at(n * 256, 256)
        out = cdot(HT[...], SG[:, cols], 1, 0).astype(BF).reshape(8, 2, d.rdg, 256)
        GA[0, :, :, cols] = out[:, 0]
        GA[1, :, :, cols] = out[:, 1]
        remote(GA.at[oy, :, :, cols], ya.at[:, :, cols], asem.at[0, 0], asem.at[1, 0], yy_dev).start()

    sends.append(over_gy(GA, ya, asem))
    def y_sum(part, buf, sem, count):
        over_gy(part, buf, sem).wait_recv()
        for b in range(count):
            buf[b] = (buf[b].astype(F32) + part[gy, b].astype(F32)).astype(BF)

    over_gy(GB, yb, bsem).wait_recv()
    for b in range(5):
        rr = pl.ds(b * 128, 128)
        yb[rr, :] = (yb[rr, :].astype(F32) + GB[gy, rr, :].astype(F32)).astype(BF)
    b_rows = d.n_zp * d.r2
    f2_over_zp = remote(yb.at[rows_at(oz * b_rows, b_rows)], zb.at[pl.ds(0, b_rows)],
                        bsem.at[0, 1], bsem.at[1, 1], zz_dev)
    go(f2_over_zp)
    wo_zp = me.rank * d.n_zp // 8
    wo_over_zp = remote(yb.at[pl.ds(d.ffs, 128)], zb.at[pl.ds(b_rows, 128)],
                        bsem.at[0, 2], bsem.at[1, 2], zz_dev)

    @pl.when(wo_zp != zp)
    def _():
        wo_over_zp.start()

    def attend_back(s, t):
        n = (t + 1) * R
        base = pl.multiple_of(s * S, S)
        rows = rows_at(s * S + t * R, R)
        query, grad = Q[rows, :], GATT[rows, :]
        cos, sin = turn_tables_of(s, t)
        halves = []
        for j in range(2):
            grad_j = of_head(grad, j)
            prob_low = PT[t][s * 2 + j]
            grad_prob = cdot(V[pl.ds(base, n), :], grad_j, 1, 1)
            prob = prob_low.astype(F32)
            both = prob * grad_prob
            inner = jnp.sum(both, axis=0, keepdims=True)
            score = (both - prob * inner).astype(BF)
            DV[pl.ds(0, n), :] += cdot(prob_low, grad_j, 1, 0)
            DK[pl.ds(0, n), :] += cdot(score, of_head(query, j), 1, 0)
            halves.append(cdot(KT[pl.ds(j * 64, 64), pl.ds(base, n)], score, 1, 0))
        grad_q = jnp.concatenate(halves, axis=0).T * 0.125
        GQKV[rows, 0:128] = turned(grad_q, cos, -sin).astype(BF)

    @pl.loop(0, 2)
    def _(s):
        DK[...] = jnp.zeros_like(DK)
        DV[...] = jnp.zeros_like(DV)
        for t in range(4):
            attend_back(s, t)
        for t in range(4):
            rows = rows_at(s * S + t * R, R)
            cos, sin = turn_tables_of(s, t)
            GQKV[rows, 128:256] = turned(DK[pl.ds(t * R, R), :], cos, -sin).astype(BF)
            GQKV[rows, 256:384] = DV[pl.ds(t * R, R), :].astype(BF)

    out = cdot(HT[...], GQKV[...], 1, 0).astype(BF).reshape(8, 2, d.rdg, d.qs)
    GQ[0] = out[:, 0]
    GQ[1] = out[:, 1]
    go(over_gy(GQ, yq, qsem))
    for h in range(2):
        add_one(mt, m2, 0, h, 0)
        go(hop_two(m2, m3, 0, h))
    for h in range(2):
        add_one(mt, m2, 0, h, 1)
    y_sum(GA, ya, asem, 8)
    f1_over_zp = remote(ya.at[pl.ds(oz * 4, 4)], za, asem.at[0, 1], asem.at[1, 1], zz_dev)
    go(f1_over_zp)


    f2_over_zp.wait_recv()
    for b in range(d.n_zp):
        rr = pl.ds(b * 128, 128)
        own = yb[rows_at(zp * b_rows + b * 128, 128), :]
        zb[rr, :] = (zb[rr, :].astype(F32) + own.astype(F32)).astype(BF)
    f2_cols = rows_at(gy * d.c2, d.c2)
    f2_mine = F2.at[rows_at(q * 128, 128), f2_cols]

    def f2_copies():
        for j in range(2):
            for ox in range(2):
                away = jnp.logical_not(jnp.logical_and(ox == gx, gx * 2 + j == q))
                src = zb.at[pl.ds(j * 128, 128)]
                yield away, src, remote(src, f2_mine, dsem.at[0, 0, j * 2 + ox], dsem.at[0, 1, q],
                                        place(gy, ox, zp, gx * 2 + j))

    for away, src, copy in f2_copies():
        here = pltpu.make_async_copy(src, f2_mine, dsem.at[0, 2, 0])

        @pl.when(away)
        def _():
            copy.start()

        @pl.when(jnp.logical_not(away))
        def _():
            here.start()
            here.wait()

    wo_src = zb.at[pl.ds(b_rows, 128)]
    wo_final = remote(wo_src, FWO.at[:, f2_cols], dsem.at[1, 0, 0], dsem.at[1, 1, 0], x_dev)
    wo_stay = pltpu.make_async_copy(wo_src, FWO.at[:, f2_cols], dsem.at[1, 2, 0])

    @pl.when(wo_zp == zp)
    def _():
        wo_over_zp.wait_recv()
        rr = pl.ds(b_rows, 128)
        zb[rr, :] = (zb[rr, :].astype(F32) + yb[pl.ds(d.ffs, 128), :].astype(F32)).astype(BF)
        wo_final.start()
        wo_stay.start()
        wo_stay.wait()

    for copy in cot_sends:
        copy.wait_send()

    @pl.loop(0, 8)
    def _(i):
        rows = rows_at(i * R, R)
        grad = cdot(SG[rows, :], WF1[...].reshape((W, d.ffs)), 1, 1)
        grad = grad + cdot(GQKV[rows, :], WQ[...].reshape(wq_all), 1, 1)
        normed, _ = normalise(TOK[rows, :])
        SUMS[0:1, :] += jnp.sum(grad * normed, axis=0, keepdims=True)
        SUMS[1:2, :] += jnp.sum(grad, axis=0, keepdims=True)
        COT[rows, :] = grad.astype(BF)
        to_twin(COT, ht, 1, i // 4, lax.rem(i, 4))

    for sq in range(4):
        away = jnp.logical_not(jnp.logical_and(gx == zl, sq == q))

        @pl.when(away)
        def _():
            remote(zb.at[pl.ds(0, 128)], F2.at[rows_at(sq * 128, 128), f2_cols], dsem.at[0, 0, 0],
                   dsem.at[0, 1, sq], x_dev).wait_recv()

    @pl.when(wo_zp != zp)
    def _():
        wo_final.wait_recv()

    go(remote(F2.at[:, f2_cols], F2.at[:, f2_cols], bsem.at[0, 3], bsem.at[1, 3], yy_dev))
    go(remote(FWO.at[:, f2_cols], FWO.at[:, f2_cols], bsem.at[0, 4], bsem.at[1, 4], yy_dev))
    add_twin(COT, ht, 1)
    for h in range(2):
        go(hop_one(ht, h2, 1, h, 0))
    SMG[...] = jnp.zeros_like(SMG)
    first_rank = jnp.where(me.rank == 0, 1.0, 0.0)
    for dd in range(d.n_dev):
        for k in range(3):
            piece = SUMS[k : k + 1, dd * 128 : (dd + 1) * 128]
            SMG[dd % 4, dd // 4, k : k + 1, :] = piece * first_rank if k == 2 else piece
    for b in range(d.ng):
        dq = gx * 2 + b % d.n_zp
        SMG[dq, b // d.n_zp, pl.ds(3 + q, 1), :] = SUMS[3:4, b * 128 : (b + 1) * 128]
    for i in range(1, 8):
        other = lax.rem(me.rank + i, 8)
        go(remote(SMG.at[lax.rem(other, 4)], s1.at[me.rank], ssem.at[0, 0, other],
                  ssem.at[0, 1, me.rank], place(gy, other // 4, zp, lax.rem(other, 4))))
    f_rows = rows_at(gy * d.rdg, d.rdg)

    def f1_pieces():
        for b in range(d.ng):
            f = ((b // d.n_zp * 2 + gx) * d.n_zp + b % d.n_zp) * 4 + q
            yield b, F1.at[f_rows, rows_at(f * 128, 128)]

    def fq_pieces():
        for k in range(3):
            yield k, FQ.at[f_rows, rows_at(k * W + me.rank * 128, 128)]

    def finish(done, mine, pieces, k):
        for b in range(4):
            done[b] = (done[b].astype(F32) + mine[zp * 4 + b].astype(F32)).astype(BF)
        for i in range(1, 8):
            other = lax.rem(me.rank + i, 8)
            ox, oq = other // 4, lax.rem(other, 4)
            for n, dst in pieces():
                remote(done.at[oq, :, pl.ds(n * 128, 128)], dst, dsem.at[k, 0, other],
                       dsem.at[k, 1, me.rank], place(gy, ox, zp, oq)).start()
        for n, dst in pieces():
            pltpu.make_async_copy(done.at[q, :, pl.ds(n * 128, 128)], dst, dsem.at[k, 2, 0]).start()
        pltpu.make_async_copy(done.at[0], done.at[0], dsem.at[k, 2, 0]).wait()

    def finished(done, k):
        for i in range(1, 8):
            other = lax.rem(me.rank + i, 8)
            remote(done.at[0], done.at[0], dsem.at[k, 0, other], dsem.at[k, 1, other],
                   x_dev).wait_recv()

    def finish_sent(done, k):
        for i in range(1, 8):
            other = lax.rem(me.rank + i, 8)
            remote(done.at[0], done.at[0], dsem.at[k, 0, other], dsem.at[k, 1, other],
                   x_dev).wait_send()

    y_sum(GQ, yq, qsem, 8)
    fq_over_zp = remote(yq.at[pl.ds(oz * 4, 4)], zq, qsem.at[0, 1], qsem.at[1, 1], zz_dev)
    go(fq_over_zp)
    f1_over_zp.wait_recv()
    finish(za, ya, f1_pieces, 2)
    for h in range(2):
        go(hop_one(ht, h2, 1, h, 1))
    for h in range(2):
        hop_two(m2, m3, 0, h).wait_recv()
        first_place = (q if h == 0 else 7 - q) * half
        rr = pl.ds(h * half, half)
        total = rows_of(m2, m3, h) + VEC[2:3, :]
        total = total + TOK[block(gx, q, h), :].astype(F32)
        MIXED[rr, :] = jnp.where(live_column(gx, first_place, half), total, 0.0).astype(BF)
    for h in range(2):
        add_one(ht, h2, 1, h, 0)
        go(hop_two(h2, h3, 1, h))
    fq_over_zp.wait_recv()
    finish(zq, yq, fq_pieces, 3)
    finished(za, 2)
    go(remote(F1.at[f_rows], F1.at[f_rows], asem.at[0, 2], asem.at[1, 2], yy_dev))
    for h in range(2):
        add_one(ht, h2, 1, h, 1)
    for i in range(1, 8):
        other = lax.rem(me.rank + i, 8)
        remote(SMG.at[0], s1.at[other], ssem.at[0, 0, other], ssem.at[0, 1, other],
               x_dev).wait_recv()
    s1[me.rank] = SMG[q]
    total = s1[0]
    for i in range(1, 8):
        total = total + s1[i]
    s2[d.ng] = total
    own_group = gy * d.n_zp + zp
    for i in range(1, d.ng):
        group = lax.rem(own_group + i, d.ng)
        to_z = lax.rem(group, d.n_zp)
        go(remote(s2.at[d.ng, to_z], s2.at[own_group, 0], ssem.at[1, 0, group],
                  ssem.at[1, 1, own_group], place(group // d.n_zp, gx, to_z, q)))
    finished(zq, 3)
    go(remote(FQ.at[f_rows], FQ.at[f_rows], qsem.at[0, 2], qsem.at[1, 2], yy_dev))
    for h in range(2):
        hop_two(h2, h3, 1, h).wait_recv()
        first_place = (q if h == 0 else 7 - q) * half
        rr = pl.ds(h * half, half)
        normed, inverse = normalise(TOK[block(gx, q, h), :])
        scaled = rows_of(h2, h3, h) * VEC[0:1, :]
        grad = inverse * (
            scaled
            - jnp.mean(scaled, axis=-1, keepdims=True)
            - normed * jnp.mean(scaled * normed, axis=-1, keepdims=True)
        )
        own = jnp.where(live_column(gx, first_place, half), OWN[rr, :].astype(F32), 0.0)
        TGRAD[rr, :] = (own + grad).astype(BF)
    for i in range(1, d.ng):
        group = lax.rem(own_group + i, d.ng)
        remote(s2.at[d.ng, 0], s2.at[group, 0], ssem.at[1, 0, group], ssem.at[1, 1, group],
               x_dev).wait_recv()
    total = s2[d.ng, zp]
    for i in range(1, d.ng):
        total = total + s2[lax.rem(own_group + i, d.ng), 0]
    FSM[...] = total
    o_rows, o_cols = rows_at(oy * d.rdg, d.rdg), rows_at(oy * d.c2, d.c2)
    remote(F2.at[:, o_cols], F2.at[:, o_cols], bsem.at[0, 3], bsem.at[1, 3], yy_dev).wait_recv()
    remote(FWO.at[:, o_cols], FWO.at[:, o_cols], bsem.at[0, 4], bsem.at[1, 4], yy_dev).wait_recv()
    remote(F1.at[o_rows], F1.at[o_rows], asem.at[0, 2], asem.at[1, 2], yy_dev).wait_recv()
    remote(FQ.at[o_rows], FQ.at[o_rows], qsem.at[0, 2], qsem.at[1, 2], yy_dev).wait_recv()
    twin_sent(MIXP, mt, 0)
    twin_sent(COT, ht, 1)
    for copy in sends:
        copy.wait_send()
    for k, buf in enumerate((WQ, WF1)):
        for i in range(1, 8):
            other = lax.rem(me.rank + i, 8)
            dst = w1_region(buf, gx, q)
            remote(dst, dst, w1s.at[k, other], w1r.at[k, other], x_dev).wait_send()

    @pl.when(jnp.logical_not(wo_mine))
    def _():
        wo_own.wait_send()

    @pl.when(wo_zp != zp)
    def _():
        wo_over_zp.wait_send()

    @pl.when(wo_zp == zp)
    def _():
        wo_final.wait_send()

    for away, src, copy in f2_copies():

        @pl.when(away)
        def _():
            copy.wait_send()

    finish_sent(za, 2)
    finish_sent(zq, 3)


def layer(d, lens, offs, tok, cot, wqkv, wo, wfc1, wf2, sm, c0, s0):
    smem = pl.BlockSpec(memory_space=pltpu.SMEM)
    vm = pl.BlockSpec(memory_space=pltpu.VMEM)
    hbm = pl.BlockSpec(memory_space=pl.ANY)
    dma = pltpu.SemaphoreType.DMA
    shape = jax.ShapeDtypeStruct
    R, W, half = d.rows, d.width, d.rows // 2
    N = 8 * R

    def bf(*dims):
        return pltpu.VMEM(dims, BF)

    def f32(*dims):
        return pltpu.VMEM(dims, F32)

    return pl.pallas_call(
        functools.partial(layer_kernel, d),
        out_shape=(
            shape((R, W), BF),
            shape((R, W), BF),
            shape((d.rd, d.ff), BF),
            shape((d.rd, 3 * W), BF),
            shape((d.ff // d.n_dev, W), BF),
            shape((d.rd, W), BF),
            shape((8, 128), F32),
        ),
        in_specs=[smem, smem] + [hbm] * 7 + [vm] * 2,
        out_specs=(vm,) * 7,
        scratch_shapes=[
            bf(N, W), bf(N, W), bf(N, W), bf(W, N),
            bf(N, 128), bf(N, 128), bf(N, 128), bf(128, N), bf(128, N),
            bf(4, R, R), bf(4, 2 * R, R), bf(4, 3 * R, R), bf(4, 4 * R, R),
            bf(N, d.ffs), bf(d.ffs + 128, N), bf(N, d.ffs), bf(N, 128), bf(N, 128), bf(N, d.qs),
            f32(4 * R, 128), f32(4 * R, 128), bf(N, W),
            bf(d.n_gy, 2, d.n_zp, 4 * d.r1, d.ffs), bf(d.n_gy, 2, d.n_zp, 4 * d.r1, d.qs),
            bf(d.n_gy, d.n_zp, d.r2, W), bf(128, W), bf(d.n_gy, 2, d.n_zp, 4, 16, 128),
            f32(16, W), f32(16, d.ffs), f32(4, d.n_zp, 8, 128), f32(8, W), bf(R, W),
            bf(2, 2, 2, half, W), bf(2, 2, half, W), bf(2, half, W),
            bf(2, 2, 2, half, W), bf(2, 2, half, W), bf(2, half, W),
            bf(d.n_gy, d.ffs + 128, d.c2), bf(d.n_gy, 8, d.rdg, d.ffs), bf(d.n_gy, 8, d.rdg, d.qs),
            bf(d.ffs + 128, d.c2), bf(8, d.rdg, d.ffs), bf(8, d.rdg, d.qs),
            bf(d.ffs // d.n_zp + 128, d.c2), bf(4, d.rdg, d.ffs), bf(4, d.rdg, d.qs),
            f32(8, d.n_zp, 8, 128), f32(d.ng + 1, d.n_zp, 8, 128),
            dma((8,)), dma((7, 2)), dma((8, 2)), dma((7, 2)), dma((8, 2)),
            dma((3, 8)), dma((3, 8)), dma((4,)), dma((4,)), dma((8,)), dma((8,)),
            dma((d.ng,)), dma((128 // d.r1,)),
            dma((2, 2, 14)), dma((2, 5)), dma((2, 3)), dma((2, 3)), dma((2, 2, 8)), dma((4, 3, 8)),
        ],
        compiler_params=pltpu.CompilerParams(
            has_side_effects=True, vmem_limit_bytes=67043328
        ),
        name="layer",
    )(lens, offs, tok, cot, wqkv, wo, wfc1, wf2, sm, c0, s0)


def place_tables(slot):
    freq = np.exp(np.arange(ROT // 2) * (-2.0 * math.log(10000.0) / ROT))
    angle = np.arange(slot)[:, None] * freq[np.arange(128) % (ROT // 2)][None]
    return np.cos(angle).astype(np.float32), np.sin(angle).astype(np.float32)


def small_pack(d, ln_gain, ln_bias, b_fc1, b_fc2):
    gap = jnp.zeros((3 * 128 - 3 * d.r1,), BF)
    rest = jnp.zeros((12 * 128,), BF)
    return jnp.concatenate([ln_gain, ln_bias, b_fc2, gap, b_fc1, rest]).reshape(16, 128)


def local_one(d, tokens, cotangent, lengths, offsets, ln_gain, ln_bias, w_qkv, w_out, w_fc1, b_fc1,
              w_fc2, b_fc2):
    sm = small_pack(d, ln_gain, ln_bias, b_fc1, b_fc2)
    c0, s0 = place_tables(4 * d.rows)
    mixed, token_grad, f1, fq, f2, fwo, small = layer(
        d, lengths, offsets, tokens, cotangent, w_qkv, w_out, w_fc1, w_fc2, sm,
        jnp.asarray(c0), jnp.asarray(s0),
    )
    per = d.rd
    return (mixed, token_grad, small[0, :per], small[1, :per], fq.astype(F32), fwo.astype(F32),
            f1.astype(F32), small[3:7].reshape(-1), f2.astype(F32), small[2, :per])


def solution(mesh):
    rows = ("grp", "dev")

    def program(*args):
        tokens, w_fc1 = args[0], args[8]
        n = mesh.shape["grp"] * mesh.shape["dev"]
        d = Dims(mesh, tokens.shape[0] // n, tokens.shape[1], w_fc1.shape[1])
        whole_tiles = d.n_gy == 2 and d.r2 == 128 and d.r1 % 16 == 0 and d.rd == 128
        return jax.shard_map(
            functools.partial(local_one if whole_tiles else local, d),
            mesh=mesh,
            in_specs=(
                P(rows, None), P(rows, None), P(), P(), P(rows), P(rows), P(rows, None),
                P(rows, None), P(rows, None), P(rows), P(rows, None), P(rows),
            ),
            out_specs=(
                P(rows, None), P(rows, None), P("dev"), P("dev"), P("dev", None), P("dev", None),
                P("dev", None), P("dev"), P("dev", None), P("dev"),
            ),
            check_vma=False,
        )(*args)

    return program
```

```python
import functools
import math

import jax
import jax.numpy as jnp
import numpy as np
from jax import lax
from jax.experimental import pallas as pl
from jax.experimental.pallas import tpu as pltpu
from jax.sharding import PartitionSpec as P

HEADS = 16
HD = 64
ROT = 32
MESH = pl.DeviceIdType.MESH
BF = jnp.bfloat16
F32 = jnp.float32


class Dims:
    def __init__(self, mesh, rows, width, ff):
        self.n_grp, self.n_dev = mesh.shape["grp"], mesh.shape["dev"]
        self.n_gy, self.n_zp = self.n_grp // 2, self.n_dev // 4
        assert self.n_gy == self.n_zp
        self.n_all = self.n_grp * self.n_dev
        self.rows, self.width, self.ff = rows, width, ff
        self.r1 = width // self.n_all
        self.r2 = ff // self.n_all
        self.ffs = ff // 8
        self.qs = 3 * width // 8
        self.ca = self.ffs + self.qs
        self.rd = width // self.n_dev
        self.rdg = self.rd // self.n_gy
        self.c2 = width // self.n_gy
        self.ng = self.n_gy * self.n_zp


class Me:
    def __init__(self, d):
        grp, dev = lax.axis_index("grp"), lax.axis_index("dev")
        self.grp, self.dev = grp, dev
        self.gy, self.gx = grp // 2, lax.rem(grp, 2)
        self.zp, self.q = dev // 4, lax.rem(dev, 4)
        self.zl, self.c = self.q // 2, lax.rem(self.q, 2)
        self.f = grp * d.n_dev + dev
        self.rank = self.gx * 4 + self.q


def place(gy, gx, zp, q):
    return {"grp": gy * 2 + gx, "dev": zp * 4 + q}


def remote(src, dst, send, recv, device):
    return pltpu.make_async_remote_copy(
        src_ref=src,
        dst_ref=dst,
        send_sem=send,
        recv_sem=recv,
        device_id=device,
        device_id_type=MESH,
    )


def gather_kernel(d, tok, cot, p1, wo, wf2, sm, TOK, COT, WA, WO, WF2, SM, loc, ts, tr, cs, cr,
                  w1s, w1r, m1s, m1r, zs, zr, ys, yr, os_, or_):
    me = Me(d)
    gy, gx, zp, q = me.gy, me.gx, me.zp, me.q
    half = d.rows // 2
    local = [
        pltpu.make_async_copy(tok, TOK.at[gx, q], loc.at[0]),
        pltpu.make_async_copy(cot, COT.at[gx, q], loc.at[1]),
        pltpu.make_async_copy(p1.at[me.rank], WA.at[gy, gx, zp, q], loc.at[2]),
        pltpu.make_async_copy(wf2, WF2.at[gy, zp], loc.at[3]),
        pltpu.make_async_copy(sm, SM.at[gy, gx, zp, q], loc.at[4]),
    ]

    def token_send(src, buf, send, recv, slot, bx, bq, h, device):
        return remote(
            src.at[pl.ds(h * half, half)],
            buf.at[bx, bq, pl.ds(h * half, half)],
            send.at[slot, h],
            recv.at[bx * 4 + bq, h],
            device,
        )

    x_dev, z_dev, c_dev = place(gy, 1 - gx, zp, q), place(gy, gx, zp, lax.rem(q + 2, 4)), place(
        gy, gx, zp, me.zl * 2 + 1 - me.c
    )
    qz = lax.rem(q + 2, 4)

    sends = []

    def go(copy):
        copy.start()
        sends.append(copy)

    def arrived(buf, send, recv, bx, bq, h):
        token_send(buf.at[bx, bq], buf, send, recv, 0, bx, bq, h, x_dev).wait_recv()

    for h in range(2):
        go(token_send(tok, TOK, ts, tr, 0, gx, q, h, x_dev))
        go(token_send(cot, COT, cs, cr, 0, gx, q, h, z_dev))
    for i in range(1, 8):
        other = lax.rem(me.rank + i, 8)
        dev = place(gy, other // 4, zp, lax.rem(other, 4))
        go(remote(p1.at[other], WA.at[gy, gx, zp, q], w1s.at[other], w1r.at[me.rank], dev))
        go(remote(sm, SM.at[gy, gx, zp, q], m1s.at[other], m1r.at[me.rank], dev))
    for copy in local:
        copy.start()
    for i in range(1, d.n_zp):
        oz = lax.rem(zp + i, d.n_zp)
        go(remote(wf2, WF2.at[gy, zp], zs.at[2, oz], zr.at[2, zp], place(gy, gx, oz, q)))
    per = 128 // d.r1
    owner = me.f // per
    part = lax.rem(me.f, per)
    ox, oq = owner // 4, lax.rem(owner, 4)
    for i in range(d.ng):
        group = lax.rem(gy * d.n_zp + zp + i, d.ng)
        oy, oz = group // d.n_zp, lax.rem(group, d.n_zp)
        copy = remote(wo, WO.at[part], os_.at[i], or_.at[part], place(oy, ox, oz, oq))
        if i == 0:
            mine = jnp.logical_and(ox == gx, oq == q)

            @pl.when(mine)
            def _():
                here = pltpu.make_async_copy(wo, WO.at[part], loc.at[5])
                here.start()
                here.wait()

            @pl.when(jnp.logical_not(mine))
            def _():
                copy.start()
                copy.wait_send()
        else:
            go(copy)
    for h in range(2):
        go(token_send(tok, TOK, ts, tr, 1, gx, q, h, z_dev))
        go(token_send(cot, COT, cs, cr, 1, gx, q, h, x_dev))
        go(token_send(tok, TOK, ts, tr, 3, gx, q, h, c_dev))
        go(token_send(cot, COT, cs, cr, 3, gx, q, h, c_dev))
    for h in range(2):
        arrived(TOK, ts, tr, 1 - gx, q, h)
        go(token_send(TOK.at[1 - gx, q], TOK, ts, tr, 2, 1 - gx, q, h, z_dev))
        go(token_send(TOK.at[1 - gx, q], TOK, ts, tr, 4, 1 - gx, q, h, c_dev))
        arrived(COT, cs, cr, gx, qz, h)
        go(token_send(COT.at[gx, qz], COT, cs, cr, 2, gx, qz, h, x_dev))
        go(token_send(COT.at[gx, qz], COT, cs, cr, 4, gx, qz, h, c_dev))
    for copy in local:
        copy.wait()
    for i in range(1, 8):
        other = lax.rem(me.rank + i, 8)
        ox_, oq_ = other // 4, lax.rem(other, 4)
        dev = place(gy, ox_, zp, oq_)
        remote(p1.at[0], WA.at[gy, ox_, zp, oq_], w1s.at[other], w1r.at[other], dev).wait_recv()
        remote(sm, SM.at[gy, ox_, zp, oq_], m1s.at[other], m1r.at[other], dev).wait_recv()
    for i in range(1, d.n_zp):
        oz = lax.rem(zp + i, d.n_zp)
        dev = place(gy, gx, oz, q)
        go(remote(WA.at[gy, :, zp], WA.at[gy, :, zp], zs.at[0, oz], zr.at[0, zp], dev))
        go(remote(SM.at[gy, :, zp], SM.at[gy, :, zp], zs.at[1, oz], zr.at[1, zp], dev))
    for i in range(1, d.n_zp):
        oz = lax.rem(zp + i, d.n_zp)
        remote(wf2, WF2.at[gy, oz], zs.at[2, oz], zr.at[2, oz], place(gy, gx, oz, q)).wait_recv()
    for i in range(1, d.n_gy):
        oy = lax.rem(gy + i, d.n_gy)
        go(remote(WF2.at[gy], WF2.at[gy], ys.at[2, oy], yr.at[2, gy], place(oy, gx, zp, q)))
    for h in range(2):
        arrived(TOK, ts, tr, gx, qz, h)
        go(token_send(TOK.at[gx, qz], TOK, ts, tr, 5, gx, qz, h, c_dev))
        arrived(COT, cs, cr, 1 - gx, q, h)
        go(token_send(COT.at[1 - gx, q], COT, cs, cr, 5, 1 - gx, q, h, c_dev))
    for h in range(2):
        arrived(TOK, ts, tr, 1 - gx, qz, h)
        go(token_send(TOK.at[1 - gx, qz], TOK, ts, tr, 6, 1 - gx, qz, h, c_dev))
        arrived(COT, cs, cr, 1 - gx, qz, h)
        go(token_send(COT.at[1 - gx, qz], COT, cs, cr, 6, 1 - gx, qz, h, c_dev))
    for i in range(1, d.n_zp):
        oz = lax.rem(zp + i, d.n_zp)
        dev = place(gy, gx, oz, q)
        remote(WA.at[gy, :, oz], WA.at[gy, :, oz], zs.at[0, oz], zr.at[0, oz], dev).wait_recv()
        remote(SM.at[gy, :, oz], SM.at[gy, :, oz], zs.at[1, oz], zr.at[1, oz], dev).wait_recv()
    for i in range(1, d.n_gy):
        oy = lax.rem(gy + i, d.n_gy)
        dev = place(oy, gx, zp, q)
        go(remote(WA.at[gy], WA.at[gy], ys.at[0, oy], yr.at[0, gy], dev))
        go(remote(SM.at[gy], SM.at[gy], ys.at[1, oy], yr.at[1, gy], dev))
    qc = me.zl * 2 + 1 - me.c
    qcz = lax.rem(qc + 2, 4)
    for bx in (gx, 1 - gx):
        for bq in (qc, qcz):
            for h in range(2):
                arrived(TOK, ts, tr, bx, bq, h)
                arrived(COT, cs, cr, bx, bq, h)
    for i in range(1, d.n_gy):
        oy = lax.rem(gy + i, d.n_gy)
        dev = place(oy, gx, zp, q)
        for k, buf in enumerate((WA, SM, WF2)):
            remote(buf.at[oy], buf.at[oy], ys.at[k, oy], yr.at[k, oy], dev).wait_recv()
    for i in range(per):
        source = me.rank * per + i

        @pl.when(source != me.f)
        def _():
            remote(wo, WO.at[i], os_.at[0], or_.at[i], x_dev).wait_recv()

    for copy in sends:
        copy.wait_send()


def gather(d, tok, cot, p1, wo, wf2, sm):
    any_spec = pl.BlockSpec(memory_space=pl.ANY)
    dma = pltpu.SemaphoreType.DMA
    shape = jax.ShapeDtypeStruct
    return pl.pallas_call(
        functools.partial(gather_kernel, d),
        out_shape=(
            shape((2, 4, d.rows, d.width), BF),
            shape((2, 4, d.rows, d.width), BF),
            shape((d.n_gy, 2, d.n_zp, 4, d.r1, d.ca), BF),
            shape((128 // d.r1, d.r1, d.width), BF),
            shape((d.n_gy, d.n_zp, d.r2, d.width), BF),
            shape((d.n_gy, 2, d.n_zp, 4, 16, 128), BF),
        ),
        in_specs=[any_spec] * 6,
        out_specs=(any_spec,) * 6,
        scratch_shapes=[
            dma((6,)), dma((7, 2)), dma((8, 2)), dma((7, 2)), dma((8, 2)),
            dma((8,)), dma((8,)), dma((8,)), dma((8,)),
            dma((3, d.n_zp)), dma((3, d.n_zp)), dma((3, d.n_gy)), dma((3, d.n_gy)),
            dma((d.ng,)), dma((128 // d.r1,)),
        ],
        compiler_params=pltpu.CompilerParams(has_side_effects=True),
        name="gather",
    )(tok, cot, p1, wo, wf2, sm)


def add_blocks(out, *terms):
    n = out.shape[0]

    @pl.loop(0, n)
    def _(i):
        total = terms[0][i].astype(F32)
        for term in terms[1:]:
            total = total + term[i].astype(F32)
        out[i] = total.astype(out.dtype)


def reduce_kernel(d, mix, gh, ga, gf2, gwo, smg, MIX, GH, FA, FF2, FWO, FSM,
                  mt, m2, m3, ht, h2, h3, ya, y2, yo, za, z2, zo, s1, s2,
                  tsem, asem, fsem, osem, ssem, dsem):
    me = Me(d)
    gy, gx, zp, q, zl, c = me.gy, me.gx, me.zp, me.q, me.zl, me.c
    x_dev, z_dev, c_dev = place(gy, 1 - gx, zp, q), place(gy, gx, zp, lax.rem(q + 2, 4)), place(
        gy, gx, zp, zl * 2 + 1 - c
    )
    sends = []

    def go(copy):
        copy.start()
        sends.append(copy)

    for i in range(1, d.n_gy):
        oy = lax.rem(gy + i, d.n_gy)
        dev = place(oy, gx, zp, q)
        go(remote(gf2.at[:, :, oy], y2.at[gy], fsem.at[0, 0, oy], fsem.at[0, 1, gy], dev))
        go(remote(gwo.at[oy], yo.at[gy], osem.at[0, 0, oy], osem.at[0, 1, gy], dev))
        go(remote(ga.at[:, :, oy], ya.at[gy], asem.at[0, 0, oy], asem.at[0, 1, gy], dev))
    row_sums = ((mix, mt, m2, m3, MIX, 0), (gh, ht, h2, h3, GH, 1))
    for src, t_buf, _, _, _, k in row_sums:
        go(remote(src.at[:, :, 1 - c], t_buf, tsem.at[k, 0, 0], tsem.at[k, 1, 0], c_dev))
    for i in range(1, 8):
        other = lax.rem(me.rank + i, 8)
        oq = lax.rem(other, 4)
        go(remote(smg.at[oq], s1.at[me.rank], ssem.at[0, 0, other], ssem.at[0, 1, me.rank],
                  place(gy, other // 4, zp, oq)))
    for src, t_buf, b2, b3, _, k in row_sums:
        remote(src.at[:, :, 1 - c], t_buf, tsem.at[k, 0, 0], tsem.at[k, 1, 0], c_dev).wait_recv()
        for bx in range(2):
            for bz in range(2):
                add_blocks(t_buf.at[bx, bz], t_buf.at[bx, bz], src.at[bx, bz, c])
        if k == 0:
            go(remote(t_buf.at[1 - gx], b2, tsem.at[k, 0, 1], tsem.at[k, 1, 1], x_dev))
        else:
            go(remote(t_buf.at[:, 1 - zl], b2, tsem.at[k, 0, 1], tsem.at[k, 1, 1], z_dev))
    for i in range(1, d.n_gy):
        oy = lax.rem(gy + i, d.n_gy)
        dev = place(oy, gx, zp, q)
        remote(gf2.at[:, :, oy], y2.at[oy], fsem.at[0, 0, oy], fsem.at[0, 1, oy], dev).wait_recv()
        remote(gwo.at[oy], yo.at[oy], osem.at[0, 0, oy], osem.at[0, 1, oy], dev).wait_recv()
    others = [lax.rem(gy + i, d.n_gy) for i in range(1, d.n_gy)]
    for a in range(d.n_gy):
        for b in range(d.n_zp):
            add_blocks(y2.at[gy, a, b], gf2.at[a, b, gy], *[y2.at[o, a, b] for o in others])
    add_blocks(yo.at[gy], gwo.at[gy], *[yo.at[o] for o in others])
    for i in range(1, d.n_zp):
        oz = lax.rem(zp + i, d.n_zp)
        dev = place(gy, gx, oz, q)
        go(remote(y2.at[gy, oz], z2.at[zp], fsem.at[1, 0, oz], fsem.at[1, 1, zp], dev))
        go(remote(yo.at[gy], zo.at[zp], osem.at[1, 0, oz], osem.at[1, 1, zp], dev))
    for i in range(1, d.n_gy):
        oy = lax.rem(gy + i, d.n_gy)
        dev = place(oy, gx, zp, q)
        remote(ga.at[:, :, oy], ya.at[oy], asem.at[0, 0, oy], asem.at[0, 1, oy], dev).wait_recv()
    for a in range(d.n_zp):
        for b in range(4):
            add_blocks(ya.at[gy, a, b], ga.at[a, b, gy], *[ya.at[o, a, b] for o in others])
    for i in range(1, d.n_zp):
        oz = lax.rem(zp + i, d.n_zp)
        go(remote(ya.at[gy, oz], za.at[zp], asem.at[1, 0, oz], asem.at[1, 1, zp],
                  place(gy, gx, oz, q)))
    for i in range(1, 8):
        other = lax.rem(me.rank + i, 8)
        remote(smg.at[0], s1.at[other], ssem.at[0, 0, other], ssem.at[0, 1, other],
               x_dev).wait_recv()
    s1[me.rank] = smg[q]
    total = s1[0]
    for i in range(1, 8):
        total = total + s1[i]
    s2[d.ng] = total
    own_group = gy * d.n_zp + zp
    for i in range(1, d.ng):
        group = lax.rem(own_group + i, d.ng)
        oy, oz = group // d.n_zp, lax.rem(group, d.n_zp)
        go(remote(s2.at[d.ng, oz], s2.at[own_group, 0], ssem.at[1, 0, group],
                  ssem.at[1, 1, own_group], place(oy, gx, oz, q)))
    for src, t_buf, b2, b3, _, k in row_sums:
        if k == 0:
            remote(t_buf.at[1 - gx], b2, tsem.at[k, 0, 1], tsem.at[k, 1, 1], x_dev).wait_recv()
            for b in range(2):
                add_blocks(b2.at[b], b2.at[b], t_buf.at[gx, b])
            go(remote(b2.at[1 - zl], b3, tsem.at[k, 0, 2], tsem.at[k, 1, 2], z_dev))
        else:
            remote(t_buf.at[:, 1 - zl], b2, tsem.at[k, 0, 1], tsem.at[k, 1, 1], z_dev).wait_recv()
            for b in range(2):
                add_blocks(b2.at[b], b2.at[b], t_buf.at[b, zl])
            go(remote(b2.at[1 - gx], b3, tsem.at[k, 0, 2], tsem.at[k, 1, 2], x_dev))
    zothers = [lax.rem(zp + i, d.n_zp) for i in range(1, d.n_zp)]
    for o in zothers:
        dev = place(gy, gx, o, q)
        remote(y2.at[gy, o], z2.at[o], fsem.at[1, 0, o], fsem.at[1, 1, o], dev).wait_recv()
        remote(yo.at[gy], zo.at[o], osem.at[1, 0, o], osem.at[1, 1, o], dev).wait_recv()
    hz = d.n_zp // 2
    for b in range(d.n_zp):
        add_blocks(z2.at[zp, b], y2.at[gy, zp, b], *[z2.at[o, b] for o in zothers])
    add_blocks(zo.at[zp], yo.at[gy], *[zo.at[o] for o in zothers])
    for j in range(2):
        dq = gx * 2 + j
        for ox in range(2):
            mine = jnp.logical_and(ox == gx, dq == q)
            src = z2.at[zp, pl.ds(j * hz, hz)]
            dst = FF2.at[gy, q]
            copy = remote(src, dst, dsem.at[0, 0, j * 2 + ox], dsem.at[0, 1, q],
                          place(gy, ox, zp, dq))

            @pl.when(mine)
            def _():
                here = pltpu.make_async_copy(src, dst, dsem.at[0, 2, 0])
                here.start()
                here.wait()

            @pl.when(jnp.logical_not(mine))
            def _():
                copy.start()
    nwo = 128 // d.rd
    wo_zp = me.rank * d.n_zp // 8
    for j in range(nwo):
        dq = lax.rem(me.rank * nwo + j, 4)
        for ox in range(2):
            here_too = jnp.logical_and(ox == gx, dq == q)
            src = zo.at[zp, pl.ds(j * (d.rd // 16), d.rd // 16)]
            dst = FWO.at[gy]
            copy = remote(src, dst, dsem.at[1, 0, j * 2 + ox], dsem.at[1, 1, 0],
                          place(gy, ox, zp, dq))

            @pl.when(jnp.logical_and(wo_zp == zp, here_too))
            def _():
                here = pltpu.make_async_copy(src, dst, dsem.at[1, 2, 0])
                here.start()
                here.wait()

            @pl.when(jnp.logical_and(wo_zp == zp, jnp.logical_not(here_too)))
            def _():
                copy.start()
    for o in zothers:
        dev = place(gy, gx, o, q)
        remote(ya.at[gy, o], za.at[o], asem.at[1, 0, o], asem.at[1, 1, o], dev).wait_recv()
    for b in range(4):
        add_blocks(za.at[zp, b], ya.at[gy, zp, b], *[za.at[o, b] for o in zothers])
    for i in range(1, 8):
        other = lax.rem(me.rank + i, 8)
        ox, oq = other // 4, lax.rem(other, 4)
        go(remote(za.at[zp, oq], FA.at[gy, gx, q], dsem.at[2, 0, other],
                  dsem.at[2, 1, me.rank], place(gy, ox, zp, oq)))
    here = pltpu.make_async_copy(za.at[zp, q], FA.at[gy, gx, q], dsem.at[2, 2, 0])
    here.start()
    here.wait()
    for src, t_buf, b2, b3, out, k in row_sums:
        if k == 0:
            remote(b2.at[1 - zl], b3, tsem.at[k, 0, 2], tsem.at[k, 1, 2], z_dev).wait_recv()
            mine = b2.at[zl]
        else:
            remote(b2.at[1 - gx], b3, tsem.at[k, 0, 2], tsem.at[k, 1, 2], x_dev).wait_recv()
            mine = b2.at[gx]
        n = out.shape[0]
        for i in range(n):
            out[i] = mine[i].astype(F32) + b3[i].astype(F32)
    for sq in range(4):
        away = jnp.logical_not(jnp.logical_and(gx == zl, sq == q))

        @pl.when(away)
        def _():
            remote(z2.at[0, pl.ds(0, hz)], FF2.at[gy, sq], dsem.at[0, 0, 0], dsem.at[0, 1, sq],
                   x_dev).wait_recv()
    source = (zp * 4 + q) // nwo
    sx, sq = source // 4, lax.rem(source, 4)

    @pl.when(jnp.logical_not(jnp.logical_and(sx == gx, sq == q)))
    def _():
        remote(zo.at[0, pl.ds(0, d.rd // 16)], FWO.at[gy], dsem.at[1, 0, 0], dsem.at[1, 1, 0],
               x_dev).wait_recv()
    for o in others:
        dev = place(o, gx, zp, q)
        go(remote(FF2.at[gy], FF2.at[gy], fsem.at[2, 0, o], fsem.at[2, 1, gy], dev))
        go(remote(FWO.at[gy], FWO.at[gy], osem.at[2, 0, o], osem.at[2, 1, gy], dev))
    for i in range(1, 8):
        other = lax.rem(me.rank + i, 8)
        ox, oq = other // 4, lax.rem(other, 4)
        remote(za.at[0, 0], FA.at[gy, ox, oq], dsem.at[2, 0, other], dsem.at[2, 1, other],
               x_dev).wait_recv()
    for o in others:
        dev = place(o, gx, zp, q)
        go(remote(FA.at[gy], FA.at[gy], asem.at[2, 0, o], asem.at[2, 1, gy], dev))
    for i in range(1, d.ng):
        group = lax.rem(own_group + i, d.ng)
        remote(s2.at[d.ng, 0], s2.at[group, 0], ssem.at[1, 0, group], ssem.at[1, 1, group],
               x_dev).wait_recv()
    total = s2[d.ng, zp]
    for i in range(1, d.ng):
        total = total + s2[lax.rem(own_group + i, d.ng), 0]
    FSM[...] = total
    for o in others:
        dev = place(o, gx, zp, q)
        for buf, sem in ((FF2, fsem), (FWO, osem), (FA, asem)):
            remote(buf.at[o], buf.at[o], sem.at[2, 0, o], sem.at[2, 1, o], dev).wait_recv()
    for copy in sends:
        copy.wait_send()
    for j in range(2):
        for ox in range(2):
            away = jnp.logical_not(jnp.logical_and(ox == gx, gx * 2 + j == q))

            @pl.when(away)
            def _():
                remote(z2.at[zp, pl.ds(j * hz, hz)], FF2.at[gy, q], dsem.at[0, 0, j * 2 + ox],
                       dsem.at[0, 1, q], x_dev).wait_send()
    for j in range(nwo):
        dq = lax.rem(me.rank * nwo + j, 4)
        for ox in range(2):
            away = jnp.logical_not(jnp.logical_and(ox == gx, dq == q))

            @pl.when(jnp.logical_and(wo_zp == zp, away))
            def _():
                remote(zo.at[zp, pl.ds(j * (d.rd // 16), d.rd // 16)], FWO.at[gy], dsem.at[1, 0, j * 2 + ox],
                       dsem.at[1, 1, 0], x_dev).wait_send()


def reduce_all(d, mix, gh, ga, gf2, gwo, smg):
    vm = pl.BlockSpec(memory_space=pltpu.VMEM)
    dma = pltpu.SemaphoreType.DMA
    shape = jax.ShapeDtypeStruct
    R = d.rows
    slabs = R // 16
    return pl.pallas_call(
        functools.partial(reduce_kernel, d),
        out_shape=(
            shape((slabs, 16, d.width), F32),
            shape((slabs, 16, d.width), F32),
            shape((d.n_gy, 2, 4, d.rdg // 16, 16, d.ca), BF),
            shape((d.n_gy, 4, d.n_zp // 2, d.r2 // 16, 16, d.c2), BF),
            shape((d.n_gy, d.rd // 16, 16, d.c2), BF),
            shape((8, 128), F32),
        ),
        in_specs=[vm] * 6,
        out_specs=(vm,) * 6,
        scratch_shapes=[
            pltpu.VMEM((2, 2, slabs, 16, d.width), BF),
            pltpu.VMEM((2, slabs, 16, d.width), BF),
            pltpu.VMEM((slabs, 16, d.width), BF),
            pltpu.VMEM((2, 2, slabs, 16, d.width), BF),
            pltpu.VMEM((2, slabs, 16, d.width), BF),
            pltpu.VMEM((slabs, 16, d.width), BF),
            pltpu.VMEM((d.n_gy, d.n_zp, 4, d.rdg // 16, 16, d.ca), BF),
            pltpu.VMEM((d.n_gy, d.n_gy, d.n_zp, d.r2 // 16, 16, d.c2), BF),
            pltpu.VMEM((d.n_gy, 8, 16, d.c2), BF),
            pltpu.VMEM((d.n_zp, 4, d.rdg // 16, 16, d.ca), BF),
            pltpu.VMEM((d.n_zp, d.n_zp, d.r2 // 16, 16, d.c2), BF),
            pltpu.VMEM((d.n_zp, 8, 16, d.c2), BF),
            pltpu.VMEM((8, d.n_zp, 8, 128), F32),
            pltpu.VMEM((d.ng + 1, d.n_zp, 8, 128), F32),
            dma((2, 2, 3)),
            dma((3, 2, max(d.n_gy, d.n_zp))),
            dma((3, 2, max(d.n_gy, d.n_zp))),
            dma((3, 2, max(d.n_gy, d.n_zp))),
            dma((2, 2, max(8, d.ng))),
            dma((3, 3, 8)),
        ],
        compiler_params=pltpu.CompilerParams(
            has_side_effects=True, vmem_limit_bytes=62 * 1024 * 1024
        ),
        name="reduce",
    )(mix, gh, ga, gf2, gwo, smg)


def gelu_parts(v):
    tangent = jnp.tanh(0.7978845608028654 * (v + 0.044715 * v * v * v))
    inner = 0.7978845608028654 * (1.0 + 0.134145 * v * v)
    act = 0.5 * v * (1.0 + tangent)
    slope = 0.5 * (1.0 + tangent) + 0.5 * v * (1.0 - tangent * tangent) * inner
    return act, slope


def places_of_slot(rows):
    slot = 4 * rows
    row = jnp.arange(slot, dtype=jnp.int32)
    piece, inner, half = row // rows, row % rows, rows // 2
    return jnp.where(inner < half, piece * half + inner, slot - (piece + 1) * half + inner - half)


def spread(vec, lane):
    n = vec.shape[0]
    if n == 128:
        return vec
    tiled = jnp.tile(vec, 128 // n)
    at = jnp.arange(128, dtype=jnp.int32) // n
    return jnp.where(at == lane, tiled, jnp.zeros_like(tiled))


def dot(a, b, dims):
    return lax.dot_general(a, b, (dims, ((), ())), preferred_element_type=F32)


def local(d, tokens, cotangent, lengths, offsets, ln_gain, ln_bias, w_qkv, w_out, w_fc1, b_fc1,
          w_fc2, b_fc2):
    me = Me(d)
    R, W = d.rows, d.width
    fc1 = w_fc1.reshape(d.r1, d.n_gy, 2, d.n_zp, 4, d.r2).transpose(2, 4, 0, 1, 3, 5)
    fc1 = fc1.reshape(8, d.r1, d.ffs)
    qkv = w_qkv.reshape(d.r1, 3, 8, 128).transpose(2, 0, 1, 3).reshape(8, d.r1, d.qs)
    p1 = jnp.concatenate([fc1, qkv], axis=2)
    lane = lax.rem(me.f, 128 // d.r1)
    pad = jnp.zeros((128 - d.r2,), BF)
    sm = jnp.stack([spread(ln_gain, lane), spread(ln_bias, lane), spread(b_fc2, lane),
                    jnp.concatenate([b_fc1, pad]) if d.r2 < 128 else b_fc1])
    sm = jnp.concatenate([sm, jnp.zeros((12, 128), BF)])
    TOK, COT, WA, WO, WF2, SM = gather(d, tokens, cotangent, p1, w_out, w_fc2, sm)
    sums = SM.reshape(8, d.n_all // 8, 16, 128).astype(F32).sum(axis=1)
    gain, bias, bfc2 = sums[:, 0].reshape(W), sums[:, 1].reshape(W), sums[:, 2].reshape(W)
    mine = lax.dynamic_index_in_dim(
        lax.dynamic_index_in_dim(SM, me.gx, 1, False), me.q, 2, False
    )
    bfc1 = mine[:, :, 3, : d.r2].reshape(d.ffs).astype(F32)
    WA = WA.reshape(W, d.ca)
    wfc1, wqkv = WA[:, : d.ffs], WA[:, d.ffs :]
    wout = WO.reshape(128, W)
    wfc2 = WF2.reshape(d.ffs, W)
    slot0 = (me.gy * 2) * d.n_zp + me.zp
    lens = jnp.stack([lengths[slot0], lengths[slot0 + d.n_zp]])
    offs = jnp.stack([offsets[slot0], offsets[slot0 + d.n_zp]])
    places = places_of_slot(R)
    live = (places[None] >= offs[:, None]) & (places[None] < (offs + lens)[:, None])
    live_f = live.reshape(8 * R, 1).astype(F32)
    tok = TOK.reshape(8 * R, W).astype(F32)
    centred = tok - jnp.mean(tok, axis=-1, keepdims=True)
    inverse = lax.rsqrt(jnp.mean(centred * centred, axis=-1, keepdims=True) + 1e-5)
    normed = centred * inverse
    h = (normed * gain + bias).astype(BF)
    grad_y = (COT.reshape(8 * R, W).astype(F32) * live_f).astype(BF)
    qkv = dot(h, wqkv, ((1,), (0,)))
    freq = jnp.exp(jnp.arange(ROT // 2, dtype=F32) * (-2.0 * math.log(10000.0) / ROT))
    angles = (places[None] - offs[:, None]).astype(F32).reshape(8 * R)[:, None] * freq[None]
    cos, sin = jnp.cos(angles)[:, None], jnp.sin(angles)[:, None]

    def turn(x, sign):
        a, b = x[..., : ROT // 2], x[..., ROT // 2 : ROT]
        return jnp.concatenate(
            [a * cos - sign * b * sin, b * cos + sign * a * sin, x[..., ROT:]], axis=-1
        )

    queries = turn(qkv[:, :128].reshape(8 * R, 2, HD), 1.0).astype(BF).reshape(2, 4 * R, 2, HD)
    keys = turn(qkv[:, 128:256].reshape(8 * R, 2, HD), 1.0).astype(BF).reshape(2, 4 * R, 2, HD)
    values = qkv[:, 256:].astype(BF).reshape(2, 4 * R, 2, HD)
    scores = jnp.einsum("sqhd,skhd->shqk", queries, keys, preferred_element_type=F32) * 0.125
    allowed = (places[None, None, :] <= places[None, :, None]) & (
        live[:, None, :] | (places[None, None, :] == places[None, :, None])
    )
    scores = jnp.where(allowed[:, None], scores, -1e30)
    expo = jnp.exp(scores - jnp.max(scores, axis=-1, keepdims=True))
    prob = expo / jnp.sum(expo, axis=-1, keepdims=True)
    low = prob.astype(BF)
    att = jnp.einsum("shqk,skhd->sqhd", low, values, preferred_element_type=F32)
    att = att.astype(BF).reshape(8 * R, 128)
    pre = dot(h, wfc1, ((1,), (0,))) + bfc1
    act, slope = gelu_parts(pre)
    act = act.astype(BF)
    mix = dot(att, wout, ((1,), (0,))) + dot(act, wfc2, ((1,), (0,)))
    g_wo = dot(att, grad_y, ((0,), (0,)))
    g_f2 = dot(act, grad_y, ((0,), (0,)))
    grad_pre = (dot(grad_y, wfc2, ((1,), (1,))) * slope).astype(BF)
    g_f1 = dot(h, grad_pre, ((0,), (0,)))
    g_bf1 = grad_pre.astype(F32).sum(axis=0)
    grad_att = dot(grad_y, wout, ((1,), (1,))).astype(BF).reshape(2, 4 * R, 2, HD)
    g_prob = jnp.einsum("sqhd,skhd->shqk", grad_att, values, preferred_element_type=F32)
    row_dot = jnp.sum(prob * g_prob, axis=-1, keepdims=True)
    g_score = (prob * (g_prob - row_dot)).astype(BF)
    g_v = jnp.einsum("shqk,sqhd->skhd", low, grad_att, preferred_element_type=F32)
    g_q = jnp.einsum("shqk,skhd->sqhd", g_score, keys, preferred_element_type=F32) * 0.125
    g_k = jnp.einsum("shqk,sqhd->skhd", g_score, queries, preferred_element_type=F32) * 0.125
    g_q = turn(g_q.reshape(8 * R, 2, HD), -1.0).reshape(8 * R, 128)
    g_k = turn(g_k.reshape(8 * R, 2, HD), -1.0).reshape(8 * R, 128)
    g_qkv = jnp.concatenate([g_q, g_k, g_v.reshape(8 * R, 128)], axis=1).astype(BF)
    g_wqkv = dot(h, g_qkv, ((0,), (0,)))
    gh = dot(grad_pre, wfc1, ((1,), (1,))) + dot(g_qkv, wqkv, ((1,), (1,)))
    g_gain, g_bias = (gh * normed).sum(axis=0), gh.sum(axis=0)
    g_bf2 = jnp.where(me.rank == 0, grad_y.astype(F32).sum(axis=0), 0.0)
    nd, per = d.n_dev, W // d.n_dev

    def wide(x):
        x = x.reshape(nd, -1)
        n = x.shape[1]
        if n < 128:
            x = jnp.concatenate([x, jnp.zeros((nd, 128 - n), F32)], axis=1)
        return x.reshape(nd, -1, 128)

    bf1_rows = max(d.ff // nd // 128, 1)
    full = jnp.zeros((d.n_gy, 2, d.n_zp, 4, d.r2), F32)
    full = lax.dynamic_update_slice(
        full, g_bf1.reshape(d.n_gy, 1, d.n_zp, 1, d.r2), (0, me.gx, 0, me.q, 0)
    )
    smg = jnp.concatenate(
        [wide(g_gain), wide(g_bias), wide(g_bf2), wide(full.reshape(d.ff)),
         jnp.zeros((nd, 5 - bf1_rows, 128), F32)], axis=1,
    )
    smg = smg.reshape(d.n_zp, 4, 8, 128).transpose(1, 0, 2, 3)
    slabs = R // 16
    mix_p = mix.astype(BF).reshape(2, 2, 2, slabs, 16, W)
    gh_p = gh.astype(BF).reshape(2, 2, 2, slabs, 16, W)
    ga = jnp.concatenate([g_f1, g_wqkv], axis=1).astype(BF)
    ga = ga.reshape(d.n_zp, 4, d.n_gy, d.rdg // 16, 16, d.ca)
    gf2 = g_f2.astype(BF).reshape(d.n_gy, d.n_zp, d.r2 // 16, 16, d.n_gy, d.c2)
    gf2 = gf2.transpose(0, 1, 4, 2, 3, 5)
    gwo = g_wo.astype(BF).reshape(8, 16, d.n_gy, d.c2).transpose(2, 0, 1, 3)
    MIX, GH, FA, FF2, FWO, FSM = reduce_all(d, mix_p, gh_p, ga, gf2, gwo, smg)
    own = me.gx * 4 + me.q

    def own_rows(x):
        return lax.dynamic_index_in_dim(x.reshape(8, R, x.shape[-1]), own, 0, False)

    my_live, my_normed, my_inv = own_rows(live_f), own_rows(normed), own_rows(inverse)
    mixed = (my_live * (tokens.astype(F32) + MIX.reshape(R, W) + bfc2)).astype(BF)
    scaled = GH.reshape(R, W) * gain
    grad_norm = my_inv * (
        scaled - jnp.mean(scaled, axis=-1, keepdims=True)
        - my_normed * jnp.mean(scaled * my_normed, axis=-1, keepdims=True)
    )
    token_grad = (cotangent.astype(F32) * my_live + grad_norm).astype(BF)
    FA = FA.reshape(d.n_gy, 2, 4, d.rdg, d.ca)
    o_f1 = FA[..., : d.ffs].reshape(d.n_gy, 2, 4, d.rdg, d.n_gy, d.n_zp, d.r2)
    o_f1 = o_f1.transpose(0, 3, 4, 1, 5, 2, 6).reshape(d.rd, d.ff).astype(F32)
    o_qkv = FA[..., d.ffs :].reshape(d.n_gy, 8, d.rdg, 3, 128)
    o_qkv = o_qkv.transpose(0, 2, 3, 1, 4).reshape(d.rd, 3 * W).astype(F32)
    o_f2 = FF2.reshape(d.n_gy, 4, d.n_zp // 2, d.r2, d.c2).transpose(2, 1, 3, 0, 4)
    o_f2 = o_f2.reshape(d.ff // nd, W).astype(F32)
    o_wo = FWO.reshape(d.n_gy, d.rd, d.c2).transpose(1, 0, 2).reshape(d.rd, W).astype(F32)
    o_gain, o_bias, o_bf2 = FSM[0, :per], FSM[1, :per], FSM[2, :per]
    o_bf1 = FSM[3 : 3 + bf1_rows].reshape(-1)[: d.ff // nd]
    return mixed, token_grad, o_gain, o_bias, o_qkv, o_wo, o_f1, o_bf1, o_f2, o_bf2


def cdot(a, b, ca, cb):
    return lax.dot_general(a, b, (((ca,), (cb,)), ((), ())), preferred_element_type=F32)


def rows_at(start, n):
    return pl.ds(pl.multiple_of(start, n), n)


def layer_kernel(d, lens, offs, tok, cot, wqkv, wo, wfc1, wf2, sm, c0, s0,
                 MIXED, TGRAD, F1, FQ, F2, FWO, FSM,
                 TOK, COT, H, HT, Q, K, V, KT, VT, P0, P1, P2, P3, ACT, AT, SG, ATT, GATT, GQKV,
                 DK, DV, MIXP, WF1, WQ, WF2, WO, SM, VEC, BF1, SMG, SUMS, OWN,
                 mt, m2, m3, ht, h2, h3, GB, GA, GQ, yb, ya, yq, zb, za, zq, s1, s2,
                 loc, ts, tr, cs, cr, w1s, w1r, zs, zr, ys, yr, os_, or_,
                 tsem, bsem, asem, qsem, ssem, dsem):
    me = Me(d)
    gy, gx, zp, q, zl, c = me.gy, me.gx, me.zp, me.q, me.zl, me.c
    half, R, W = d.rows // 2, d.rows, d.width
    S = 4 * R
    PT = (P0, P1, P2, P3)
    qz, qc = lax.rem(q + 2, 4), zl * 2 + 1 - c
    qcz = lax.rem(qc + 2, 4)
    x_dev, z_dev, c_dev = place(gy, 1 - gx, zp, q), place(gy, gx, zp, qz), place(gy, gx, zp, qc)
    oz, oy = 1 - zp, 1 - gy
    zz_dev, yy_dev = place(gy, gx, oz, q), place(oy, gx, zp, q)
    sends, cot_sends = [], []

    def go(copy, kept=sends):
        copy.start()
        kept.append(copy)

    def block(bx, bq, h):
        pb = bq if h == 0 else 7 - bq
        return rows_at(bx * S + pb * half, half)

    def tsend(src, buf, send, recv, slot, bx, bq, h, device):
        return remote(src, buf.at[block(bx, bq, h)], send.at[slot, h], recv.at[bx * 4 + bq, h], device)

    TOKS, COTS = (tok, TOK, ts, tr, sends), (cot, COT, cs, cr, cot_sends)

    def x_first(arr, h):
        return h == 0

    def own_half(src, h):
        return src.at[pl.ds(h * half, half)]

    def first(arr, h):
        src, buf, send, recv, kept = arr
        go(tsend(own_half(src, h), buf, send, recv, 0, gx, q, h, x_dev if x_first(arr, h) else z_dev), kept)

    def second(arr, h):
        src, buf, send, recv, kept = arr
        go(tsend(own_half(src, h), buf, send, recv, 1, gx, q, h, z_dev if x_first(arr, h) else x_dev), kept)
        go(tsend(own_half(src, h), buf, send, recv, 3, gx, q, h, c_dev), kept)

    def wait_block(arr, bx, bq, h):
        _, buf, send, recv, kept = arr
        tsend(buf.at[block(bx, bq, h)], buf, send, recv, 0, bx, bq, h, x_dev).wait_recv()

    def pass_on(arr, slot, bx, bq, h, device):
        _, buf, send, recv, kept = arr
        go(tsend(buf.at[block(bx, bq, h)], buf, send, recv, slot, bx, bq, h, device), kept)

    def relay_first(arr, h):
        bx, bq = (1 - gx, q) if x_first(arr, h) else (gx, qz)
        wait_block(arr, bx, bq, h)
        pass_on(arr, 2, bx, bq, h, z_dev if x_first(arr, h) else x_dev)
        pass_on(arr, 4, bx, bq, h, c_dev)

    def relay_second(arr, h):
        bx, bq = (gx, qz) if x_first(arr, h) else (1 - gx, q)
        wait_block(arr, bx, bq, h)
        pass_on(arr, 5, bx, bq, h, c_dev)
        wait_block(arr, 1 - gx, qz, h)
        pass_on(arr, 6, 1 - gx, qz, h, c_dev)

    def wait_twin(arr):
        for bx in (gx, 1 - gx):
            for bq in (qc, qcz):
                for h in range(2):
                    wait_block(arr, bx, bq, h)

    own_rows = rows_at(q * d.r1, d.r1)
    local = [
        pltpu.make_async_copy(sm, SM.at[gy, gx, zp, q], loc.at[0]),
        pltpu.make_async_copy(wf2, WF2.at[gy, zp], loc.at[1]),
    ]
    for h in range(2):
        local.append(pltpu.make_async_copy(own_half(tok, h), TOK.at[block(gx, q, h)], loc.at[2 + h]))
        local.append(pltpu.make_async_copy(own_half(cot, h), COT.at[block(gx, q, h)], loc.at[4 + h]))
    local.append(pltpu.make_async_copy(cot, OWN, loc.at[7]))

    def fc1_pieces(ox, oq):
        for b in range(d.ng):
            f = ((b // d.n_zp * 2 + ox) * d.n_zp + b % d.n_zp) * 4 + oq
            yield (wfc1.at[:, rows_at(f * d.r2, d.r2)],
                   WF1.at[gy, gx, zp, own_rows, pl.ds(b * d.r2, d.r2)])

    def qkv_pieces(rank):
        for k in range(3):
            yield (wqkv.at[:, rows_at(k * W + rank * 128, 128)],
                   WQ.at[gy, gx, zp, own_rows, pl.ds(k * 128, 128)])

    for i in range(1, 8):
        other = lax.rem(me.rank + i, 8)
        ox, oq = other // 4, lax.rem(other, 4)
        dev = place(gy, ox, zp, oq)
        for src, dst in qkv_pieces(other):
            remote(src, dst, w1s.at[0, other], w1r.at[0, me.rank], dev).start()
        go(remote(sm, SM.at[gy, gx, zp, q], w1s.at[2, other], w1r.at[2, me.rank], dev))
    for src, dst in qkv_pieces(me.rank):
        pltpu.make_async_copy(src, dst, w1r.at[0, me.rank]).start()
    for h in range(2):
        first(TOKS, h)
    for copy in local:
        copy.start()
    for i in range(1, 8):
        other = lax.rem(me.rank + i, 8)
        ox, oq = other // 4, lax.rem(other, 4)
        for src, dst in fc1_pieces(ox, oq):
            remote(src, dst, w1s.at[1, other], w1r.at[1, me.rank], place(gy, ox, zp, oq)).start()
    for src, dst in fc1_pieces(gx, q):
        pltpu.make_async_copy(src, dst, w1r.at[1, me.rank]).start()
    def w1_region(buf, ox, oq):
        return buf.at[gy, ox, zp, rows_at(oq * d.r1, d.r1)]

    def wait_w1(k, buf):
        for i in range(1, 8):
            other = lax.rem(me.rank + i, 8)
            dst = w1_region(buf, other // 4, lax.rem(other, 4))
            remote(dst, dst, w1s.at[k, other], w1r.at[k, other], x_dev).wait_recv()
        dst = w1_region(buf, gx, q)
        pltpu.make_async_copy(dst, dst, w1r.at[k, me.rank]).wait()

    for copy in local:
        copy.wait()
    wait_w1(0, WQ)
    for i in range(1, 8):
        other = lax.rem(me.rank + i, 8)
        dst = SM.at[gy, other // 4, zp, lax.rem(other, 4)]
        remote(sm, dst, w1s.at[2, other], w1r.at[2, other], x_dev).wait_recv()
    def own_part(k, buf):
        part = buf.at[gy, :, zp]
        go(remote(part, part, zs.at[k], zr.at[k], zz_dev))
        go(remote(part, part, ys.at[k], yr.at[k], yy_dev))

    def far_part(k, buf):
        part = buf.at[gy, :, oz]
        remote(part, part, zs.at[k], zr.at[k], zz_dev).wait_recv()
        go(remote(part, part, ys.at[4 + k], yr.at[4 + k], yy_dev))

    def complete(k, buf):
        for part, n in ((zp, k), (oz, 4 + k)):
            dst = buf.at[oy, :, part]
            remote(dst, dst, ys.at[n], yr.at[n], yy_dev).wait_recv()

    own_part(2, SM)
    own_part(0, WQ)
    for h in range(2):
        second(TOKS, h)
    wait_w1(1, WF1)
    own_part(1, WF1)
    for h in range(2):
        relay_first(TOKS, h)
    go(remote(wf2, WF2.at[gy, zp], zs.at[3], zr.at[3], zz_dev))
    go(remote(wf2, WF2.at[gy, zp], ys.at[3], yr.at[3], yy_dev))
    for h in range(2):
        first(COTS, h)
    for h in range(2):
        second(COTS, h)
    per = 128 // d.r1
    owner = me.f // per
    part = lax.rem(me.f, per)
    wx, wq = owner // 4, lax.rem(owner, 4)
    wo_mine = jnp.logical_and(wx == gx, wq == q)
    wo_dst = WO.at[rows_at(part * d.r1, d.r1)]
    wo_own = remote(wo, wo_dst, os_.at[0], or_.at[part], place(gy, wx, zp, wq))
    wo_here = pltpu.make_async_copy(wo, wo_dst, loc.at[6])
    far_part(2, SM)
    far_part(0, WQ)
    for h in range(2):
        relay_second(TOKS, h)
    wait_twin(TOKS)
    complete(2, SM)
    in_lane = lax.broadcasted_iota(jnp.int32, (8, 128), 1) // d.r1
    parts = 128 // d.r1
    for j in range(8):
        rows3 = [jnp.zeros((8, 128), F32)] * 3
        for k in range(parts):
            g_, dv = divmod(j * parts + k, d.n_dev)
            packed = SM[g_ // 2, g_ % 2, dv // 4, dv % 4].astype(F32)[0:8]
            for v in range(3):
                turn = (k - v) % parts * d.r1
                moved = pltpu.roll(packed, turn, 1) if turn else packed
                rows3[v] = jnp.where(in_lane == k, moved, rows3[v])
        for v in range(3):
            VEC[v : v + 1, j * 128 : (j + 1) * 128] = rows3[v][0:1]
    for b in range(d.ng):
        BF1[:, b * 128 : (b + 1) * 128] = SM[b // d.n_zp, gx, b % d.n_zp, q].astype(F32)
    SUMS[...] = jnp.zeros_like(SUMS)

    def slot_of(s):
        index = (gy * 2 + s) * d.n_zp + zp
        return lens[index], offs[index]

    def normalise(rows):
        x = rows.astype(F32)
        centred = x - jnp.mean(x, axis=-1, keepdims=True)
        inverse = lax.rsqrt(jnp.mean(centred * centred, axis=-1, keepdims=True) + 1e-5)
        return centred * inverse, inverse

    def live_column(s, first_place, n):
        length, offset = slot_of(s)
        at = lax.broadcasted_iota(jnp.int32, (n, 1), 0) + first_place
        return jnp.logical_and(at >= offset, at < offset + length)

    def live_row(s, first_place, n):
        length, offset = slot_of(s)
        at = lax.broadcasted_iota(jnp.int32, (1, n), 1) + first_place
        return jnp.logical_and(at >= offset, at < offset + length)

    @pl.loop(0, 8)
    def _(i):
        normed, _ = normalise(TOK[rows_at(i * R, R), :])
        h = (normed * VEC[0:1, :] + VEC[1:2, :]).astype(BF)
        H[rows_at(i * R, R), :] = h
        HT[:, rows_at(i * R, R)] = h.T

    relay_first(COTS, 0)
    far_part(1, WF1)
    for i in range(1, d.ng):
        group = lax.rem(gy * d.n_zp + zp + i, d.ng)
        go(remote(wo, wo_dst, os_.at[i], or_.at[part],
                  place(group // d.n_zp, wx, lax.rem(group, d.n_zp), wq)))

    @pl.when(wo_mine)
    def _():
        wo_here.start()

    @pl.when(jnp.logical_not(wo_mine))
    def _():
        wo_own.start()

    complete(0, WQ)

    lane = lax.rem(lax.broadcasted_iota(jnp.int32, (1, 128), 1), 64)

    def turn_tables_of(s, t):
        _, offset = slot_of(s)
        co, so = c0[pl.ds(offset, 1), :], s0[pl.ds(offset, 1), :]
        cc, ss = c0[rows_at(t * R, R), :], s0[rows_at(t * R, R), :]
        cos = cc * co + ss * so
        sin = ss * co - cc * so
        cos = jnp.where(lane < ROT, cos, 1.0)
        sin = jnp.where(lane < ROT // 2, -sin, jnp.where(lane < ROT, sin, 0.0))
        return cos, sin

    def turned(x, cos, sin):
        other = jnp.where(lane < ROT // 2, pltpu.roll(x, 128 - ROT // 2, 1), pltpu.roll(x, ROT // 2, 1))
        return x * cos + other * sin

    wq_all = (W, d.qs)

    @pl.loop(0, 8)
    def _(i):
        s, t = i // 4, lax.rem(i, 4)
        rows = rows_at(i * R, R)
        qkv = cdot(H[rows, :], WQ[...].reshape(wq_all), 1, 0)
        cos, sin = turn_tables_of(s, t)
        query = turned(qkv[:, :128], cos, sin).astype(BF)
        Q[rows, :] = (query.astype(F32) * 0.125).astype(BF)
        key = turned(qkv[:, 128:256], cos, sin).astype(BF)
        K[rows, :] = key
        KT[:, rows] = key.T
        value = qkv[:, 256:].astype(BF)
        V[rows, :] = value
        VT[:, rows] = value.T

    relay_first(COTS, 1)
    remote(WF2.at[gy, oz], WF2.at[gy, oz], zs.at[3], zr.at[3], zz_dev).wait_recv()
    go(remote(WF2.at[gy, oz], WF2.at[gy, oz], ys.at[7], yr.at[7], yy_dev))
    lane128 = lax.broadcasted_iota(jnp.int32, (1, 128), 1)

    def of_head(x, j):
        keep = (lane128 < 64) if j == 0 else (lane128 >= 64)
        return jnp.where(keep, x, jnp.zeros_like(x))

    def attend(s, t):
        n = (t + 1) * R
        base = pl.multiple_of(s * S, S)
        rows = rows_at(s * S + t * R, R)
        query = Q[rows, :]
        bias = jnp.where(live_column(s, 0, n), 0.0, -1e30)
        key_at = lax.broadcasted_iota(jnp.int32, (R, R), 0)
        query_at = lax.broadcasted_iota(jnp.int32, (R, R), 1)
        for j in range(2):
            scores = cdot(K[pl.ds(base, n), :], of_head(query, j), 1, 1)
            diag = scores[t * R :] + jnp.where(key_at == query_at, 0.0, bias[t * R :])
            diag = jnp.where(key_at <= query_at, diag, -1e30)
            top = jnp.max(diag, axis=0, keepdims=True)
            if t > 0:
                left = scores[: t * R] + bias[: t * R]
                top = jnp.maximum(top, jnp.max(left, axis=0, keepdims=True))
                left = jnp.exp(left - top)
            diag = jnp.exp(diag - top)
            total = jnp.sum(diag, axis=0, keepdims=True)
            if t > 0:
                total = total + jnp.sum(left, axis=0, keepdims=True)
            scale = 1.0 / total
            prob = PT[t].at[s * 2 + j]
            prob[pl.ds(t * R, R), :] = (diag * scale).astype(BF)
            if t > 0:
                prob[pl.ds(0, t * R), :] = (left * scale).astype(BF)
            out = cdot(VT[pl.ds(j * 64, 64), pl.ds(base, n)], prob[...], 1, 0)
            ATT[rows, pl.ds(j * 64, 64)] = out.T.astype(BF)
            keep = live_row(s, t * R, R)
            AT[pl.ds(d.ffs + j * 64, 64), rows] = jnp.where(keep, out, 0.0).astype(BF)

    @pl.loop(0, 2)
    def _(s):
        for t in range(4):
            attend(s, t)

    relay_second(COTS, 0)
    complete(1, WF1)

    @pl.loop(0, 8)
    def _(i):
        rows = rows_at(i * R, R)
        pre = cdot(H[rows, :], WF1[...].reshape((W, d.ffs)), 1, 0) + BF1[3:4, :]
        act, slope = gelu_parts(pre)
        act = act.astype(BF)
        ACT[rows, :] = act
        SG[rows, :] = slope.astype(BF)
        keep = live_column(i // 4, lax.rem(i, 4) * R, R)
        AT[pl.ds(0, d.ffs), rows] = jnp.where(keep, act, jnp.zeros_like(act)).T

    relay_second(COTS, 1)
    wait_twin(COTS)

    def over_gy(part, buf, sem):
        return remote(part.at[oy], buf, sem.at[0, 0], sem.at[1, 0], yy_dev)

    for side in (oy, gy):
        for m in range(d.c2 // 256):
            cols = pl.ds(m * 256, 256)
            out = cdot(AT[...], COT[:, rows_at(side * d.c2 + m * 256, 256)], 1, 0).astype(BF)
            GB[side, :, cols] = out
            if side is oy:
                remote(GB.at[oy, :, cols], yb.at[:, cols], bsem.at[0, 0], bsem.at[1, 0], yy_dev).start()
    sends.append(over_gy(GB, yb, bsem))
    for part, n in ((zp, 3), (oz, 7)):
        dst = WF2.at[oy, part]
        remote(dst, dst, ys.at[n], yr.at[n], yy_dev).wait_recv()
    for i in range(per):
        source = me.rank * per + i
        dst = WO.at[pl.ds(i * d.r1, d.r1)]

        @pl.when(source != me.f)
        def _():
            remote(wo, dst, os_.at[0], or_.at[i], x_dev).wait_recv()

    @pl.when(wo_mine)
    def _():
        wo_here.wait()

    def to_twin(src, t_buf, k, s, t):
        h = t // 2
        bz = jnp.where(t < 2, t, 3 - t)
        pb = 2 * t + jnp.where(t < 2, 1 - c, c)
        n = (s * 2 + bz) * 2 + h
        remote(src.at[rows_at(s * S + pb * half, half)], t_buf.at[s, bz, h], tsem.at[k, 0, n],
               tsem.at[k, 1, n], c_dev).start()

    def twin_blocks(src, t_buf, k):
        for bx in range(2):
            for bz in range(2):
                for h in range(2):
                    n = (bx * 2 + bz) * 2 + h
                    own = src.at[block(bx, bz * 2 + c, h)]
                    copy = remote(own, t_buf.at[bx, bz, h], tsem.at[k, 0, n], tsem.at[k, 1, n], c_dev)
                    yield bx, bz, h, own, copy

    def add_twin(src, t_buf, k):
        for bx, bz, h, own, copy in twin_blocks(src, t_buf, k):
            copy.wait_recv()
            t_buf[bx, bz, h] = (t_buf[bx, bz, h].astype(F32) + own[...].astype(F32)).astype(BF)

    def twin_sent(src, t_buf, k):
        for _, _, _, _, copy in twin_blocks(src, t_buf, k):
            copy.wait_send()

    def block_of(h, part):
        mine = zl if h == 0 else gx
        return 1 - mine if part == 0 else mine

    def hop_one(t_buf, b2, k, h, part):
        b, n = block_of(h, part), 8 + h * 2 + part
        src, dev = (t_buf.at[1 - gx, b, 0], x_dev) if h == 0 else (t_buf.at[b, 1 - zl, 1], z_dev)
        return remote(src, b2.at[h, b], tsem.at[k, 0, n], tsem.at[k, 1, n], dev)

    def add_one(t_buf, b2, k, h, part):
        hop_one(t_buf, b2, k, h, part).wait_recv()
        b = block_of(h, part)
        own = t_buf[gx, b, 0] if h == 0 else t_buf[b, zl, 1]
        b2[h, b] = (b2[h, b].astype(F32) + own.astype(F32)).astype(BF)

    def hop_two(b2, b3, k, h):
        src, dev = (b2.at[0, 1 - zl], z_dev) if h == 0 else (b2.at[1, 1 - gx], x_dev)
        return remote(src, b3.at[h], tsem.at[k, 0, 12 + h], tsem.at[k, 1, 12 + h], dev)

    def rows_of(b2, b3, h):
        return b2[h, zl if h == 0 else gx].astype(F32) + b3[h].astype(F32)


    wf2_all = (d.ffs, W)

    @pl.loop(0, 8)
    def _(i):
        rows = rows_at(i * R, R)
        mix = cdot(ATT[rows, :], WO[...], 1, 0) + cdot(ACT[rows, :], WF2[...].reshape(wf2_all), 1, 0)
        MIXP[rows, :] = mix.astype(BF)
        to_twin(MIXP, mt, 0, i // 4, lax.rem(i, 4))

    @pl.loop(0, 8)
    def _(i):
        rows = rows_at(i * R, R)
        keep = live_column(i // 4, lax.rem(i, 4) * R, R)
        grad = COT[rows, :]
        grad = jnp.where(keep, grad, jnp.zeros_like(grad))
        grad_act = cdot(grad, WF2[...].reshape(wf2_all), 1, 1)
        grad_pre = (grad_act * SG[rows, :].astype(F32)).astype(BF)
        SG[rows, :] = grad_pre
        GATT[rows, :] = cdot(grad, WO[...], 1, 1).astype(BF)
        SUMS[2:3, :] += jnp.sum(grad.astype(F32), axis=0, keepdims=True)
        SUMS[3:4, : d.ffs] += jnp.sum(grad_pre.astype(F32), axis=0, keepdims=True)

    add_twin(MIXP, mt, 0)
    for part in range(2):
        for h in range(2):
            go(hop_one(mt, m2, 0, h, part))

    @pl.loop(0, d.ffs // 256)
    def _(n):
        cols = rows_at(n * 256, 256)
        out = cdot(HT[...], SG[:, cols], 1, 0).astype(BF).reshape(8, 2, d.rdg, 256)
        GA[0, :, :, cols] = out[:, 0]
        GA[1, :, :, cols] = out[:, 1]
        remote(GA.at[oy, :, :, cols], ya.at[:, :, cols], asem.at[0, 0], asem.at[1, 0], yy_dev).start()

    sends.append(over_gy(GA, ya, asem))
    def y_sum(part, buf, sem, count):
        over_gy(part, buf, sem).wait_recv()
        for b in range(count):
            buf[b] = (buf[b].astype(F32) + part[gy, b].astype(F32)).astype(BF)

    over_gy(GB, yb, bsem).wait_recv()
    for b in range(5):
        rr = pl.ds(b * 128, 128)
        yb[rr, :] = (yb[rr, :].astype(F32) + GB[gy, rr, :].astype(F32)).astype(BF)
    b_rows = d.n_zp * d.r2
    f2_over_zp = remote(yb.at[rows_at(oz * b_rows, b_rows)], zb.at[pl.ds(0, b_rows)],
                        bsem.at[0, 1], bsem.at[1, 1], zz_dev)
    go(f2_over_zp)
    wo_zp = me.rank * d.n_zp // 8
    wo_over_zp = remote(yb.at[pl.ds(d.ffs, 128)], zb.at[pl.ds(b_rows, 128)],
                        bsem.at[0, 2], bsem.at[1, 2], zz_dev)

    @pl.when(wo_zp != zp)
    def _():
        wo_over_zp.start()

    def attend_back(s, t):
        n = (t + 1) * R
        base = pl.multiple_of(s * S, S)
        rows = rows_at(s * S + t * R, R)
        query, grad = Q[rows, :], GATT[rows, :]
        cos, sin = turn_tables_of(s, t)
        halves = []
        for j in range(2):
            grad_j = of_head(grad, j)
            prob_low = PT[t][s * 2 + j]
            grad_prob = cdot(V[pl.ds(base, n), :], grad_j, 1, 1)
            prob = prob_low.astype(F32)
            both = prob * grad_prob
            inner = jnp.sum(both, axis=0, keepdims=True)
            score = (both - prob * inner).astype(BF)
            DV[pl.ds(0, n), :] += cdot(prob_low, grad_j, 1, 0)
            DK[pl.ds(0, n), :] += cdot(score, of_head(query, j), 1, 0)
            halves.append(cdot(KT[pl.ds(j * 64, 64), pl.ds(base, n)], score, 1, 0))
        grad_q = jnp.concatenate(halves, axis=0).T * 0.125
        GQKV[rows, 0:128] = turned(grad_q, cos, -sin).astype(BF)

    @pl.loop(0, 2)
    def _(s):
        DK[...] = jnp.zeros_like(DK)
        DV[...] = jnp.zeros_like(DV)
        for t in range(4):
            attend_back(s, t)
        for t in range(4):
            rows = rows_at(s * S + t * R, R)
            cos, sin = turn_tables_of(s, t)
            GQKV[rows, 128:256] = turned(DK[pl.ds(t * R, R), :], cos, -sin).astype(BF)
            GQKV[rows, 256:384] = DV[pl.ds(t * R, R), :].astype(BF)

    out = cdot(HT[...], GQKV[...], 1, 0).astype(BF).reshape(8, 2, d.rdg, d.qs)
    GQ[0] = out[:, 0]
    GQ[1] = out[:, 1]
    go(over_gy(GQ, yq, qsem))
    for h in range(2):
        add_one(mt, m2, 0, h, 0)
        go(hop_two(m2, m3, 0, h))
    y_sum(GA, ya, asem, 8)
    f1_over_zp = remote(ya.at[pl.ds(oz * 4, 4)], za, asem.at[0, 1], asem.at[1, 1], zz_dev)
    go(f1_over_zp)


    f2_over_zp.wait_recv()
    for b in range(d.n_zp):
        rr = pl.ds(b * 128, 128)
        own = yb[rows_at(zp * b_rows + b * 128, 128), :]
        zb[rr, :] = (zb[rr, :].astype(F32) + own.astype(F32)).astype(BF)
    f2_cols = rows_at(gy * d.c2, d.c2)
    f2_mine = F2.at[rows_at(q * 128, 128), f2_cols]

    def f2_copies():
        for j in range(2):
            for ox in range(2):
                away = jnp.logical_not(jnp.logical_and(ox == gx, gx * 2 + j == q))
                src = zb.at[pl.ds(j * 128, 128)]
                yield away, src, remote(src, f2_mine, dsem.at[0, 0, j * 2 + ox], dsem.at[0, 1, q],
                                        place(gy, ox, zp, gx * 2 + j))

    for away, src, copy in f2_copies():
        here = pltpu.make_async_copy(src, f2_mine, dsem.at[0, 2, 0])

        @pl.when(away)
        def _():
            copy.start()

        @pl.when(jnp.logical_not(away))
        def _():
            here.start()
            here.wait()

    wo_src = zb.at[pl.ds(b_rows, 128)]
    wo_final = remote(wo_src, FWO.at[:, f2_cols], dsem.at[1, 0, 0], dsem.at[1, 1, 0], x_dev)
    wo_stay = pltpu.make_async_copy(wo_src, FWO.at[:, f2_cols], dsem.at[1, 2, 0])

    @pl.when(wo_zp == zp)
    def _():
        wo_over_zp.wait_recv()
        rr = pl.ds(b_rows, 128)
        zb[rr, :] = (zb[rr, :].astype(F32) + yb[pl.ds(d.ffs, 128), :].astype(F32)).astype(BF)
        wo_final.start()
        wo_stay.start()
        wo_stay.wait()

    for copy in cot_sends:
        copy.wait_send()

    @pl.loop(0, 8)
    def _(i):
        rows = rows_at(i * R, R)
        grad = cdot(SG[rows, :], WF1[...].reshape((W, d.ffs)), 1, 1)
        grad = grad + cdot(GQKV[rows, :], WQ[...].reshape(wq_all), 1, 1)
        normed, _ = normalise(TOK[rows, :])
        SUMS[0:1, :] += jnp.sum(grad * normed, axis=0, keepdims=True)
        SUMS[1:2, :] += jnp.sum(grad, axis=0, keepdims=True)
        COT[rows, :] = grad.astype(BF)
        to_twin(COT, ht, 1, i // 4, lax.rem(i, 4))

    for sq in range(4):
        away = jnp.logical_not(jnp.logical_and(gx == zl, sq == q))

        @pl.when(away)
        def _():
            remote(zb.at[pl.ds(0, 128)], F2.at[rows_at(sq * 128, 128), f2_cols], dsem.at[0, 0, 0],
                   dsem.at[0, 1, sq], x_dev).wait_recv()

    @pl.when(wo_zp != zp)
    def _():
        wo_final.wait_recv()

    go(remote(F2.at[:, f2_cols], F2.at[:, f2_cols], bsem.at[0, 3], bsem.at[1, 3], yy_dev))
    go(remote(FWO.at[:, f2_cols], FWO.at[:, f2_cols], bsem.at[0, 4], bsem.at[1, 4], yy_dev))
    add_twin(COT, ht, 1)
    for h in range(2):
        go(hop_one(ht, h2, 1, h, 0))
    SMG[...] = jnp.zeros_like(SMG)
    first_rank = jnp.where(me.rank == 0, 1.0, 0.0)
    for dd in range(d.n_dev):
        for k in range(3):
            piece = SUMS[k : k + 1, dd * 128 : (dd + 1) * 128]
            SMG[dd % 4, dd // 4, k : k + 1, :] = piece * first_rank if k == 2 else piece
    for b in range(d.ng):
        dq = gx * 2 + b % d.n_zp
        SMG[dq, b // d.n_zp, pl.ds(3 + q, 1), :] = SUMS[3:4, b * 128 : (b + 1) * 128]
    for i in range(1, 8):
        other = lax.rem(me.rank + i, 8)
        go(remote(SMG.at[lax.rem(other, 4)], s1.at[me.rank], ssem.at[0, 0, other],
                  ssem.at[0, 1, me.rank], place(gy, other // 4, zp, lax.rem(other, 4))))
    f_rows = rows_at(gy * d.rdg, d.rdg)

    def f1_pieces():
        for b in range(d.ng):
            f = ((b // d.n_zp * 2 + gx) * d.n_zp + b % d.n_zp) * 4 + q
            yield b, F1.at[f_rows, rows_at(f * 128, 128)]

    def fq_pieces():
        for k in range(3):
            yield k, FQ.at[f_rows, rows_at(k * W + me.rank * 128, 128)]

    def finish(done, mine, pieces, k):
        for b in range(4):
            done[b] = (done[b].astype(F32) + mine[zp * 4 + b].astype(F32)).astype(BF)
        for i in range(1, 8):
            other = lax.rem(me.rank + i, 8)
            ox, oq = other // 4, lax.rem(other, 4)
            for n, dst in pieces():
                remote(done.at[oq, :, pl.ds(n * 128, 128)], dst, dsem.at[k, 0, other],
                       dsem.at[k, 1, me.rank], place(gy, ox, zp, oq)).start()
        for n, dst in pieces():
            pltpu.make_async_copy(done.at[q, :, pl.ds(n * 128, 128)], dst, dsem.at[k, 2, 0]).start()
        pltpu.make_async_copy(done.at[0], done.at[0], dsem.at[k, 2, 0]).wait()

    def finished(done, k):
        for i in range(1, 8):
            other = lax.rem(me.rank + i, 8)
            remote(done.at[0], done.at[0], dsem.at[k, 0, other], dsem.at[k, 1, other],
                   x_dev).wait_recv()

    def finish_sent(done, k):
        for i in range(1, 8):
            other = lax.rem(me.rank + i, 8)
            remote(done.at[0], done.at[0], dsem.at[k, 0, other], dsem.at[k, 1, other],
                   x_dev).wait_send()

    y_sum(GQ, yq, qsem, 8)
    fq_over_zp = remote(yq.at[pl.ds(oz * 4, 4)], zq, qsem.at[0, 1], qsem.at[1, 1], zz_dev)
    go(fq_over_zp)
    f1_over_zp.wait_recv()
    finish(za, ya, f1_pieces, 2)
    for h in range(2):
        go(hop_one(ht, h2, 1, h, 1))
    for h in range(2):
        add_one(mt, m2, 0, h, 1)
    for h in range(2):
        hop_two(m2, m3, 0, h).wait_recv()
        first_place = (q if h == 0 else 7 - q) * half
        rr = pl.ds(h * half, half)
        total = rows_of(m2, m3, h) + VEC[2:3, :]
        total = total + TOK[block(gx, q, h), :].astype(F32)
        MIXED[rr, :] = jnp.where(live_column(gx, first_place, half), total, 0.0).astype(BF)
    for h in range(2):
        add_one(ht, h2, 1, h, 0)
        go(hop_two(h2, h3, 1, h))
    fq_over_zp.wait_recv()
    finish(zq, yq, fq_pieces, 3)
    finished(za, 2)
    go(remote(F1.at[f_rows], F1.at[f_rows], asem.at[0, 2], asem.at[1, 2], yy_dev))
    for h in range(2):
        add_one(ht, h2, 1, h, 1)
    for i in range(1, 8):
        other = lax.rem(me.rank + i, 8)
        remote(SMG.at[0], s1.at[other], ssem.at[0, 0, other], ssem.at[0, 1, other],
               x_dev).wait_recv()
    s1[me.rank] = SMG[q]
    total = s1[0]
    for i in range(1, 8):
        total = total + s1[i]
    s2[d.ng] = total
    own_group = gy * d.n_zp + zp
    for i in range(1, d.ng):
        group = lax.rem(own_group + i, d.ng)
        to_z = lax.rem(group, d.n_zp)
        go(remote(s2.at[d.ng, to_z], s2.at[own_group, 0], ssem.at[1, 0, group],
                  ssem.at[1, 1, own_group], place(group // d.n_zp, gx, to_z, q)))
    finished(zq, 3)
    go(remote(FQ.at[f_rows], FQ.at[f_rows], qsem.at[0, 2], qsem.at[1, 2], yy_dev))
    for h in range(2):
        hop_two(h2, h3, 1, h).wait_recv()
        first_place = (q if h == 0 else 7 - q) * half
        rr = pl.ds(h * half, half)
        normed, inverse = normalise(TOK[block(gx, q, h), :])
        scaled = rows_of(h2, h3, h) * VEC[0:1, :]
        grad = inverse * (
            scaled
            - jnp.mean(scaled, axis=-1, keepdims=True)
            - normed * jnp.mean(scaled * normed, axis=-1, keepdims=True)
        )
        own = jnp.where(live_column(gx, first_place, half), OWN[rr, :].astype(F32), 0.0)
        TGRAD[rr, :] = (own + grad).astype(BF)
    for i in range(1, d.ng):
        group = lax.rem(own_group + i, d.ng)
        remote(s2.at[d.ng, 0], s2.at[group, 0], ssem.at[1, 0, group], ssem.at[1, 1, group],
               x_dev).wait_recv()
    total = s2[d.ng, zp]
    for i in range(1, d.ng):
        total = total + s2[lax.rem(own_group + i, d.ng), 0]
    FSM[...] = total
    o_rows, o_cols = rows_at(oy * d.rdg, d.rdg), rows_at(oy * d.c2, d.c2)
    remote(F2.at[:, o_cols], F2.at[:, o_cols], bsem.at[0, 3], bsem.at[1, 3], yy_dev).wait_recv()
    remote(FWO.at[:, o_cols], FWO.at[:, o_cols], bsem.at[0, 4], bsem.at[1, 4], yy_dev).wait_recv()
    remote(F1.at[o_rows], F1.at[o_rows], asem.at[0, 2], asem.at[1, 2], yy_dev).wait_recv()
    remote(FQ.at[o_rows], FQ.at[o_rows], qsem.at[0, 2], qsem.at[1, 2], yy_dev).wait_recv()
    twin_sent(MIXP, mt, 0)
    twin_sent(COT, ht, 1)
    for copy in sends:
        copy.wait_send()
    for k, buf in enumerate((WQ, WF1)):
        for i in range(1, 8):
            other = lax.rem(me.rank + i, 8)
            dst = w1_region(buf, gx, q)
            remote(dst, dst, w1s.at[k, other], w1r.at[k, other], x_dev).wait_send()

    @pl.when(jnp.logical_not(wo_mine))
    def _():
        wo_own.wait_send()

    @pl.when(wo_zp != zp)
    def _():
        wo_over_zp.wait_send()

    @pl.when(wo_zp == zp)
    def _():
        wo_final.wait_send()

    for away, src, copy in f2_copies():

        @pl.when(away)
        def _():
            copy.wait_send()

    finish_sent(za, 2)
    finish_sent(zq, 3)


def layer(d, lens, offs, tok, cot, wqkv, wo, wfc1, wf2, sm, c0, s0):
    smem = pl.BlockSpec(memory_space=pltpu.SMEM)
    vm = pl.BlockSpec(memory_space=pltpu.VMEM)
    hbm = pl.BlockSpec(memory_space=pl.ANY)
    dma = pltpu.SemaphoreType.DMA
    shape = jax.ShapeDtypeStruct
    R, W, half = d.rows, d.width, d.rows // 2
    N = 8 * R

    def bf(*dims):
        return pltpu.VMEM(dims, BF)

    def f32(*dims):
        return pltpu.VMEM(dims, F32)

    return pl.pallas_call(
        functools.partial(layer_kernel, d),
        out_shape=(
            shape((R, W), BF),
            shape((R, W), BF),
            shape((d.rd, d.ff), BF),
            shape((d.rd, 3 * W), BF),
            shape((d.ff // d.n_dev, W), BF),
            shape((d.rd, W), BF),
            shape((8, 128), F32),
        ),
        in_specs=[smem, smem] + [hbm] * 7 + [vm] * 2,
        out_specs=(vm,) * 7,
        scratch_shapes=[
            bf(N, W), bf(N, W), bf(N, W), bf(W, N),
            bf(N, 128), bf(N, 128), bf(N, 128), bf(128, N), bf(128, N),
            bf(4, R, R), bf(4, 2 * R, R), bf(4, 3 * R, R), bf(4, 4 * R, R),
            bf(N, d.ffs), bf(d.ffs + 128, N), bf(N, d.ffs), bf(N, 128), bf(N, 128), bf(N, d.qs),
            f32(4 * R, 128), f32(4 * R, 128), bf(N, W),
            bf(d.n_gy, 2, d.n_zp, 4 * d.r1, d.ffs), bf(d.n_gy, 2, d.n_zp, 4 * d.r1, d.qs),
            bf(d.n_gy, d.n_zp, d.r2, W), bf(128, W), bf(d.n_gy, 2, d.n_zp, 4, 16, 128),
            f32(16, W), f32(16, d.ffs), f32(4, d.n_zp, 8, 128), f32(8, W), bf(R, W),
            bf(2, 2, 2, half, W), bf(2, 2, half, W), bf(2, half, W),
            bf(2, 2, 2, half, W), bf(2, 2, half, W), bf(2, half, W),
            bf(d.n_gy, d.ffs + 128, d.c2), bf(d.n_gy, 8, d.rdg, d.ffs), bf(d.n_gy, 8, d.rdg, d.qs),
            bf(d.ffs + 128, d.c2), bf(8, d.rdg, d.ffs), bf(8, d.rdg, d.qs),
            bf(d.ffs // d.n_zp + 128, d.c2), bf(4, d.rdg, d.ffs), bf(4, d.rdg, d.qs),
            f32(8, d.n_zp, 8, 128), f32(d.ng + 1, d.n_zp, 8, 128),
            dma((8,)), dma((7, 2)), dma((8, 2)), dma((7, 2)), dma((8, 2)),
            dma((3, 8)), dma((3, 8)), dma((4,)), dma((4,)), dma((8,)), dma((8,)),
            dma((d.ng,)), dma((128 // d.r1,)),
            dma((2, 2, 14)), dma((2, 5)), dma((2, 3)), dma((2, 3)), dma((2, 2, 8)), dma((4, 3, 8)),
        ],
        compiler_params=pltpu.CompilerParams(
            has_side_effects=True, vmem_limit_bytes=67043328
        ),
        name="layer",
    )(lens, offs, tok, cot, wqkv, wo, wfc1, wf2, sm, c0, s0)


def place_tables(slot):
    freq = np.exp(np.arange(ROT // 2) * (-2.0 * math.log(10000.0) / ROT))
    angle = np.arange(slot)[:, None] * freq[np.arange(128) % (ROT // 2)][None]
    return np.cos(angle).astype(np.float32), np.sin(angle).astype(np.float32)


def small_pack(d, ln_gain, ln_bias, b_fc1, b_fc2):
    gap = jnp.zeros((3 * 128 - 3 * d.r1,), BF)
    rest = jnp.zeros((12 * 128,), BF)
    return jnp.concatenate([ln_gain, ln_bias, b_fc2, gap, b_fc1, rest]).reshape(16, 128)


def local_one(d, tokens, cotangent, lengths, offsets, ln_gain, ln_bias, w_qkv, w_out, w_fc1, b_fc1,
              w_fc2, b_fc2):
    sm = small_pack(d, ln_gain, ln_bias, b_fc1, b_fc2)
    c0, s0 = place_tables(4 * d.rows)
    mixed, token_grad, f1, fq, f2, fwo, small = layer(
        d, lengths, offsets, tokens, cotangent, w_qkv, w_out, w_fc1, w_fc2, sm,
        jnp.asarray(c0), jnp.asarray(s0),
    )
    per = d.rd
    return (mixed, token_grad, small[0, :per], small[1, :per], fq.astype(F32), fwo.astype(F32),
            f1.astype(F32), small[3:7].reshape(-1), f2.astype(F32), small[2, :per])


def solution(mesh):
    rows = ("grp", "dev")

    def program(*args):
        tokens, w_fc1 = args[0], args[8]
        n = mesh.shape["grp"] * mesh.shape["dev"]
        d = Dims(mesh, tokens.shape[0] // n, tokens.shape[1], w_fc1.shape[1])
        whole_tiles = d.n_gy == 2 and d.r2 == 128 and d.r1 % 16 == 0 and d.rd == 128
        return jax.shard_map(
            functools.partial(local_one if whole_tiles else local, d),
            mesh=mesh,
            in_specs=(
                P(rows, None), P(rows, None), P(), P(), P(rows), P(rows), P(rows, None),
                P(rows, None), P(rows, None), P(rows), P(rows, None), P(rows),
            ),
            out_specs=(
                P(rows, None), P(rows, None), P("dev"), P("dev"), P("dev", None), P("dev", None),
                P("dev", None), P("dev"), P("dev", None), P("dev"),
            ),
            check_vma=False,
        )(*args)

    return program
```
